32 devices in a mesh: gx: 2 (over y), gy: 16 (over z, x, core).
Axes of the slice: x: 2, y: 2, z: 4, core: 2. Of those that a mesh axis runs over, the one named last changes fastest.
Arguments:
- start_state: float32 [14, 8, 128, 256], P(None, None, 'gy', 'gx'), may hold values from -5 to 5, as said below
- final_adjoint: float32 [14, 8, 128, 256], P(None, None, 'gy', 'gx'), may hold values from -46 to 46
- face_words: int32 [2, 2, 2, 128, 256], P(None, None, None, 'gy', 'gx'), may hold values from 0 to 65535
- terrain: int32 [128, 256], P('gy', 'gx'), may hold values from 0 to 23
- drag_coef: float32 [24], replicated, may hold values from 0.05 to 1
Outputs:
- start_adjoint: float32 [14, 8, 128, 256], P(None, None, 'gy', 'gx')
- drag_grad: float32 [24], replicated
The draws below stay inside these ranges and needn't reach their ends.
Inputs may be any that keep to these rules, and one draw needn't show every extreme that they name: `start_state`: fields 0, 5, 8 and 11 are masses between 0.5 and 3.5.
All inputs are finite; a program needn't handle non-finite values.
Results may differ from the reference program's by a relative error of at most 0.0003.
Values sent between devices are 32-bit elements; how exact they have to be, the bound alone decides.
No kernel may reach another device: no remote copies, remote signals or barrier semaphores. Data moves between devices by JAX's collectives and lax.ppermute only.
A program may use at most 64 MiB of HBM per device.

```python
import math
import jax
import jax.numpy as jnp
from jax import lax

FIELDS = 14
LEV = 8
NCLASS = 24
NX = 256
NY = 128


def draw_start_state(key, part):
    shape = (FIELDS, LEV, NY, NX)
    first_key = jax.random.fold_in(key, 11)
    second_key = jax.random.fold_in(key, 12)
    values = jnp.clip(jax.random.normal(first_key, shape, jnp.float32), -5.0, 5.0)
    masses = 0.5 + 1.5 * jax.random.uniform(second_key, shape, jnp.float32)
    indices = jnp.arange(FIELDS)
    is_mass = ((indices == 0) | (indices >= 5) & (indices % 3 == 2))[:, None, None, None]
    return jnp.where(is_mass, masses, values)


def draw_final_adjoint(key, part):
    shape = (FIELDS, LEV, NY, NX)
    first_key = jax.random.fold_in(key, 21)
    ramp_x = 1.0 + 2.0 * jnp.arange(NX, dtype=jnp.float32) / NX
    ramp_y = 1.0 + 2.0 * jnp.arange(NY, dtype=jnp.float32) / NY
    values = jnp.clip(jax.random.normal(first_key, shape, jnp.float32), -4.0, 4.0)
    return values * ramp_y[:, None] * ramp_x[None, :]


def place_ends(array, key, smallest, largest):
    place = [jax.random.randint(jax.random.fold_in(key, axis), (), 0, length) for axis, length in enumerate(array.shape)]
    widest = array.shape.index(max(array.shape))
    next_to = place[:widest] + [(place[widest] + 1) % array.shape[widest]] + place[widest + 1:]
    return array.at[tuple(place)].set(smallest).at[tuple(next_to)].set(largest)


def setup_inputs(seed: int = 0) -> dict:
    key_list = jax.random.split(jax.random.key(seed), 6)
    return {
        "start_state": draw_start_state(jax.random.fold_in(key_list[5], 71), 0),
        "final_adjoint": draw_final_adjoint(jax.random.fold_in(key_list[5], 71), 0),
        "face_words": place_ends(jax.random.randint(key_list[2], (2, 2, 2, NY, NX), 0, 2 ** (2 * LEV)), jax.random.fold_in(key_list[2], 1), 0, (2 ** (2 * LEV)) - 1).astype(jnp.int32),
        "terrain": place_ends(jax.random.randint(key_list[3], (NY, NX), 0, NCLASS), jax.random.fold_in(key_list[3], 1), 0, NCLASS - 1).astype(jnp.int32),
        "drag_coef": jnp.clip(jnp.exp(jax.random.uniform(key_list[4], (NCLASS,), jnp.float32, math.log(0.05), math.log(1.0))), 0.05, 1.0),
    }


COURANT = 0.3
COUPLING = 0.5
DRAG_STEP = 0.5
PHASES = ((0, 5), (5, 3), (8, 3), (11, 3))

def velocity(masses, momentum):
    return momentum / jnp.sqrt(masses * masses + 1.0)

def face_values(values, upwind, along_axis):
    count_faces = values.shape[along_axis] - 3

    def window(start_at):
        return lax.slice_in_dim(values, start_at, start_at + count_faces, axis=along_axis)
    from_low = 1.5 * window(1) - 0.5 * window(0)
    from_high = 1.5 * window(2) - 0.5 * window(3)
    return upwind * from_low + (1.0 - upwind) * from_high

def unpack(halves, level_ids):
    shifts = jnp.arange(2, dtype=jnp.int32)[:, None] * LEV + level_ids[None, :]
    powers = jnp.left_shift(jnp.ones_like(shifts), shifts)
    flag_bits = halves[:, None, None] // powers[None, :, :, None, None] % 2
    return flag_bits.reshape(4, level_ids.shape[0], halves.shape[-2], halves.shape[-1]).astype(jnp.float32)

def step_inputs(packed, classes, step_index, depth_cells, reach_cells, x_first, y_first, total_x, total_y, level_ids):
    tall_rows = classes.shape[0] - 2 * depth_cells + 2 * reach_cells
    wide_cols = classes.shape[1] - 2 * depth_cells + 2 * reach_cells
    offset = depth_cells - reach_cells
    mask_x = unpack(packed[step_index, 0][:, offset:offset + tall_rows, offset - 1:offset + wide_cols], level_ids)
    mask_y = unpack(packed[step_index, 1][:, offset - 1:offset + tall_rows, offset:offset + wide_cols], level_ids)
    region = classes[offset:offset + tall_rows, offset:offset + wide_cols]
    class_table = (region[None] == jnp.arange(NCLASS, dtype=jnp.int32)[:, None, None]).astype(jnp.float32)
    cells_x = x_first - reach_cells + jnp.arange(wide_cols + 1, dtype=jnp.int32)
    cells_y = y_first - reach_cells + jnp.arange(tall_rows + 1, dtype=jnp.int32)
    wall_x = ((cells_x >= 1) & (cells_x <= total_x - 1)).astype(jnp.float32)
    wall_y = ((cells_y >= 1) & (cells_y <= total_y - 1)).astype(jnp.float32)[:, None]
    inside_x = (cells_x[:-1] >= 0) & (cells_x[:-1] < total_x)
    inside_y = (cells_y[:-1] >= 0) & (cells_y[:-1] < total_y)
    inside = (inside_y[:, None] & inside_x[None, :]).astype(jnp.float32)
    weight = DRAG_STEP * jnp.power(0.5, level_ids.astype(jnp.float32))
    return (mask_x, mask_y, wall_x, wall_y, class_table, weight, inside)

def advance(padded, coefficients, mask_x, mask_y, wall_x, wall_y, class_table, weight, inside):
    band_rows = padded[:, :, 2:-2, :]
    band_cols = padded[:, :, :, 2:-2]
    centre = padded[:, :, 2:-2, 2:-2]
    drag_cell = weight[:, None, None] * lax.optimization_barrier(jnp.sum(class_table * coefficients[:, None, None], axis=0))[None]
    carried = []
    for phase_id, (lead_field, members) in enumerate(PHASES):
        speed_x = velocity(band_rows[lead_field], band_rows[lead_field + 1])
        speed_y = velocity(band_cols[lead_field], band_cols[lead_field + 2])
        face_u = 0.5 * (speed_x[:, :, 1:-2] + speed_x[:, :, 2:-1]) * wall_x
        face_v = 0.5 * (speed_y[:, 1:-2, :] + speed_y[:, 2:-1, :]) * wall_y
        flux_x = face_u * face_values(band_rows[lead_field:lead_field + members], mask_x[phase_id], 3)
        flux_y = face_v * face_values(band_cols[lead_field:lead_field + members], mask_y[phase_id], 2)
        carried.append(centre[lead_field:lead_field + members] - COURANT * (flux_x[..., 1:] - flux_x[..., :-1]) - COURANT * (flux_y[:, :, 1:, :] - flux_y[:, :, :-1, :]))
    gas_phase = carried[0]
    gas_x = velocity(gas_phase[0], gas_phase[1])
    gas_y = velocity(gas_phase[0], gas_phase[2])
    pull_x = jnp.zeros_like(gas_x)
    pull_y = jnp.zeros_like(gas_y)
    phases_after = []
    for grain_phase in carried[1:]:
        relax_x = COUPLING * (grain_phase[0] * gas_x - grain_phase[1])
        relax_y = COUPLING * (grain_phase[0] * gas_y - grain_phase[2])
        pull_x = pull_x + relax_x
        pull_y = pull_y + relax_y
        phases_after.append(jnp.stack([grain_phase[0], grain_phase[1] + relax_x, grain_phase[2] + relax_y]))
    gas_after = jnp.concatenate([gas_phase[:1], (gas_phase[1] - pull_x)[None], (gas_phase[2] - pull_y)[None], gas_phase[3:]])
    pieces = []
    for phase_fields in [gas_after] + phases_after:
        speed_x = velocity(phase_fields[0], phase_fields[1])
        speed_y = velocity(phase_fields[0], phase_fields[2])
        drag_loss = drag_cell * jnp.sqrt(speed_x * speed_x + speed_y * speed_y + 1.0)
        pieces.extend([phase_fields[:1], phase_fields[1:3] * (1.0 - drag_loss), phase_fields[3:]])
    return jnp.concatenate(pieces) * inside

def reference(start_state, final_adjoint, face_words, terrain, drag_coef):
    packed = jnp.pad(face_words, ((0, 0), (0, 0), (0, 0), (1, 1), (1, 1)))
    classes = jnp.pad(terrain, 1)
    rim = ((0, 0), (0, 0), (2, 2), (2, 2))

    def one_level(inputs):
        state_level, adjoint_level, level_id = inputs
        level_ids = level_id[None]
        first_inputs = step_inputs(packed, classes, 0, 1, 0, 0, 0, NX, NY, level_ids)
        second_inputs = step_inputs(packed, classes, 1, 1, 0, 0, 0, NX, NY, level_ids)

        def both_steps(state_field, coefficients):
            middle_state = advance(jnp.pad(state_field, rim), coefficients, *first_inputs)
            return advance(jnp.pad(middle_state, rim), coefficients, *second_inputs)
        unused, pullback = jax.vjp(both_steps, state_level[:, None], drag_coef)
        backward, grad_terms = pullback(adjoint_level[:, None])
        return (backward[:, 0], grad_terms)
    backs, grads = lax.map(one_level, (jnp.moveaxis(start_state, 1, 0), jnp.moveaxis(final_adjoint, 1, 0), jnp.arange(LEV, dtype=jnp.int32)))
    grad_scale = math.sqrt(NCLASS / (NX * NY * LEV))
    return (jnp.moveaxis(backs, 0, 1), lax.optimization_barrier(jnp.sum(grads, axis=0)) * grad_scale)
```

```python
import math

import jax
import jax.numpy as jnp
from jax import lax
from jax.experimental import pallas as pl
from jax.experimental.pallas import tpu as pltpu
from jax.sharding import PartitionSpec as P

LEV = 8
NCLASS = 24
FIELDS = 14
ROWS = 8
LANES = 128
PHASES = ((0, 5), (5, 3), (8, 3), (11, 3))
FACE = 0.3 * 0.5 * 0.5
COUPLING = 0.5
DRAG_STEP = 0.5


def roll(v, shift):
    return pltpu.roll(v, shift % LANES if isinstance(shift, int) else shift, 1)


def lane_ids():
    return lax.broadcasted_iota(jnp.int32, (8, LANES), 1)


def strip_pos():
    return lane_ids() % 16


def strip_row():
    return lane_ids() // 16


def level_bits():
    levels = lax.broadcasted_iota(jnp.int32, (8, LANES), 0)
    return [jnp.left_shift(jnp.ones_like(levels), levels + LEV * k) for k in range(2)]


def edge_lanes():
    lanes = lane_ids()
    return (lanes < 2) | (lanes >= LANES - 2)


def spread(ref, index):
    return jnp.broadcast_to(ref[pl.ds(index, 1), :], (8, LANES))


def plane(step, direction, pair):
    return step * 4 + direction * 2 + pair


def position(axis):
    return lax.axis_index(axis), lax.axis_size(axis)


def into_slots(values):
    pos = strip_pos() // 4
    total = jnp.zeros((8, LANES), jnp.float32)
    for slot, value in enumerate(values):
        total = jnp.where(pos == slot, value, total)
    return total


def add_edges(edges_ref, values, row):
    mine = strip_row() == row
    for f, value in enumerate(values):
        edges_ref[f] = jnp.where(mine, roll(value, 16 * row + 4), edges_ref[f])


def zero_edges(edges_ref, count=FIELDS):
    for f in range(count):
        edges_ref[f] = jnp.zeros((8, LANES), edges_ref.dtype)


def edge_payload(edges_ref, out_ref):
    for g in range(4):
        fields = range(4 * g, min(4 * g + 4, FIELDS))
        out_ref[g] = into_slots([roll(edges_ref[f], 4 * (f % 4) - 2) for f in fields])


def side_payloads(even_ref, odd_ref):
    index, _ = position("gx")
    is_even = index % 2 == 0

    def pick(k):
        a = even_ref[k]
        b = jnp.zeros_like(a) if odd_ref is None else odd_ref[k]
        return jnp.where(is_even, b, a), jnp.where(is_even, a, b)

    return pick


def build_strip(edges_ref, pick, strip_ref):
    pos = strip_pos()
    for g in range(4):
        left, right = pick(g)
        for f in range(4 * g, min(4 * g + 4, FIELDS)):
            q = f % 4
            own = edges_ref[f]
            value = jnp.where(pos < 4, own, roll(right, 2 - 4 * q))
            value = jnp.where(pos < 6, value, roll(left, 6 - 4 * q))
            value = jnp.where(pos < 8, value, roll(own, 4))
            strip_ref[f] = jnp.where(pos < 12, value, 0.0)


def strip_words(edge_words_ref, left_words, which):
    pos = strip_pos()
    own = spread(edge_words_ref, which)
    left = jnp.broadcast_to(left_words[which : which + 1], (8, LANES))
    value = jnp.where(pos < 4, own, roll(own, 4))
    return jnp.where(pos == 7, roll(left, 4), value)


def face_walls():
    gx, nx = position("gx")
    pos = strip_pos()
    shut = ((pos == 7) & (gx == 0)) | ((pos == 3) & (gx == nx - 1))
    return jnp.where(shut, 0.0, FACE)


def row_wall(j):
    gy, ny = position("gy")
    shut = ((j == 0) & (gy == 0)) | ((j == ROWS) & (gy == ny - 1))
    return jnp.where(shut, 0.0, FACE)


def inverse_root(mass):
    return lax.rsqrt(mass * mass + 1.0)


def gather_edges(v):
    pos = strip_pos()
    return jnp.where((pos == 4) | (pos == 5), roll(v, -4), v)


def face_values(behind, here, ahead, beyond, flag):
    return jnp.where(flag, 3.0 * here - behind, 3.0 * ahead - beyond)


def forward_strip(step, strip, edge_words, left_words, sfv, su, sdx):
    bits = level_bits()
    walls = face_walls()
    for p, (lead, members) in enumerate(PHASES):
        word = strip_words(edge_words, left_words, plane(step, 0, p // 2))
        flag = (word & bits[p % 2]) != 0
        u = strip[lead + 1] * inverse_root(strip[lead])
        speed = walls * (u + roll(u, -1))
        su[p] = speed
        for f in range(lead, lead + members):
            c = strip[f]
            ahead = roll(c, -1)
            value = face_values(roll(c, 1), c, ahead, roll(c, -2), flag)
            sfv[f] = value
            flux = speed * value
            sdx[f] = gather_edges(flux - roll(flux, 1))


def forward_rows(step, ext, words, low_words, fvy, vy):
    bits = level_bits()

    def face(j, carry):
        wall = row_wall(j)
        for p, (lead, members) in enumerate(PHASES):
            here = spread(words, plane(step, 1, p // 2) * ROWS + jnp.maximum(j - 1, 0))
            low = jnp.broadcast_to(low_words[plane(step, 1, p // 2)][None], (8, LANES))
            word = jnp.where(j == 0, low, here)
            flag = (word & bits[p % 2]) != 0
            v_low = ext[lead + 2, j + 1] * inverse_root(ext[lead, j + 1])
            v_high = ext[lead + 2, j + 2] * inverse_root(ext[lead, j + 2])
            vy[p, j] = wall * (v_low + v_high)
            for f in range(lead, lead + members):
                fvy[f, j] = face_values(ext[f, j], ext[f, j + 1], ext[f, j + 2], ext[f, j + 3], flag)
        return carry

    lax.fori_loop(0, ROWS + 1, face, 0)


def carried_row(step, r, ext, words, sdx, fvx, ux, fvy, vy):
    bits = level_bits()
    edges = edge_lanes()
    carried = []
    for p, (lead, members) in enumerate(PHASES):
        word = spread(words, plane(step, 0, p // 2) * ROWS + r)
        flag = (word & bits[p % 2]) != 0
        u = ext[lead + 1, r + 2] * inverse_root(ext[lead, r + 2])
        speed = FACE * (u + roll(u, -1))
        ux[p, r] = speed
        below, above = vy[p, r], vy[p, r + 1]
        for f in range(lead, lead + members):
            c = ext[f, r + 2]
            value = face_values(roll(c, 1), c, roll(c, -1), roll(c, -2), flag)
            fvx[f, r] = value
            flux = speed * value
            along_x = jnp.where(edges, roll(sdx[f], 124 - 16 * r), flux - roll(flux, 1))
            along_y = above * fvy[f, r + 1] - below * fvy[f, r]
            carried.append(c - along_x - along_y)
    return carried


def coupled(c):
    s = inverse_root(c[0])
    u, v = c[1] * s, c[2] * s
    gas_x, gas_y = c[1], c[2]
    out = [None] * FIELDS
    for lead, _ in PHASES[1:]:
        pull_x = COUPLING * (c[lead] * u - c[lead + 1])
        pull_y = COUPLING * (c[lead] * v - c[lead + 2])
        gas_x, gas_y = gas_x - pull_x, gas_y - pull_y
        out[lead] = c[lead]
        out[lead + 1], out[lead + 2] = c[lead + 1] + pull_x, c[lead + 2] + pull_y
    out[0], out[1], out[2], out[3], out[4] = c[0], gas_x, gas_y, c[3], c[4]
    return out, s, u, v


def stepped(c, drag):
    q, _, _, _ = coupled(c)
    for lead, _ in PHASES:
        s = inverse_root(q[lead])
        u, v = q[lead + 1] * s, q[lead + 2] * s
        factor = 1.0 - drag * jnp.sqrt(u * u + v * v + 1.0)
        q[lead + 1], q[lead + 2] = q[lead + 1] * factor, q[lead + 2] * factor
    return q


def stepped_back(c, drag, a):
    q, s0, gas_u, gas_v = coupled(c)
    a = list(a)
    drag_terms = jnp.zeros((8, LANES), jnp.float32)
    for lead, _ in PHASES:
        m, x, y = q[lead], q[lead + 1], q[lead + 2]
        s = s0 if lead == 0 else inverse_root(m)
        u, v = x * s, y * s
        energy = u * u + v * v
        root = lax.rsqrt(energy + 1.0)
        w = (energy + 1.0) * root
        dot = a[lead + 1] * x + a[lead + 2] * y
        drag_terms = drag_terms - w * dot
        k = drag * dot * root
        factor = 1.0 - drag * w
        ks = k * s
        a[lead + 1] = a[lead + 1] * factor - ks * u
        a[lead + 2] = a[lead + 2] * factor - ks * v
        a[lead] = a[lead] + k * energy * m * (s * s)
    du = jnp.zeros_like(drag_terms)
    dv = jnp.zeros_like(drag_terms)
    for lead, _ in PHASES[1:]:
        rx, ry = COUPLING * (a[lead + 1] - a[1]), COUPLING * (a[lead + 2] - a[2])
        a[lead] = a[lead] + rx * gas_u + ry * gas_v
        du, dv = du + c[lead] * rx, dv + c[lead] * ry
        a[lead + 1], a[lead + 2] = a[lead + 1] - rx, a[lead + 2] - ry
    a[1], a[2] = a[1] + du * s0, a[2] + dv * s0
    a[0] = a[0] - (gas_u * du + gas_v * dv) * c[0] * (s0 * s0)
    return a, drag_terms


def add_speed_terms(total, state, lead, du, dv):
    m, x, y = state
    s = inverse_root(m)
    pull = None
    if du is not None:
        total[lead + 1] = total[lead + 1] + s * du
        pull = x * s * du
    if dv is not None:
        total[lead + 2] = total[lead + 2] + s * dv
        pull = y * s * dv if pull is None else pull + y * s * dv
    total[lead] = total[lead] - pull * m * (s * s)


def scatter_x(a, value, speed, flag):
    ahead = roll(a, -1) - a
    g = speed * ahead
    low = jnp.where(flag, g, 0.0)
    high = roll(g - low, 1)
    return 3.0 * (low + high) - roll(low, -1) - roll(high, 1), value * ahead


def expand_edges(own):
    pos = strip_pos()
    value = jnp.where(pos < 4, own, jnp.where((pos >= 8) & (pos < 12), roll(own, 4), 0.0))
    return value


def backward_strip(step, strip, edges_a, edge_words, left_words, sfv, su, sdc, sdu, out_c):
    bits = level_bits()
    walls = face_walls()
    ghosts = []
    for p, (lead, members) in enumerate(PHASES):
        word = strip_words(edge_words, left_words, plane(step, 0, p // 2))
        flag = (word & bits[p % 2]) != 0
        speed = su[p]
        du = jnp.zeros((8, LANES), jnp.float32)
        total = {}
        for f in range(lead, lead + members):
            total[f], term = scatter_x(expand_edges(edges_a[f]), sfv[f], speed, flag)
            sdc[f] = gather_edges(total[f])
            du = du + term
        du = walls * du
        du = du + roll(du, 1)
        sdu[p] = gather_edges(du)
        add_speed_terms(total, (strip[lead], strip[lead + 1], strip[lead + 2]), lead, du, None)
        ghosts.extend(total[f] for f in range(lead, lead + members))
    for g in range(4):
        fields = range(4 * g, min(4 * g + 4, FIELDS))
        out_c[g] = into_slots([roll(ghosts[f], 4 * (f % 4) - 4) for f in fields])


def backward_fluxes(step, ext, words, low_words, a_ext, fvx, ux, fvy, vy, sdc, sdu, gl, gh, dvy, put):
    bits = level_bits()
    edges = edge_lanes()
    zero = jnp.zeros((8, LANES), jnp.float32)
    for k in (0, 1, 2, 12, 13, 14):
        for f in range(FIELDS):
            gl[f, k] = zero
            gh[f, k] = zero
        for p in range(4):
            dvy[p, k] = zero

    def face(j, carry):
        wall = row_wall(j)
        for p, (lead, members) in enumerate(PHASES):
            here = spread(words, plane(step, 1, p // 2) * ROWS + jnp.maximum(j - 1, 0))
            low_word = jnp.broadcast_to(low_words[plane(step, 1, p // 2)][None], (8, LANES))
            word = jnp.where(j == 0, low_word, here)
            flag = (word & bits[p % 2]) != 0
            speed = vy[p, j]
            dv = jnp.zeros((8, LANES), jnp.float32)
            for f in range(lead, lead + members):
                ahead = a_ext[f, j + 1] - a_ext[f, j]
                g = speed * ahead
                low = jnp.where(flag, g, 0.0)
                gl[f, j + 3] = low
                gh[f, j + 3] = g - low
                dv = dv + fvy[f, j] * ahead
            dvy[p, j + 3] = wall * dv
        return carry

    lax.fori_loop(0, ROWS + 1, face, 0)

    def along_y(f, i):
        return 3.0 * (gl[f, i + 4] + gh[f, i + 3]) - gl[f, i + 5] - gh[f, i + 2]

    def own(r, carry):
        total = [None] * FIELDS
        for p, (lead, members) in enumerate(PHASES):
            word = spread(words, plane(step, 0, p // 2) * ROWS + r)
            flag = (word & bits[p % 2]) != 0
            speed = ux[p, r]
            du = jnp.zeros((8, LANES), jnp.float32)
            for f in range(lead, lead + members):
                a = a_ext[f, r + 1]
                part, term = scatter_x(a, fvx[f, r], speed, flag)
                part = jnp.where(edges, roll(sdc[f], 124 - 16 * r), part)
                total[f] = a + part + along_y(f, r)
                du = du + term
            du = FACE * (du + roll(du, 1))
            du = jnp.where(edges, roll(sdu[p], 124 - 16 * r), du)
            dv = dvy[p, r + 4] + dvy[p, r + 3]
            state = (ext[lead, r + 2], ext[lead + 1, r + 2], ext[lead + 2, r + 2])
            add_speed_terms(total, state, lead, du, dv)
        put(r, total)
        return carry

    lax.fori_loop(0, ROWS, own, 0)

    def ghost(t, carry):
        i = jnp.where(t < 2, t - 2, t + 6)
        total = [along_y(f, i) for f in range(FIELDS)]
        for p, (lead, members) in enumerate(PHASES):
            dv = dvy[p, i + 4] + dvy[p, i + 3]
            state = (ext[lead, i + 2], ext[lead + 1, i + 2], ext[lead + 2, i + 2])
            add_speed_terms(total, state, lead, None, dv)
        put(i, total)
        return carry

    lax.fori_loop(0, 4, ghost, 0)


def drag_row(drag_ref, r):
    levels = lax.broadcasted_iota(jnp.int32, (8, LANES), 0)
    weight = jnp.full((8, LANES), DRAG_STEP, jnp.float32)
    for k in range(3):
        weight = jnp.where((levels // 2**k) % 2 == 1, weight * 0.5 ** (2**k), weight)
    return weight, weight * spread(drag_ref, r)


def drag_table(terrain, coef, drag_ref):
    classes = terrain[...]
    drag = jnp.zeros((8, LANES), jnp.float32)
    for k in range(NCLASS):
        drag = jnp.where(classes == k, coef[k], drag)
    drag_ref[...] = drag


def row_bases():
    gy, _ = position("gy")
    is_even = gy % 2 == 0
    return is_even


def fill_ghost_rows(ext, from_a, from_b):
    is_even = row_bases()
    a_row = jnp.where(is_even, ROWS + 2, 0)
    b_row = jnp.where(is_even, 0, ROWS + 2)
    for f in range(FIELDS):
        for j in range(2):
            ext[f, a_row + j] = from_a[2 * f + j]
            ext[f, b_row + j] = from_b[2 * f + j]


def put_edge_rows(source, offset, to_a, to_b):
    is_even = row_bases()
    a_row = jnp.where(is_even, ROWS - 2, 0) + offset
    b_row = jnp.where(is_even, 0, ROWS - 2) + offset
    for f in range(FIELDS):
        for j in range(2):
            to_a[2 * f + j] = source[f, a_row + j]
            to_b[2 * f + j] = source[f, b_row + j]


def pack_kernel(start, words, rows, edges, edge_words, to_a, to_b, to_c):
    zero_edges(edges)
    edge_words[...] = jnp.zeros((8, LANES), jnp.int32)

    def one_row(r, carry):
        values = [start[f, pl.ds(r, 8, stride=8), :] for f in range(FIELDS)]
        for f in range(FIELDS):
            rows[f, r] = values[f]
        add_edges(edges, values, r)
        mine = strip_row() == r
        edge_words[...] = jnp.where(mine, roll(words[pl.ds(r, 8, stride=8), :], 16 * r + 4), edge_words[...])
        return carry

    lax.fori_loop(0, ROWS, one_row, 0)
    put_edge_rows(rows, 0, to_a, to_b)
    top = words[pl.ds(ROWS - 1, 8, stride=8), :].astype(jnp.float32)
    to_a[2 * FIELDS] = top
    to_b[2 * FIELDS] = top
    edge_payload(edges, to_c)
    to_c[4] = edge_words[...].astype(jnp.float32)


def neighbour_words(from_a, from_b, pick):
    low = jnp.where(row_bases(), from_b[2 * FIELDS], from_a[2 * FIELDS]).astype(jnp.int32)
    left, _ = pick(4)
    return low, left.astype(jnp.int32)


def first_kernel(has_odd):
    def kernel(*refs):
        rows, edges, edge_words, words, terrain, coef, from_a, from_b, from_c = refs[:9]
        from_d = refs[9] if has_odd else None
        outs = refs[9 + has_odd :]
        (ext, strip, carried_ref, fvx, ux, fvy, vy, sfv, su, drag_ref, low_ref, left_ref) = outs[:12]
        middle, middle_edges, to_a, to_b, to_c = outs[12:17]
        (sdx,) = outs[17:]
        pick = side_payloads(from_c, from_d)

        def copy_row(r, carry):
            for f in range(FIELDS):
                ext[f, r + 2] = rows[f, r]
            return carry

        lax.fori_loop(0, ROWS, copy_row, 0)
        fill_ghost_rows(ext, from_a, from_b)
        build_strip(edges, pick, strip)
        low_words, left_words = neighbour_words(from_a, from_b, pick)
        low_ref[...] = low_words
        left_ref[...] = left_words
        drag_table(terrain, coef, drag_ref)
        forward_strip(0, strip, edge_words, left_words, sfv, su, sdx)
        forward_rows(0, ext, words, low_words, fvy, vy)
        zero_edges(middle_edges)

        def one_row(r, carry):
            c = carried_row(0, r, ext, words, sdx, fvx, ux, fvy, vy)
            for f in range(FIELDS):
                carried_ref[f, r] = c[f]
            _, drag = drag_row(drag_ref, r)
            q = stepped(c, drag)
            for f in range(FIELDS):
                middle[f, r] = q[f]
            add_edges(middle_edges, q, r)
            return carry

        lax.fori_loop(0, ROWS, one_row, 0)
        put_edge_rows(middle, 0, to_a, to_b)
        edge_payload(middle_edges, to_c)

    return kernel


def ghost_rows_out(part, to_a, to_b):
    is_even = row_bases()
    a_row = jnp.where(is_even, ROWS + 2, 0)
    b_row = jnp.where(is_even, 0, ROWS + 2)
    for f in range(FIELDS):
        for j in range(2):
            to_a[2 * f + j] = part[f, a_row + j]
            to_b[2 * f + j] = part[f, b_row + j]


def second_kernel(has_odd):
    def kernel(*refs):
        middle, middle_edges, edge_words, words, drag_ref, low_ref, left_ref, adjoint = refs[:8]
        from_a, from_b, from_c = refs[8:11]
        from_d = refs[11] if has_odd else None
        outs = refs[11 + has_odd :]
        part, to_a, to_b, to_c, grad_cells = outs[:5]
        (ext, strip, fvx, ux, fvy, vy, sfv, su, sdx, a_ext, edges_a, sdc, sdu, gl, gh, dvy) = outs[5:]
        pick = side_payloads(from_c, from_d)
        low_words, left_words = low_ref[...], left_ref[...]

        def copy_row(r, carry):
            for f in range(FIELDS):
                ext[f, r + 2] = middle[f, r]
            return carry

        lax.fori_loop(0, ROWS, copy_row, 0)
        fill_ghost_rows(ext, from_a, from_b)
        build_strip(middle_edges, pick, strip)
        forward_strip(1, strip, edge_words, left_words, sfv, su, sdx)
        forward_rows(1, ext, words, low_words, fvy, vy)
        zero_edges(edges_a)
        for f in range(FIELDS):
            a_ext[f, 0] = jnp.zeros((8, LANES), jnp.float32)
            a_ext[f, ROWS + 1] = jnp.zeros((8, LANES), jnp.float32)

        def one_row(r, carry):
            c = carried_row(1, r, ext, words, sdx, fvx, ux, fvy, vy)
            weight, drag = drag_row(drag_ref, r)
            a = [adjoint[f, pl.ds(r, 8, stride=8), :] for f in range(FIELDS)]
            a, terms = stepped_back(c, drag, a)
            grad_cells[pl.ds(r, 1), :] = jnp.sum(weight * terms, axis=0, keepdims=True)
            for f in range(FIELDS):
                a_ext[f, r + 1] = a[f]
            add_edges(edges_a, a, r)
            return carry

        lax.fori_loop(0, ROWS, one_row, 0)
        backward_strip(1, strip, edges_a, edge_words, left_words, sfv, su, sdc, sdu, to_c)

        def put(row, values):
            for f in range(FIELDS):
                part[f, row + 2] = values[f]

        backward_fluxes(1, ext, words, low_words, a_ext, fvx, ux, fvy, vy, sdc, sdu, gl, gh, dvy, put)
        ghost_rows_out(part, to_a, to_b)

    return kernel


def collect(part, from_a, from_b, pick, incoming):
    is_even = row_bases()
    a_row = jnp.where(is_even, ROWS, 2)
    b_row = jnp.where(is_even, 2, ROWS)
    for f in range(FIELDS):
        for j in range(2):
            part[f, a_row + j] = part[f, a_row + j] + from_a[2 * f + j]
            part[f, b_row + j] = part[f, b_row + j] + from_b[2 * f + j]
    pos = strip_pos()
    for g in range(4):
        left, right = pick(g)
        for f in range(4 * g, min(4 * g + 4, FIELDS)):
            q = f % 4
            at_left = (pos == 4) | (pos == 5)
            at_right = (pos == 2) | (pos == 3)
            value = jnp.where(at_left, roll(left, 4 - 4 * q), jnp.where(at_right, roll(right, -4 * q), 0.0))
            incoming[f] = value


def third_kernel(has_odd):
    def kernel(*refs):
        (part_in, grad_cells, terrain, ext, strip, carried_ref, fvx, ux, fvy, vy, sfv, su) = refs[:12]
        drag_ref, low_ref, left_ref, edge_words, words = refs[12:17]
        from_a, from_b, from_c = refs[17:20]
        from_d = refs[20] if has_odd else None
        outs = refs[20 + has_odd :]
        part, to_a, to_b, to_c, grads = outs[:5]
        (incoming, a_ext, edges_a, sdc, sdu, gl, gh, dvy, cells) = outs[5:]
        pick = side_payloads(from_c, from_d)
        low_words, left_words = low_ref[...], left_ref[...]

        def copy_row(r, carry):
            for f in range(FIELDS):
                part[f, r + 2] = part_in[f, r + 2]
            return carry

        lax.fori_loop(0, ROWS, copy_row, 0)
        collect(part, from_a, from_b, pick, incoming)
        zero_edges(edges_a)
        for f in range(FIELDS):
            a_ext[f, 0] = jnp.zeros((8, LANES), jnp.float32)
            a_ext[f, ROWS + 1] = jnp.zeros((8, LANES), jnp.float32)
        edges = edge_lanes()

        def one_row(r, carry):
            c = [carried_ref[f, r] for f in range(FIELDS)]
            weight, drag = drag_row(drag_ref, r)
            a = [
                part[f, r + 2] + jnp.where(edges, roll(incoming[f], 124 - 16 * r), 0.0)
                for f in range(FIELDS)
            ]
            a, terms = stepped_back(c, drag, a)
            cells[pl.ds(r, 1), :] = jnp.sum(weight * terms, axis=0, keepdims=True)
            for f in range(FIELDS):
                a_ext[f, r + 1] = a[f]
            add_edges(edges_a, a, r)
            return carry

        lax.fori_loop(0, ROWS, one_row, 0)
        total = cells[...] + grad_cells[...]
        classes = terrain[...]
        lanes = lane_ids()
        binned = jnp.zeros((8, LANES), jnp.float32)
        for k in range(NCLASS):
            one = jnp.sum(jnp.where(classes == k, total, 0.0), axis=0, keepdims=True)
            one = jnp.sum(one, axis=1, keepdims=True)
            binned = jnp.where(lanes == k, one, binned)
        grads[...] = binned
        backward_strip(0, strip, edges_a, edge_words, left_words, sfv, su, sdc, sdu, to_c)

        def put(row, values):
            for f in range(FIELDS):
                part[f, row + 2] = values[f]

        backward_fluxes(0, ext, words, low_words, a_ext, fvx, ux, fvy, vy, sdc, sdu, gl, gh, dvy, put)
        ghost_rows_out(part, to_a, to_b)

    return kernel


def last_kernel(has_odd):
    def kernel(*refs):
        part_in, from_a, from_b, from_c = refs[:4]
        from_d = refs[4] if has_odd else None
        out, part, incoming = refs[4 + has_odd :]
        pick = side_payloads(from_c, from_d)

        def copy_row(r, carry):
            for f in range(FIELDS):
                part[f, r + 2] = part_in[f, r + 2]
            return carry

        lax.fori_loop(0, ROWS, copy_row, 0)
        collect(part, from_a, from_b, pick, incoming)
        edges = edge_lanes()

        def one_row(r, carry):
            for f in range(FIELDS):
                value = part[f, r + 2] + jnp.where(edges, roll(incoming[f], 124 - 16 * r), 0.0)
                out[f, pl.ds(r, 8, stride=8), :] = value
            return carry

        lax.fori_loop(0, ROWS, one_row, 0)

    return kernel


def shaped(*shape, dtype=jnp.float32):
    return jax.ShapeDtypeStruct(shape, dtype)


def tiles(*shape, dtype=jnp.float32):
    return shaped(*shape, 8, LANES, dtype=dtype)


def scratch(*shape, dtype=jnp.float32):
    return pltpu.VMEM((*shape, 8, LANES), dtype)


def call(kernel, outs, scratches, args, smem=()):
    in_specs = [
        pl.BlockSpec(memory_space=pltpu.SMEM if k in smem else pltpu.VMEM) for k in range(len(args))
    ]
    return pl.pallas_call(
        kernel,
        out_shape=outs,
        in_specs=in_specs,
        out_specs=[pl.BlockSpec(memory_space=pltpu.VMEM)] * len(outs),
        scratch_shapes=scratches,
        compiler_params=pltpu.CompilerParams(vmem_limit_bytes=32 << 20),
    )(*args)


def swap(x, axis, first):
    peers = lax.axis_size(axis)
    pairs = [(i, i + 1) for i in range(first, peers - 1, 2)]
    if not pairs:
        return None
    return lax.ppermute(x, axis, pairs + [(j, i) for i, j in pairs])


def exchange(to_a, to_b, to_c):
    from_a = swap(to_a, "gy", 0)
    from_b = swap(to_b, "gy", 1)
    from_c = swap(to_c, "gx", 0)
    from_d = swap(to_c, "gx", 1)
    if from_b is None:
        from_b = jnp.zeros_like(to_b)
    return (from_a, from_b, from_c) + (() if from_d is None else (from_d,))


def summed_over(x, axis):
    peers = lax.axis_size(axis)
    distance = 1
    while distance < peers:
        x = x + lax.ppermute(x, axis, [(i, i ^ distance) for i in range(peers)])
        distance *= 2
    return x


def body(start_state, final_adjoint, face_words, terrain, drag_coef):
    has_odd = lax.axis_size("gx") > 2
    start = start_state.reshape(FIELDS, LEV * ROWS, LANES)
    adjoint = final_adjoint.reshape(FIELDS, LEV * ROWS, LANES)
    words = face_words.reshape(8 * ROWS, LANES)
    ints = jnp.int32

    rows, edges, edge_words, to_a, to_b, to_c = call(
        pack_kernel,
        [tiles(14, 8), tiles(14), tiles(dtype=ints), tiles(29), tiles(29), tiles(5)],
        [],
        [start, words],
    )
    got = exchange(to_a, to_b, to_c)
    faces = [tiles(14, 8), tiles(4, 8), tiles(14, 9), tiles(4, 9), tiles(14), tiles(4)]
    res = call(
        first_kernel(has_odd),
        [tiles(14, 12), tiles(14), tiles(14, 8), *faces, tiles(), tiles(dtype=ints), tiles(dtype=ints)]
        + [tiles(14, 8), tiles(14), tiles(28), tiles(28), tiles(4)],
        [scratch(14)],
        [rows, edges, edge_words, words, terrain, drag_coef, *got],
        smem=(5,),
    )
    ext, strip, carried_ref = res[:3]
    saved = res[3:9]
    drag_ref, low_ref, left_ref = res[9:12]
    middle, middle_edges = res[12:14]
    got = exchange(*res[14:17])
    back = [scratch(14, 10), scratch(14), scratch(14), scratch(4), scratch(14, 15), scratch(14, 15), scratch(4, 15)]
    part, to_a, to_b, to_c, grad_cells = call(
        second_kernel(has_odd),
        [tiles(14, 12), tiles(28), tiles(28), tiles(4), tiles()],
        [scratch(14, 12), scratch(14), scratch(14, 8), scratch(4, 8), scratch(14, 9), scratch(4, 9)]
        + [scratch(14), scratch(4), scratch(14), *back],
        [middle, middle_edges, edge_words, words, drag_ref, low_ref, left_ref, adjoint, *got],
    )
    got = exchange(to_a, to_b, to_c)
    part, to_a, to_b, to_c, grads = call(
        third_kernel(has_odd),
        [tiles(14, 12), tiles(28), tiles(28), tiles(4), tiles()],
        [scratch(14), *back, scratch()],
        [part, grad_cells, terrain, ext, strip, carried_ref, *saved]
        + [drag_ref, low_ref, left_ref, edge_words, words, *got],
    )
    got = exchange(to_a, to_b, to_c)
    (out,) = call(
        last_kernel(has_odd),
        [shaped(FIELDS, LEV * ROWS, LANES)],
        [scratch(14, 12), scratch(14)],
        [part, *got],
    )
    total_cells = terrain.size * lax.axis_size("gx") * lax.axis_size("gy") * LEV
    grad_scale = math.sqrt(NCLASS / total_cells)
    summed = summed_over(summed_over(grads, "gy"), "gx")[0, :NCLASS]
    return (out.reshape(start_state.shape), summed * grad_scale)


def solution(mesh):
    placed = (
        P(None, None, "gy", "gx"),
        P(None, None, "gy", "gx"),
        P(None, None, None, "gy", "gx"),
        P("gy", "gx"),
        P(),
    )
    return jax.shard_map(
        body,
        mesh=mesh,
        in_specs=placed,
        out_specs=(P(None, None, "gy", "gx"), P()),
        check_vma=False,
    )
```

```python
import math

import jax
import jax.numpy as jnp
from jax import lax
from jax.experimental import pallas as pl
from jax.experimental.pallas import tpu as pltpu
from jax.sharding import PartitionSpec as P

LEV = 8
NCLASS = 24
FIELDS = 14
ROWS = 8
LANES = 128
PHASES = ((0, 5), (5, 3), (8, 3), (11, 3))
FACE = 0.3 * 0.5 * 0.5
COUPLING = 0.5
DRAG_STEP = 0.5
TERRAIN_SLOT = 2


def roll(v, shift):
    return pltpu.roll(v, shift % LANES if isinstance(shift, int) else shift, 1)


def lane_ids():
    return lax.broadcasted_iota(jnp.int32, (8, LANES), 1)


def strip_pos():
    return lane_ids() % 16


def strip_row():
    return lane_ids() // 16


def level_bits():
    levels = lax.broadcasted_iota(jnp.int32, (8, LANES), 0)
    return [jnp.left_shift(jnp.ones_like(levels), levels + LEV * k) for k in range(2)]


def edge_lanes():
    lanes = lane_ids()
    return (lanes < 2) | (lanes >= LANES - 2)


def spread(ref, index):
    return jnp.broadcast_to(ref[pl.ds(index, 1), :], (8, LANES))


def plane(step, direction, pair):
    return step * 4 + direction * 2 + pair


def position(axis):
    return lax.axis_index(axis), lax.axis_size(axis)


def into_slots(values):
    pos = strip_pos() // 4
    total = jnp.zeros((8, LANES), jnp.float32)
    for slot, value in enumerate(values):
        total = jnp.where(pos == slot, value, total)
    return total


def add_edges(edges_ref, values, row):
    mine = strip_row() == row
    for f, value in enumerate(values):
        edges_ref[f] = jnp.where(mine, roll(value, 16 * row + 4), edges_ref[f])


def zero_edges(edges_ref, count=FIELDS):
    for f in range(count):
        edges_ref[f] = jnp.zeros((8, LANES), edges_ref.dtype)


def edge_payload(edges_ref, out_ref):
    for g in range(4):
        fields = range(4 * g, min(4 * g + 4, FIELDS))
        out_ref[g] = into_slots([roll(edges_ref[f], 4 * (f % 4) - 2) for f in fields])


def side_payloads(even_ref, odd_ref):
    index, _ = position("gx")
    is_even = index % 2 == 0

    def pick(k):
        a = even_ref[k]
        b = jnp.zeros_like(a) if odd_ref is None else odd_ref[k]
        return jnp.where(is_even, b, a), jnp.where(is_even, a, b)

    return pick


def build_strip(edges_ref, pick, strip_ref):
    pos = strip_pos()
    for g in range(4):
        left, right = pick(g)
        for f in range(4 * g, min(4 * g + 4, FIELDS)):
            q = f % 4
            own = edges_ref[f]
            value = jnp.where(pos < 4, own, roll(right, 2 - 4 * q))
            value = jnp.where(pos < 6, value, roll(left, 6 - 4 * q))
            value = jnp.where(pos < 8, value, roll(own, 4))
            strip_ref[f] = jnp.where(pos < 12, value, 0.0)


def strip_words(edge_words_ref, left_words, which):
    pos = strip_pos()
    own = spread(edge_words_ref, which)
    left = jnp.broadcast_to(left_words[which : which + 1], (8, LANES))
    value = jnp.where(pos < 4, own, roll(own, 4))
    return jnp.where(pos == 7, roll(left, 4), value)


def strip_classes(edge_words_ref, pick):
    pos = strip_pos()
    own = spread(edge_words_ref, TERRAIN_SLOT)
    left, right = [jnp.broadcast_to(v[TERRAIN_SLOT : TERRAIN_SLOT + 1], (8, LANES)).astype(jnp.int32) for v in pick(4)]
    value = jnp.where(pos < 4, own, jnp.where(pos < 6, right, jnp.where(pos < 8, roll(left, 4), roll(own, 4))))
    return value


def face_walls():
    gx, nx = position("gx")
    pos = strip_pos()
    shut = ((pos == 7) & (gx == 0)) | ((pos == 3) & (gx == nx - 1))
    return jnp.where(shut, 0.0, FACE)


def row_wall(j):
    gy, ny = position("gy")
    shut = ((j == 0) & (gy == 0)) | ((j == ROWS) & (gy == ny - 1))
    return jnp.where(shut, 0.0, FACE)


def inverse_root(mass):
    return lax.rsqrt(mass * mass + 1.0)


def gather_edges(v):
    pos = strip_pos()
    return jnp.where((pos == 4) | (pos == 5), roll(v, -4), v)


def face_values(behind, here, ahead, beyond, flag):
    return jnp.where(flag, 3.0 * here - behind, 3.0 * ahead - beyond)


def forward_strip(step, strip, edge_words, left_words, sfv, su, sdx):
    bits = level_bits()
    walls = face_walls()
    for p, (lead, members) in enumerate(PHASES):
        word = strip_words(edge_words, left_words, plane(step, 0, p // 2))
        flag = (word & bits[p % 2]) != 0
        u = strip[lead + 1] * inverse_root(strip[lead])
        speed = walls * (u + roll(u, -1))
        su[p] = speed
        for f in range(lead, lead + members):
            c = strip[f]
            ahead = roll(c, -1)
            value = face_values(roll(c, 1), c, ahead, roll(c, -2), flag)
            sfv[f] = value
            flux = speed * value
            sdx[f] = gather_edges(flux - roll(flux, 1))


def forward_rows(step, ext, words, low_words, fvy, vy):
    bits = level_bits()

    def face(j, carry):
        wall = row_wall(j)
        for p, (lead, members) in enumerate(PHASES):
            here = spread(words, plane(step, 1, p // 2) * ROWS + jnp.maximum(j - 1, 0))
            low = jnp.broadcast_to(low_words[plane(step, 1, p // 2)][None], (8, LANES))
            word = jnp.where(j == 0, low, here)
            flag = (word & bits[p % 2]) != 0
            v_low = ext[lead + 2, j + 1] * inverse_root(ext[lead, j + 1])
            v_high = ext[lead + 2, j + 2] * inverse_root(ext[lead, j + 2])
            vy[p, j] = wall * (v_low + v_high)
            for f in range(lead, lead + members):
                fvy[f, j] = face_values(ext[f, j], ext[f, j + 1], ext[f, j + 2], ext[f, j + 3], flag)
        return carry

    lax.fori_loop(0, ROWS + 1, face, 0)


def carried_row(step, r, ext, words, sdx, fvx, ux, fvy, vy):
    bits = level_bits()
    edges = edge_lanes()
    carried = []
    for p, (lead, members) in enumerate(PHASES):
        word = spread(words, plane(step, 0, p // 2) * ROWS + r)
        flag = (word & bits[p % 2]) != 0
        u = ext[lead + 1, r + 2] * inverse_root(ext[lead, r + 2])
        speed = FACE * (u + roll(u, -1))
        ux[p, r] = speed
        below, above = vy[p, r], vy[p, r + 1]
        for f in range(lead, lead + members):
            c = ext[f, r + 2]
            value = face_values(roll(c, 1), c, roll(c, -1), roll(c, -2), flag)
            fvx[f, r] = value
            flux = speed * value
            along_x = jnp.where(edges, roll(sdx[f], 124 - 16 * r), flux - roll(flux, 1))
            along_y = above * fvy[f, r + 1] - below * fvy[f, r]
            carried.append(c - along_x - along_y)
    return carried


def coupled(c):
    s = inverse_root(c[0])
    u, v = c[1] * s, c[2] * s
    gas_x, gas_y = c[1], c[2]
    out = [None] * FIELDS
    for lead, _ in PHASES[1:]:
        pull_x = COUPLING * (c[lead] * u - c[lead + 1])
        pull_y = COUPLING * (c[lead] * v - c[lead + 2])
        gas_x, gas_y = gas_x - pull_x, gas_y - pull_y
        out[lead] = c[lead]
        out[lead + 1], out[lead + 2] = c[lead + 1] + pull_x, c[lead + 2] + pull_y
    out[0], out[1], out[2], out[3], out[4] = c[0], gas_x, gas_y, c[3], c[4]
    return out, s, u, v


def dragged(q, drag):
    q = list(q)
    for lead, _ in PHASES:
        s = inverse_root(q[lead])
        u, v = q[lead + 1] * s, q[lead + 2] * s
        factor = 1.0 - drag * jnp.sqrt(u * u + v * v + 1.0)
        q[lead + 1], q[lead + 2] = q[lead + 1] * factor, q[lead + 2] * factor
    return q


def drag_terms(q, a):
    total = None
    for lead, _ in PHASES:
        s = inverse_root(q(lead))
        x, y = q(lead + 1), q(lead + 2)
        u, v = x * s, y * s
        term = jnp.sqrt(u * u + v * v + 1.0) * (a[lead + 1] * x + a[lead + 2] * y)
        total = term if total is None else total + term
    return -total


def stepped_back(c, drag, a, want_terms):
    q, s0, gas_u, gas_v = coupled(c)
    a = list(a)
    terms = jnp.zeros((8, LANES), jnp.float32)
    for lead, _ in PHASES:
        m, x, y = q[lead], q[lead + 1], q[lead + 2]
        s = s0 if lead == 0 else inverse_root(m)
        u, v = x * s, y * s
        energy = u * u + v * v
        root = lax.rsqrt(energy + 1.0)
        w = (energy + 1.0) * root
        dot = a[lead + 1] * x + a[lead + 2] * y
        if want_terms:
            terms = terms - w * dot
        k = drag * dot * root
        factor = 1.0 - drag * w
        ks = k * s
        a[lead + 1] = a[lead + 1] * factor - ks * u
        a[lead + 2] = a[lead + 2] * factor - ks * v
        a[lead] = a[lead] + k * energy * m * (s * s)
    du = jnp.zeros((8, LANES), jnp.float32)
    dv = jnp.zeros((8, LANES), jnp.float32)
    for lead, _ in PHASES[1:]:
        rx, ry = COUPLING * (a[lead + 1] - a[1]), COUPLING * (a[lead + 2] - a[2])
        a[lead] = a[lead] + rx * gas_u + ry * gas_v
        du, dv = du + c[lead] * rx, dv + c[lead] * ry
        a[lead + 1], a[lead + 2] = a[lead + 1] - rx, a[lead + 2] - ry
    a[1], a[2] = a[1] + du * s0, a[2] + dv * s0
    a[0] = a[0] - (gas_u * du + gas_v * dv) * c[0] * (s0 * s0)
    return a, terms


def add_speed_terms(total, state, lead, du, dv):
    m, x, y = state
    s = inverse_root(m)
    pull = None
    if du is not None:
        total[lead + 1] = total[lead + 1] + s * du
        pull = x * s * du
    if dv is not None:
        total[lead + 2] = total[lead + 2] + s * dv
        pull = y * s * dv if pull is None else pull + y * s * dv
    total[lead] = total[lead] - pull * m * (s * s)


def scatter_x(a, value, speed, flag):
    ahead = roll(a, -1) - a
    g = speed * ahead
    low = jnp.where(flag, g, 0.0)
    high = roll(g - low, 1)
    return 3.0 * (low + high) - roll(low, -1) - roll(high, 1), value * ahead


def expand_edges(own):
    pos = strip_pos()
    value = jnp.where(pos < 4, own, jnp.where((pos >= 8) & (pos < 12), roll(own, 4), 0.0))
    return value


def backward_strip(step, strip, edges_a, edge_words, left_words, sfv, su, sdc, sdu, out_c):
    bits = level_bits()
    walls = face_walls()
    ghosts = []
    for p, (lead, members) in enumerate(PHASES):
        word = strip_words(edge_words, left_words, plane(step, 0, p // 2))
        flag = (word & bits[p % 2]) != 0
        speed = su[p]
        du = jnp.zeros((8, LANES), jnp.float32)
        total = {}
        for f in range(lead, lead + members):
            total[f], term = scatter_x(expand_edges(edges_a[f]), sfv[f], speed, flag)
            sdc[f] = gather_edges(total[f])
            du = du + term
        du = walls * du
        du = du + roll(du, 1)
        sdu[p] = gather_edges(du)
        add_speed_terms(total, (strip[lead], strip[lead + 1], strip[lead + 2]), lead, du, None)
        ghosts.extend(total[f] for f in range(lead, lead + members))
    for g in range(4):
        fields = range(4 * g, min(4 * g + 4, FIELDS))
        out_c[g] = into_slots([roll(ghosts[f], 4 * (f % 4) - 4) for f in fields])
    return ghosts


def backward_fluxes(step, ext, words, low_words, a_ext, fvx, ux, fvy, vy, sdc, sdu, gl, gh, dvy, put):
    bits = level_bits()
    edges = edge_lanes()
    zero = jnp.zeros((8, LANES), jnp.float32)
    for k in (0, 1, 2, 12, 13, 14):
        for f in range(FIELDS):
            gl[f, k] = zero
            gh[f, k] = zero
        for p in range(4):
            dvy[p, k] = zero

    def face(j, carry):
        wall = row_wall(j)
        for p, (lead, members) in enumerate(PHASES):
            here = spread(words, plane(step, 1, p // 2) * ROWS + jnp.maximum(j - 1, 0))
            low_word = jnp.broadcast_to(low_words[plane(step, 1, p // 2)][None], (8, LANES))
            word = jnp.where(j == 0, low_word, here)
            flag = (word & bits[p % 2]) != 0
            speed = vy[p, j]
            dv = jnp.zeros((8, LANES), jnp.float32)
            for f in range(lead, lead + members):
                ahead = a_ext[f, j + 1] - a_ext[f, j]
                g = speed * ahead
                low = jnp.where(flag, g, 0.0)
                gl[f, j + 3] = low
                gh[f, j + 3] = g - low
                dv = dv + fvy[f, j] * ahead
            dvy[p, j + 3] = wall * dv
        return carry

    lax.fori_loop(0, ROWS + 1, face, 0)

    def along_y(f, i):
        return 3.0 * (gl[f, i + 4] + gh[f, i + 3]) - gl[f, i + 5] - gh[f, i + 2]

    def own(r, carry):
        total = [None] * FIELDS
        for p, (lead, members) in enumerate(PHASES):
            word = spread(words, plane(step, 0, p // 2) * ROWS + r)
            flag = (word & bits[p % 2]) != 0
            speed = ux[p, r]
            du = jnp.zeros((8, LANES), jnp.float32)
            for f in range(lead, lead + members):
                a = a_ext[f, r + 1]
                part, term = scatter_x(a, fvx[f, r], speed, flag)
                part = jnp.where(edges, roll(sdc[f], 124 - 16 * r), part)
                total[f] = a + part + along_y(f, r)
                du = du + term
            du = FACE * (du + roll(du, 1))
            du = jnp.where(edges, roll(sdu[p], 124 - 16 * r), du)
            dv = dvy[p, r + 4] + dvy[p, r + 3]
            state = (ext[lead, r + 2], ext[lead + 1, r + 2], ext[lead + 2, r + 2])
            add_speed_terms(total, state, lead, du, dv)
        put(r, total)
        return carry

    lax.fori_loop(0, ROWS, own, 0)

    def ghost(t, carry):
        i = jnp.where(t < 2, t - 2, t + 6)
        total = [along_y(f, i) for f in range(FIELDS)]
        for p, (lead, members) in enumerate(PHASES):
            dv = dvy[p, i + 4] + dvy[p, i + 3]
            state = (ext[lead, i + 2], ext[lead + 1, i + 2], ext[lead + 2, i + 2])
            add_speed_terms(total, state, lead, None, dv)
        put(i, total)
        return carry

    lax.fori_loop(0, 4, ghost, 0)


def level_weight():
    levels = lax.broadcasted_iota(jnp.int32, (8, LANES), 0)
    weight = jnp.full((8, LANES), DRAG_STEP, jnp.float32)
    for k in range(3):
        weight = jnp.where((levels // 2**k) % 2 == 1, weight * 0.5 ** (2**k), weight)
    return weight


def drag_table(classes, coef):
    drag = jnp.zeros(classes.shape, jnp.float32)
    for k in range(NCLASS):
        drag = jnp.where(classes == k, coef[k], drag)
    return drag


def level_sum(v):
    return jnp.sum(v, axis=0, keepdims=True)


def row_bases():
    gy, _ = position("gy")
    is_even = gy % 2 == 0
    return is_even


def fill_ghost_rows(ext, from_a, from_b):
    is_even = row_bases()
    a_row = jnp.where(is_even, ROWS + 2, 0)
    b_row = jnp.where(is_even, 0, ROWS + 2)
    for f in range(FIELDS):
        for j in range(2):
            ext[f, a_row + j] = from_a[2 * f + j]
            ext[f, b_row + j] = from_b[2 * f + j]


def put_edge_rows(source, offset, to_a, to_b):
    is_even = row_bases()
    a_row = jnp.where(is_even, ROWS - 2, 0) + offset
    b_row = jnp.where(is_even, 0, ROWS - 2) + offset
    for f in range(FIELDS):
        for j in range(2):
            to_a[2 * f + j] = source[f, a_row + j]
            to_b[2 * f + j] = source[f, b_row + j]


def pack_kernel(start, words, terrain, rows, edges, edge_words, to_a, to_b, to_c):
    zero_edges(edges)
    edge_words[...] = jnp.zeros((8, LANES), jnp.int32)
    slots = lax.broadcasted_iota(jnp.int32, (8, LANES), 0)

    def one_row(r, carry):
        values = [start[f, pl.ds(r, 8, stride=8), :] for f in range(FIELDS)]
        for f in range(FIELDS):
            rows[f, r] = values[f]
        add_edges(edges, values, r)
        mine = strip_row() == r
        row_words = jnp.where(slots == TERRAIN_SLOT, spread(terrain, r), words[pl.ds(r, 8, stride=8), :])
        edge_words[...] = jnp.where(mine, roll(row_words, 16 * r + 4), edge_words[...])
        return carry

    lax.fori_loop(0, ROWS, one_row, 0)
    put_edge_rows(rows, 0, to_a, to_b)
    top = words[pl.ds(ROWS - 1, 8, stride=8), :]
    is_even = row_bases()
    a_row = jnp.where(is_even, ROWS - 2, 0)
    for target, row in ((to_a, a_row), (to_b, ROWS - 2 - a_row)):
        mixed = jnp.where(slots == 0, spread(terrain, row), jnp.where(slots == 1, spread(terrain, row + 1), top))
        target[2 * FIELDS] = mixed.astype(jnp.float32)
    edge_payload(edges, to_c)
    to_c[4] = edge_words[...].astype(jnp.float32)


def neighbour_words(from_a, from_b, pick):
    low = jnp.where(row_bases(), from_b[2 * FIELDS], from_a[2 * FIELDS]).astype(jnp.int32)
    left, _ = pick(4)
    return low, left.astype(jnp.int32)


def first_kernel(has_odd):
    def kernel(*refs):
        rows, edges, edge_words, words, terrain, coef, from_a, from_b, from_c = refs[:9]
        from_d = refs[9] if has_odd else None
        outs = refs[9 + has_odd :]
        (ext, strip, carried_ref, fvx, ux, fvy, vy, sfv, su, drag_ref, class_ref, low_ref, left_ref) = outs[:13]
        middle, before, before_edges, to_a, to_b, to_c = outs[13:19]
        (sdx,) = outs[19:]
        pick = side_payloads(from_c, from_d)

        def copy_row(r, carry):
            for f in range(FIELDS):
                ext[f, r + 2] = rows[f, r]
            return carry

        lax.fori_loop(0, ROWS, copy_row, 0)
        fill_ghost_rows(ext, from_a, from_b)
        build_strip(edges, pick, strip)
        low_words, left_words = neighbour_words(from_a, from_b, pick)
        low_ref[...] = low_words
        left_ref[...] = left_words
        is_even = row_bases()
        a_row = jnp.where(is_even, ROWS + 2, 0)
        class_ref[pl.ds(2, ROWS), :] = terrain[...]
        for source, row in ((from_a, a_row), (from_b, ROWS + 2 - a_row)):
            for j in range(2):
                class_ref[pl.ds(row + j, 1), :] = source[2 * FIELDS, pl.ds(j, 1), :].astype(jnp.int32)
        class_ref[pl.ds(12, 4), :] = strip_classes(edge_words, pick)[:4]
        drag_ref[...] = drag_table(class_ref[...], coef)
        forward_strip(0, strip, edge_words, left_words, sfv, su, sdx)
        forward_rows(0, ext, words, low_words, fvy, vy)
        zero_edges(before_edges)
        weight = level_weight()

        def one_row(r, carry):
            c = carried_row(0, r, ext, words, sdx, fvx, ux, fvy, vy)
            for f in range(FIELDS):
                carried_ref[f, r] = c[f]
            q = coupled(c)[0]
            for f in range(FIELDS):
                before[f, r] = q[f]
            add_edges(before_edges, q, r)
            q = dragged(q, weight * spread(drag_ref, r + 2))
            for f in range(FIELDS):
                middle[f, r] = q[f]
            return carry

        lax.fori_loop(0, ROWS, one_row, 0)
        put_edge_rows(before, 0, to_a, to_b)
        edge_payload(before_edges, to_c)

    return kernel


def ghost_rows_out(part, to_a, to_b):
    is_even = row_bases()
    a_row = jnp.where(is_even, ROWS + 2, 0)
    b_row = jnp.where(is_even, 0, ROWS + 2)
    for f in range(FIELDS):
        for j in range(2):
            to_a[2 * f + j] = part[f, a_row + j]
            to_b[2 * f + j] = part[f, b_row + j]


def second_kernel(has_odd):
    def kernel(*refs):
        middle, before, before_edges, edge_words, words, drag_ref, class_ref, low_ref, left_ref, adjoint = refs[:10]
        from_a, from_b, from_c = refs[10:13]
        from_d = refs[13] if has_odd else None
        outs = refs[13 + has_odd :]
        part, to_a, to_b, to_c = outs[:4]
        (ext, strip, fvx, ux, fvy, vy, sfv, su, sdx, a_ext, edges_a, sdc, sdu, gl, gh, dvy) = outs[4:20]
        before_ext, before_strip, cells = outs[20:]
        pick = side_payloads(from_c, from_d)
        low_words, left_words = low_ref[...], left_ref[...]
        weight = level_weight()

        def copy_row(r, carry):
            for f in range(FIELDS):
                ext[f, r + 2] = middle[f, r]
                before_ext[f, r + 2] = before[f, r]
            return carry

        lax.fori_loop(0, ROWS, copy_row, 0)
        fill_ghost_rows(before_ext, from_a, from_b)

        def ghost_row(t, carry):
            row = jnp.where(t < 2, t, t + 8)
            q = dragged([before_ext[f, row] for f in range(FIELDS)], weight * spread(drag_ref, row))
            for f in range(FIELDS):
                ext[f, row] = q[f]
            return carry

        lax.fori_loop(0, 4, ghost_row, 0)
        build_strip(before_edges, pick, before_strip)
        q = dragged([before_strip[f] for f in range(FIELDS)], weight * spread(drag_ref, 12))
        for f in range(FIELDS):
            strip[f] = q[f]
        forward_strip(1, strip, edge_words, left_words, sfv, su, sdx)
        forward_rows(1, ext, words, low_words, fvy, vy)
        zero_edges(edges_a)
        for f in range(FIELDS):
            a_ext[f, 0] = jnp.zeros((8, LANES), jnp.float32)
            a_ext[f, ROWS + 1] = jnp.zeros((8, LANES), jnp.float32)
        cells[...] = jnp.zeros((16, LANES), jnp.float32)

        def one_row(r, carry):
            c = carried_row(1, r, ext, words, sdx, fvx, ux, fvy, vy)
            a = [adjoint[f, pl.ds(r, 8, stride=8), :] for f in range(FIELDS)]
            a, terms = stepped_back(c, weight * spread(drag_ref, r + 2), a, True)
            cells[pl.ds(r + 2, 1), :] = level_sum(weight * terms)
            for f in range(FIELDS):
                a_ext[f, r + 1] = a[f]
            add_edges(edges_a, a, r)
            return carry

        lax.fori_loop(0, ROWS, one_row, 0)
        ghosts = backward_strip(1, strip, edges_a, edge_words, left_words, sfv, su, sdc, sdu, to_c)
        pos = strip_pos()
        terms = jnp.where((pos >= 4) & (pos < 8), drag_terms(lambda f: before_strip[f], ghosts), 0.0)
        cells[pl.ds(12, 1), :] = level_sum(weight * terms)

        def put(row, values):
            for f in range(FIELDS):
                part[f, row + 2] = values[f]
            terms = drag_terms(lambda f: before_ext[f, row + 2], values)
            at = pl.ds(row + 2, 1)
            cells[at, :] = cells[at, :] + level_sum(weight * terms)

        backward_fluxes(1, ext, words, low_words, a_ext, fvx, ux, fvy, vy, sdc, sdu, gl, gh, dvy, put)
        ghost_rows_out(part, to_a, to_b)
        to_c[4] = binned(class_ref[...], cells[...])

    return kernel


def binned(classes, cells):
    lanes = lane_ids()
    slots = lax.broadcasted_iota(jnp.int32, (8, LANES), 0)
    total = jnp.zeros((8, LANES), jnp.float32)
    for first in range(0, NCLASS, 8):
        block = jnp.zeros((8, LANES), jnp.float32)
        for k in range(first, min(first + 8, NCLASS)):
            block = jnp.where(slots == k - first, level_sum(jnp.where(classes == k, cells, 0.0)), block)
        block = jnp.sum(block, axis=1, keepdims=True)
        total = jnp.where(lanes == first + slots, block, total)
    return jnp.broadcast_to(level_sum(total), (8, LANES))


def collect(part, from_a, from_b, pick, incoming):
    is_even = row_bases()
    a_row = jnp.where(is_even, ROWS, 2)
    b_row = jnp.where(is_even, 2, ROWS)
    for f in range(FIELDS):
        for j in range(2):
            part[f, a_row + j] = part[f, a_row + j] + from_a[2 * f + j]
            part[f, b_row + j] = part[f, b_row + j] + from_b[2 * f + j]
    pos = strip_pos()
    for g in range(4):
        left, right = pick(g)
        for f in range(4 * g, min(4 * g + 4, FIELDS)):
            q = f % 4
            at_left = (pos == 4) | (pos == 5)
            at_right = (pos == 2) | (pos == 3)
            value = jnp.where(at_left, roll(left, 4 - 4 * q), jnp.where(at_right, roll(right, -4 * q), 0.0))
            incoming[f] = value


def third_kernel(has_odd):
    def kernel(*refs):
        (part_in, grads, ext, strip, carried_ref, fvx, ux, fvy, vy, sfv, su) = refs[:11]
        drag_ref, low_ref, left_ref, edge_words, words = refs[11:16]
        from_a, from_b, from_c = refs[16:19]
        from_d = refs[19] if has_odd else None
        outs = refs[19 + has_odd :]
        part, to_a, to_b, to_c = outs[:4]
        (incoming, a_ext, edges_a, sdc, sdu, gl, gh, dvy) = outs[4:]
        pick = side_payloads(from_c, from_d)
        low_words, left_words = low_ref[...], left_ref[...]

        def copy_row(r, carry):
            for f in range(FIELDS):
                part[f, r + 2] = part_in[f, r + 2]
            return carry

        lax.fori_loop(0, ROWS, copy_row, 0)
        collect(part, from_a, from_b, pick, incoming)
        zero_edges(edges_a)
        for f in range(FIELDS):
            a_ext[f, 0] = jnp.zeros((8, LANES), jnp.float32)
            a_ext[f, ROWS + 1] = jnp.zeros((8, LANES), jnp.float32)
        edges = edge_lanes()
        weight = level_weight()

        def one_row(r, carry):
            c = [carried_ref[f, r] for f in range(FIELDS)]
            a = [
                part[f, r + 2] + jnp.where(edges, roll(incoming[f], 124 - 16 * r), 0.0)
                for f in range(FIELDS)
            ]
            a, _ = stepped_back(c, weight * spread(drag_ref, r + 2), a, False)
            for f in range(FIELDS):
                a_ext[f, r + 1] = a[f]
            add_edges(edges_a, a, r)
            return carry

        lax.fori_loop(0, ROWS, one_row, 0)
        to_a[2 * FIELDS] = grads[...]
        backward_strip(0, strip, edges_a, edge_words, left_words, sfv, su, sdc, sdu, to_c)

        def put(row, values):
            for f in range(FIELDS):
                part[f, row + 2] = values[f]

        backward_fluxes(0, ext, words, low_words, a_ext, fvx, ux, fvy, vy, sdc, sdu, gl, gh, dvy, put)
        ghost_rows_out(part, to_a, to_b)

    return kernel


def last_kernel(has_odd):
    def kernel(*refs):
        part_in, from_a, from_b, from_c = refs[:4]
        from_d = refs[4] if has_odd else None
        out, part, incoming = refs[4 + has_odd :]
        pick = side_payloads(from_c, from_d)

        def copy_row(r, carry):
            for f in range(FIELDS):
                part[f, r + 2] = part_in[f, r + 2]
            return carry

        lax.fori_loop(0, ROWS, copy_row, 0)
        collect(part, from_a, from_b, pick, incoming)
        edges = edge_lanes()

        def one_row(r, carry):
            for f in range(FIELDS):
                value = part[f, r + 2] + jnp.where(edges, roll(incoming[f], 124 - 16 * r), 0.0)
                out[f, pl.ds(r, 8, stride=8), :] = value
            return carry

        lax.fori_loop(0, ROWS, one_row, 0)

    return kernel


def shaped(*shape, dtype=jnp.float32):
    return jax.ShapeDtypeStruct(shape, dtype)


def tiles(*shape, dtype=jnp.float32):
    return shaped(*shape, 8, LANES, dtype=dtype)


def scratch(*shape, dtype=jnp.float32):
    return pltpu.VMEM((*shape, 8, LANES), dtype)


def call(kernel, outs, scratches, args, smem=()):
    in_specs = [
        pl.BlockSpec(memory_space=pltpu.SMEM if k in smem else pltpu.VMEM) for k in range(len(args))
    ]
    return pl.pallas_call(
        kernel,
        out_shape=outs,
        in_specs=in_specs,
        out_specs=[pl.BlockSpec(memory_space=pltpu.VMEM)] * len(outs),
        scratch_shapes=scratches,
        compiler_params=pltpu.CompilerParams(vmem_limit_bytes=32 << 20),
    )(*args)


def swap(x, axis, first):
    peers = lax.axis_size(axis)
    pairs = [(i, i + 1) for i in range(first, peers - 1, 2)]
    if not pairs:
        return None
    return lax.ppermute(x, axis, pairs + [(j, i) for i, j in pairs])


def exchange(to_a, to_b, to_c):
    from_a = swap(to_a, "gy", 0)
    from_b = swap(to_b, "gy", 1)
    from_c = swap(to_c, "gx", 0)
    from_d = swap(to_c, "gx", 1)
    if from_b is None:
        from_b = jnp.zeros_like(to_b)
    return (from_a, from_b, from_c) + (() if from_d is None else (from_d,))


def add_partner(x, axis, distance):
    return x + lax.ppermute(x, axis, [(i, i ^ distance) for i in range(lax.axis_size(axis))])


def body(start_state, final_adjoint, face_words, terrain, drag_coef):
    nx, ny = lax.axis_size("gx"), lax.axis_size("gy")
    has_odd = nx > 2
    start = start_state.reshape(FIELDS, LEV * ROWS, LANES)
    adjoint = final_adjoint.reshape(FIELDS, LEV * ROWS, LANES)
    words = face_words.reshape(8 * ROWS, LANES)
    ints = jnp.int32

    rows, edges, edge_words, to_a, to_b, to_c = call(
        pack_kernel,
        [tiles(14, 8), tiles(14), tiles(dtype=ints), tiles(29), tiles(29), tiles(5)],
        [],
        [start, words, terrain],
    )
    got = exchange(to_a, to_b, to_c)
    faces = [tiles(14, 8), tiles(4, 8), tiles(14, 9), tiles(4, 9), tiles(14), tiles(4)]
    res = call(
        first_kernel(has_odd),
        [tiles(14, 12), tiles(14), tiles(14, 8), *faces, shaped(16, LANES), shaped(16, LANES, dtype=ints)]
        + [tiles(dtype=ints), tiles(dtype=ints), tiles(14, 8), tiles(14, 8), tiles(14), tiles(28), tiles(28), tiles(4)],
        [scratch(14)],
        [rows, edges, edge_words, words, terrain, drag_coef, *got],
        smem=(5,),
    )
    ext, strip, carried_ref = res[:3]
    saved = res[3:9]
    drag_ref, class_ref, low_ref, left_ref = res[9:13]
    middle, before, before_edges = res[13:16]
    got = exchange(*res[16:19])
    back = [scratch(14, 10), scratch(14), scratch(14), scratch(4), scratch(14, 15), scratch(14, 15), scratch(4, 15)]
    part, to_a, to_b, to_c = call(
        second_kernel(has_odd),
        [tiles(14, 12), tiles(28), tiles(28), tiles(5)],
        [scratch(14, 12), scratch(14), scratch(14, 8), scratch(4, 8), scratch(14, 9), scratch(4, 9)]
        + [scratch(14), scratch(4), scratch(14), *back]
        + [scratch(14, 12), scratch(14), pltpu.VMEM((16, LANES), jnp.float32)],
        [middle, before, before_edges, edge_words, words, drag_ref, class_ref, low_ref, left_ref, adjoint, *got],
    )
    got = exchange(to_a, to_b, to_c)
    grads = to_c[4] + got[2][4]
    distance = 2
    while distance < nx:
        grads = add_partner(grads, "gx", distance)
        distance *= 2
    if ny > 2:
        grads = add_partner(grads, "gy", 2)
    part, to_a, to_b, to_c = call(
        third_kernel(has_odd),
        [tiles(14, 12), tiles(29), tiles(28), tiles(4)],
        [scratch(14), *back],
        [part, grads, ext, strip, carried_ref, *saved]
        + [drag_ref, low_ref, left_ref, edge_words, words, *got],
    )
    got = exchange(to_a, to_b, to_c)
    grads = grads + got[0][2 * FIELDS]
    distance = 4
    while distance < ny:
        grads = add_partner(grads, "gy", distance)
        distance *= 2
    (out,) = call(
        last_kernel(has_odd),
        [shaped(FIELDS, LEV * ROWS, LANES)],
        [scratch(14, 12), scratch(14)],
        [part, *got],
    )
    grad_scale = math.sqrt(NCLASS / (terrain.size * nx * ny * LEV))
    return (out.reshape(start_state.shape), grads[0, :NCLASS] * grad_scale)


def solution(mesh):
    placed = (
        P(None, None, "gy", "gx"),
        P(None, None, "gy", "gx"),
        P(None, None, None, "gy", "gx"),
        P("gy", "gx"),
        P(),
    )
    return jax.shard_map(
        body,
        mesh=mesh,
        in_specs=placed,
        out_specs=(P(None, None, "gy", "gx"), P()),
        check_vma=False,
    )
```

```python
import math

import jax
import jax.numpy as jnp
from jax import lax
from jax.experimental import pallas as pl
from jax.experimental.pallas import tpu as pltpu
from jax.sharding import PartitionSpec as P

LEV = 8
NCLASS = 24
FIELDS = 14
ROWS = 8
LANES = 128
PHASES = ((0, 5), (5, 3), (8, 3), (11, 3))
FACE = 0.3 * 0.5 * 0.5
COUPLING = 0.5
DRAG_STEP = 0.5
TERRAIN_SLOT = 2


def roll(v, shift):
    return pltpu.roll(v, shift % LANES if isinstance(shift, int) else shift, 1)


def lane_ids():
    return lax.broadcasted_iota(jnp.int32, (8, LANES), 1)


def strip_pos():
    return lane_ids() % 16


def strip_row():
    return lane_ids() // 16


def level_bits():
    levels = lax.broadcasted_iota(jnp.int32, (8, LANES), 0)
    return [jnp.left_shift(jnp.ones_like(levels), levels + LEV * k) for k in range(2)]


def edge_lanes():
    lanes = lane_ids()
    return (lanes < 2) | (lanes >= LANES - 2)


def spread(ref, index):
    return jnp.broadcast_to(ref[pl.ds(index, 1), :], (8, LANES))


def plane(step, direction, pair):
    return step * 4 + direction * 2 + pair


def position(axis):
    return lax.axis_index(axis), lax.axis_size(axis)


def into_slots(values):
    pos = strip_pos() // 4
    total = jnp.zeros((8, LANES), jnp.float32)
    for slot, value in enumerate(values):
        total = jnp.where(pos == slot, value, total)
    return total


def add_edges(edges_ref, values, row):
    mine = strip_row() == row
    for f, value in enumerate(values):
        edges_ref[f] = jnp.where(mine, roll(value, 16 * row + 4), edges_ref[f])


def zero_edges(edges_ref, count=FIELDS):
    for f in range(count):
        edges_ref[f] = jnp.zeros((8, LANES), edges_ref.dtype)


def edge_payload(edges_ref, out_ref):
    for g in range(4):
        fields = range(4 * g, min(4 * g + 4, FIELDS))
        out_ref[g] = into_slots([roll(edges_ref[f], 4 * (f % 4) - 2) for f in fields])


def side_payloads(even_ref, odd_ref):
    index, _ = position("gx")
    is_even = index % 2 == 0

    def pick(k):
        a = even_ref[k]
        b = jnp.zeros_like(a) if odd_ref is None else odd_ref[k]
        return jnp.where(is_even, b, a), jnp.where(is_even, a, b)

    return pick


def build_strip(edges_ref, pick, strip_ref):
    pos = strip_pos()
    for g in range(4):
        left, right = pick(g)
        for f in range(4 * g, min(4 * g + 4, FIELDS)):
            q = f % 4
            own = edges_ref[f]
            value = jnp.where(pos < 4, own, roll(right, 2 - 4 * q))
            value = jnp.where(pos < 6, value, roll(left, 6 - 4 * q))
            value = jnp.where(pos < 8, value, roll(own, 4))
            strip_ref[f] = jnp.where(pos < 12, value, 0.0)


def strip_words(edge_words_ref, left_words, which):
    pos = strip_pos()
    own = spread(edge_words_ref, which)
    left = jnp.broadcast_to(left_words[which : which + 1], (8, LANES))
    value = jnp.where(pos < 4, own, roll(own, 4))
    return jnp.where(pos == 7, roll(left, 4), value)


def strip_classes(edge_words_ref, pick):
    pos = strip_pos()
    own = spread(edge_words_ref, TERRAIN_SLOT)
    left, right = [jnp.broadcast_to(v[TERRAIN_SLOT : TERRAIN_SLOT + 1], (8, LANES)).astype(jnp.int32) for v in pick(4)]
    value = jnp.where(pos < 4, own, jnp.where(pos < 6, right, jnp.where(pos < 8, roll(left, 4), roll(own, 4))))
    return value


def face_walls():
    gx, nx = position("gx")
    pos = strip_pos()
    shut = ((pos == 7) & (gx == 0)) | ((pos == 3) & (gx == nx - 1))
    return jnp.where(shut, 0.0, FACE)


def row_wall(j):
    gy, ny = position("gy")
    shut = ((j == 0) & (gy == 0)) | ((j == ROWS) & (gy == ny - 1))
    return jnp.where(shut, 0.0, FACE)


def inverse_root(mass):
    return lax.rsqrt(mass * mass + 1.0)


def gather_edges(v):
    pos = strip_pos()
    return jnp.where((pos == 4) | (pos == 5), roll(v, -4), v)


def face_values(behind, here, ahead, beyond, flag):
    return jnp.where(flag, 3.0 * here - behind, 3.0 * ahead - beyond)


def forward_strip(step, strip, edge_words, left_words, sfv, su, sdx):
    bits = level_bits()
    walls = face_walls()
    for p, (lead, members) in enumerate(PHASES):
        word = strip_words(edge_words, left_words, plane(step, 0, p // 2))
        flag = (word & bits[p % 2]) != 0
        u = strip[lead + 1] * inverse_root(strip[lead])
        speed = walls * (u + roll(u, -1))
        su[p] = speed
        for f in range(lead, lead + members):
            c = strip[f]
            ahead = roll(c, -1)
            value = face_values(roll(c, 1), c, ahead, roll(c, -2), flag)
            sfv[f] = value
            flux = speed * value
            sdx[f] = gather_edges(flux - roll(flux, 1))


def forward_face(j, step, ext, words, low_words, fvy, vy):
    bits = level_bits()
    wall = FACE if low_words is None else row_wall(j)
    for p, (lead, members) in enumerate(PHASES):
        which = plane(step, 1, p // 2)
        word = face_word(j, words, low_words, which)
        flag = (word & bits[p % 2]) != 0
        v_low = ext[lead + 2, j + 1] * inverse_root(ext[lead, j + 1])
        v_high = ext[lead + 2, j + 2] * inverse_root(ext[lead, j + 2])
        vy[p, j] = wall * (v_low + v_high)
        for f in range(lead, lead + members):
            fvy[f, j] = face_values(ext[f, j], ext[f, j + 1], ext[f, j + 2], ext[f, j + 3], flag)


def face_word(j, words, low_words, which):
    if low_words is None:
        return spread(words, which * ROWS + j - 1)
    here = spread(words, which * ROWS + jnp.maximum(j - 1, 0))
    low = jnp.broadcast_to(low_words[which : which + 1], (8, LANES))
    return jnp.where(j == 0, low, here)


def carried_row(r, edges, ext, sdx, along, fvy, vy):
    carried = []
    for p, (lead, members) in enumerate(PHASES):
        below, above = vy[p, r], vy[p, r + 1]
        for f in range(lead, lead + members):
            seam = ext[f, r + 2] - roll(sdx[f], 124 - 16 * r)
            along_y = above * fvy[f, r + 1] - below * fvy[f, r]
            carried.append(jnp.where(edges, seam, along[f, r]) - along_y)
    return carried


def early_kernel(step):
    def kernel(ext, words, fvx, ux, along, fvy, vy):
        bits = level_bits()

        def one_row(r, carry):
            for p, (lead, members) in enumerate(PHASES):
                word = spread(words, plane(step, 0, p // 2) * ROWS + r)
                flag = (word & bits[p % 2]) != 0
                u = ext[lead + 1, r + 2] * inverse_root(ext[lead, r + 2])
                speed = FACE * (u + roll(u, -1))
                ux[p, r] = speed
                for f in range(lead, lead + members):
                    c = ext[f, r + 2]
                    value = face_values(roll(c, 1), c, roll(c, -1), roll(c, -2), flag)
                    fvx[f, r] = value
                    flux = speed * value
                    along[f, r] = c - (flux - roll(flux, 1))
            return carry

        lax.fori_loop(0, ROWS, one_row, 0, unroll=2)
        for j in range(2, ROWS - 1):
            forward_face(j, step, ext, words, None, fvy, vy)

    return kernel


def outer_faces(step, ext, words, low_words, fvy, vy):
    for j in (0, 1, ROWS - 1, ROWS):
        forward_face(j, step, ext, words, low_words, fvy, vy)


def coupled(c):
    s = inverse_root(c[0])
    u, v = c[1] * s, c[2] * s
    gas_x, gas_y = c[1], c[2]
    out = [None] * FIELDS
    for lead, _ in PHASES[1:]:
        pull_x = COUPLING * (c[lead] * u - c[lead + 1])
        pull_y = COUPLING * (c[lead] * v - c[lead + 2])
        gas_x, gas_y = gas_x - pull_x, gas_y - pull_y
        out[lead] = c[lead]
        out[lead + 1], out[lead + 2] = c[lead + 1] + pull_x, c[lead + 2] + pull_y
    out[0], out[1], out[2], out[3], out[4] = c[0], gas_x, gas_y, c[3], c[4]
    return out, s, u, v


def dragged(q, drag):
    q = list(q)
    for lead, _ in PHASES:
        s = inverse_root(q[lead])
        u, v = q[lead + 1] * s, q[lead + 2] * s
        factor = 1.0 - drag * jnp.sqrt(u * u + v * v + 1.0)
        q[lead + 1], q[lead + 2] = q[lead + 1] * factor, q[lead + 2] * factor
    return q


def drag_terms(q, a):
    total = None
    for lead, _ in PHASES:
        s = inverse_root(q(lead))
        x, y = q(lead + 1), q(lead + 2)
        u, v = x * s, y * s
        term = jnp.sqrt(u * u + v * v + 1.0) * (a[lead + 1] * x + a[lead + 2] * y)
        total = term if total is None else total + term
    return -total


def stepped_back(c, drag, a, want_terms):
    q, s0, gas_u, gas_v = coupled(c)
    a = list(a)
    terms = jnp.zeros((8, LANES), jnp.float32)
    for lead, _ in PHASES:
        m, x, y = q[lead], q[lead + 1], q[lead + 2]
        s = s0 if lead == 0 else inverse_root(m)
        u, v = x * s, y * s
        energy = u * u + v * v
        root = lax.rsqrt(energy + 1.0)
        w = (energy + 1.0) * root
        dot = a[lead + 1] * x + a[lead + 2] * y
        if want_terms:
            terms = terms - w * dot
        k = drag * dot * root
        factor = 1.0 - drag * w
        ks = k * s
        a[lead + 1] = a[lead + 1] * factor - ks * u
        a[lead + 2] = a[lead + 2] * factor - ks * v
        a[lead] = a[lead] + k * energy * m * (s * s)
    du = jnp.zeros((8, LANES), jnp.float32)
    dv = jnp.zeros((8, LANES), jnp.float32)
    for lead, _ in PHASES[1:]:
        rx, ry = COUPLING * (a[lead + 1] - a[1]), COUPLING * (a[lead + 2] - a[2])
        a[lead] = a[lead] + rx * gas_u + ry * gas_v
        du, dv = du + c[lead] * rx, dv + c[lead] * ry
        a[lead + 1], a[lead + 2] = a[lead + 1] - rx, a[lead + 2] - ry
    a[1], a[2] = a[1] + du * s0, a[2] + dv * s0
    a[0] = a[0] - (gas_u * du + gas_v * dv) * c[0] * (s0 * s0)
    return a, terms


def add_speed_terms(total, state, lead, du, dv):
    m, x, y = state
    s = inverse_root(m)
    pull = None
    if du is not None:
        total[lead + 1] = total[lead + 1] + s * du
        pull = x * s * du
    if dv is not None:
        total[lead + 2] = total[lead + 2] + s * dv
        pull = y * s * dv if pull is None else pull + y * s * dv
    total[lead] = total[lead] - pull * m * (s * s)


def scatter_x(a, value, speed, flag):
    ahead = roll(a, -1) - a
    g = speed * ahead
    low = jnp.where(flag, g, 0.0)
    high = roll(g - low, 1)
    return 3.0 * (low + high) - roll(low, -1) - roll(high, 1), value * ahead


def expand_edges(own):
    pos = strip_pos()
    value = jnp.where(pos < 4, own, jnp.where((pos >= 8) & (pos < 12), roll(own, 4), 0.0))
    return value


def backward_strip(step, strip, edges_a, edge_words, left_words, sfv, su, sdc, sdu, out_c):
    bits = level_bits()
    walls = face_walls()
    ghosts = []
    for p, (lead, members) in enumerate(PHASES):
        word = strip_words(edge_words, left_words, plane(step, 0, p // 2))
        flag = (word & bits[p % 2]) != 0
        speed = su[p]
        du = jnp.zeros((8, LANES), jnp.float32)
        total = {}
        for f in range(lead, lead + members):
            total[f], term = scatter_x(expand_edges(edges_a[f]), sfv[f], speed, flag)
            sdc[f] = gather_edges(total[f])
            du = du + term
        du = walls * du
        du = du + roll(du, 1)
        sdu[p] = gather_edges(du)
        add_speed_terms(total, (strip[lead], strip[lead + 1], strip[lead + 2]), lead, du, None)
        ghosts.extend(total[f] for f in range(lead, lead + members))
    for g in range(4):
        fields = range(4 * g, min(4 * g + 4, FIELDS))
        out_c[g] = into_slots([roll(ghosts[f], 4 * (f % 4) - 4) for f in fields])
    return ghosts


def backward_faces(step, ext, words, low_words, a_ext, fvy, vy, gl, gh, dvy, put):
    bits = level_bits()
    zero = jnp.zeros((8, LANES), jnp.float32)
    for k in (0, 1, 2, 12, 13, 14):
        for f in range(FIELDS):
            gl[f, k] = zero
            gh[f, k] = zero
        for p in range(4):
            dvy[p, k] = zero

    def face(j, carry):
        wall = row_wall(j)
        for p, (lead, members) in enumerate(PHASES):
            word = face_word(j, words, low_words, plane(step, 1, p // 2))
            flag = (word & bits[p % 2]) != 0
            speed = vy[p, j]
            dv = jnp.zeros((8, LANES), jnp.float32)
            for f in range(lead, lead + members):
                ahead = a_ext[f, j + 1] - a_ext[f, j]
                g = speed * ahead
                low = jnp.where(flag, g, 0.0)
                gl[f, j + 3] = low
                gh[f, j + 3] = g - low
                dv = dv + fvy[f, j] * ahead
            dvy[p, j + 3] = wall * dv
        return carry

    lax.fori_loop(0, ROWS + 1, face, 0, unroll=9)
    for i in (-2, -1, ROWS, ROWS + 1):
        total = [transposed_y(gl, gh, f, i) for f in range(FIELDS)]
        for p, (lead, members) in enumerate(PHASES):
            dv = dvy[p, i + 4] + dvy[p, i + 3]
            state = (ext[lead, i + 2], ext[lead + 1, i + 2], ext[lead + 2, i + 2])
            add_speed_terms(total, state, lead, None, dv)
        put(i, total)


def transposed_y(gl, gh, f, i):
    return 3.0 * (gl[f, i + 4] + gh[f, i + 3]) - gl[f, i + 5] - gh[f, i + 2]


def backward_own(step, ext, words, a_ext, fvx, ux, sdc, sdu, gl, gh, dvy, put):
    bits = level_bits()
    edges = edge_lanes()

    def own(r, carry):
        total = [None] * FIELDS
        for p, (lead, members) in enumerate(PHASES):
            word = spread(words, plane(step, 0, p // 2) * ROWS + r)
            flag = (word & bits[p % 2]) != 0
            speed = ux[p, r]
            du = jnp.zeros((8, LANES), jnp.float32)
            for f in range(lead, lead + members):
                a = a_ext[f, r + 1]
                part, term = scatter_x(a, fvx[f, r], speed, flag)
                part = jnp.where(edges, roll(sdc[f], 124 - 16 * r), part)
                total[f] = a + part + transposed_y(gl, gh, f, r)
                du = du + term
            du = FACE * (du + roll(du, 1))
            du = jnp.where(edges, roll(sdu[p], 124 - 16 * r), du)
            dv = dvy[p, r + 4] + dvy[p, r + 3]
            state = (ext[lead, r + 2], ext[lead + 1, r + 2], ext[lead + 2, r + 2])
            add_speed_terms(total, state, lead, du, dv)
        put(r, total)
        return carry

    lax.fori_loop(0, ROWS, own, 0, unroll=2)


def level_weight():
    levels = lax.broadcasted_iota(jnp.int32, (8, LANES), 0)
    weight = jnp.full((8, LANES), DRAG_STEP, jnp.float32)
    for k in range(3):
        weight = jnp.where((levels // 2**k) % 2 == 1, weight * 0.5 ** (2**k), weight)
    return weight


def drag_table(classes, coef):
    drag = jnp.zeros(classes.shape, jnp.float32)
    for k in range(NCLASS):
        drag = jnp.where(classes == k, coef[k], drag)
    return drag


def level_sum(v):
    return jnp.sum(v, axis=0, keepdims=True)


def row_bases():
    gy, _ = position("gy")
    is_even = gy % 2 == 0
    return is_even


def fill_ghost_rows(ext, from_a, from_b):
    is_even = row_bases()
    a_row = jnp.where(is_even, ROWS + 2, 0)
    b_row = jnp.where(is_even, 0, ROWS + 2)
    for f in range(FIELDS):
        for j in range(2):
            ext[f, a_row + j] = from_a[2 * f + j]
            ext[f, b_row + j] = from_b[2 * f + j]


def put_edge_rows(source, offset, to_a, to_b):
    is_even = row_bases()
    a_row = jnp.where(is_even, ROWS - 2, 0) + offset
    b_row = jnp.where(is_even, 0, ROWS - 2) + offset
    for f in range(FIELDS):
        for j in range(2):
            to_a[2 * f + j] = source[f, a_row + j]
            to_b[2 * f + j] = source[f, b_row + j]


def pack_kernel(start_in, words_in, terrain_in, ext, edges, edge_words, to_a, to_b, to_c, start, words, terrain, sems):
    copies = [
        pltpu.make_async_copy(source, target, sems.at[k])
        for k, (source, target) in enumerate(((start_in, start), (words_in, words), (terrain_in, terrain)))
    ]
    for copy in copies:
        copy.start()
    zero_edges(edges)
    edge_words[...] = jnp.zeros((8, LANES), jnp.int32)
    slots = lax.broadcasted_iota(jnp.int32, (8, LANES), 0)
    for copy in copies:
        copy.wait()

    def one_row(r, carry):
        values = [start[f, pl.ds(r, 8, stride=8), :] for f in range(FIELDS)]
        for f in range(FIELDS):
            ext[f, r + 2] = values[f]
        add_edges(edges, values, r)
        mine = strip_row() == r
        row_words = jnp.where(slots == TERRAIN_SLOT, spread(terrain, r), words[pl.ds(r, 8, stride=8), :])
        edge_words[...] = jnp.where(mine, roll(row_words, (16 * r + 4) % LANES), edge_words[...])
        return carry

    lax.fori_loop(0, ROWS, one_row, 0, unroll=8)
    put_edge_rows(ext, 2, to_a, to_b)
    top = words[pl.ds(ROWS - 1, 8, stride=8), :]
    is_even = row_bases()
    a_row = jnp.where(is_even, ROWS - 2, 0)
    for target, row in ((to_a, a_row), (to_b, ROWS - 2 - a_row)):
        mixed = jnp.where(slots == 0, spread(terrain, row), jnp.where(slots == 1, spread(terrain, row + 1), top))
        target[2 * FIELDS] = mixed.astype(jnp.float32)
    edge_payload(edges, to_c)
    to_c[4] = edge_words[...].astype(jnp.float32)


def neighbour_words(from_a, from_b, pick):
    low = jnp.where(row_bases(), from_b[2 * FIELDS], from_a[2 * FIELDS]).astype(jnp.int32)
    left, _ = pick(4)
    return low, left.astype(jnp.int32)


def first_kernel(has_odd):
    def kernel(*refs):
        (_, _, _, edges, edge_words, along, words, terrain, coef, from_a, from_b, from_c) = refs[:12]
        from_d = refs[12] if has_odd else None
        outs = refs[12 + has_odd :]
        (ext, fvy, vy, strip, carried_ref, sfv, su, drag_ref, class_ref, low_ref, left_ref) = outs[:11]
        middle, before, before_edges, to_a, to_b, to_c = outs[11:17]
        (sdx,) = outs[17:]
        pick = side_payloads(from_c, from_d)
        fill_ghost_rows(ext, from_a, from_b)
        build_strip(edges, pick, strip)
        low_words, left_words = neighbour_words(from_a, from_b, pick)
        low_ref[...] = low_words
        left_ref[...] = left_words
        is_even = row_bases()
        a_row = jnp.where(is_even, ROWS + 2, 0)
        class_ref[pl.ds(2, ROWS), :] = terrain[...]
        for source, row in ((from_a, a_row), (from_b, ROWS + 2 - a_row)):
            for j in range(2):
                class_ref[pl.ds(row + j, 1), :] = source[2 * FIELDS, pl.ds(j, 1), :].astype(jnp.int32)
        class_ref[pl.ds(12, 4), :] = strip_classes(edge_words, pick)[:4]
        drag_ref[...] = drag_table(class_ref[...], coef)
        forward_strip(0, strip, edge_words, left_words, sfv, su, sdx)
        outer_faces(0, ext, words, low_words, fvy, vy)
        zero_edges(before_edges)
        weight = level_weight()
        seams = edge_lanes()

        def one_row(r, carry):
            c = carried_row(r, seams, ext, sdx, along, fvy, vy)
            for f in range(FIELDS):
                carried_ref[f, r] = c[f]
            q = coupled(c)[0]
            for f in range(FIELDS):
                before[f, r + 2] = q[f]
            add_edges(before_edges, q, r)
            q = dragged(q, weight * spread(drag_ref, r + 2))
            for f in range(FIELDS):
                middle[f, r + 2] = q[f]
            return carry

        lax.fori_loop(0, ROWS, one_row, 0, unroll=2)
        put_edge_rows(before, 2, to_a, to_b)
        edge_payload(before_edges, to_c)

    return kernel


def put_ghost_rows(values, row, to_a, to_b):
    is_even = row_bases()
    j = row % 2
    above = row >= ROWS

    @pl.when(is_even if above else jnp.logical_not(is_even))
    def _():
        for f in range(FIELDS):
            to_a[2 * f + j] = values[f]

    @pl.when(jnp.logical_not(is_even) if above else is_even)
    def _():
        for f in range(FIELDS):
            to_b[2 * f + j] = values[f]


def second_kernel(has_odd):
    def kernel(*refs):
        (_, _, _, _, before_edges, edge_words, along, fvx, ux, words) = refs[:10]
        (drag_ref, class_ref, low_ref, left_ref, adjoint, from_a, from_b, from_c) = refs[10:18]
        from_d = refs[18] if has_odd else None
        outs = refs[18 + has_odd :]
        ext, before, fvy, vy, part, to_a, to_b, to_c = outs[:8]
        (strip, sfv, su, sdx, a_ext, edges_a, sdc, sdu, gl, gh, dvy, before_strip, cells) = outs[8:]
        pick = side_payloads(from_c, from_d)
        low_words, left_words = low_ref[...], left_ref[...]
        weight = level_weight()
        fill_ghost_rows(before, from_a, from_b)
        for row in (0, 1, ROWS + 2, ROWS + 3):
            q = dragged([before[f, row] for f in range(FIELDS)], weight * spread(drag_ref, row))
            for f in range(FIELDS):
                ext[f, row] = q[f]
        build_strip(before_edges, pick, before_strip)
        q = dragged([before_strip[f] for f in range(FIELDS)], weight * spread(drag_ref, 12))
        for f in range(FIELDS):
            strip[f] = q[f]
        forward_strip(1, strip, edge_words, left_words, sfv, su, sdx)
        outer_faces(1, ext, words, low_words, fvy, vy)
        zero_edges(edges_a)
        for f in range(FIELDS):
            a_ext[f, 0] = jnp.zeros((8, LANES), jnp.float32)
            a_ext[f, ROWS + 1] = jnp.zeros((8, LANES), jnp.float32)
        cells[...] = jnp.zeros((16, LANES), jnp.float32)
        seams = edge_lanes()

        def one_row(r, carry):
            c = carried_row(r, seams, ext, sdx, along, fvy, vy)
            a = [adjoint[f, pl.ds(r, 8, stride=8), :] for f in range(FIELDS)]
            a, terms = stepped_back(c, weight * spread(drag_ref, r + 2), a, True)
            cells[pl.ds(r + 2, 1), :] = level_sum(weight * terms)
            for f in range(FIELDS):
                a_ext[f, r + 1] = a[f]
            add_edges(edges_a, a, r)
            return carry

        lax.fori_loop(0, ROWS, one_row, 0, unroll=2)
        ghosts = backward_strip(1, strip, edges_a, edge_words, left_words, sfv, su, sdc, sdu, to_c)
        pos = strip_pos()
        terms = jnp.where((pos >= 4) & (pos < 8), drag_terms(lambda f: before_strip[f], ghosts), 0.0)
        cells[pl.ds(12, 1), :] = level_sum(weight * terms)

        def put_terms(row, values):
            terms = drag_terms(lambda f: before[f, row + 2], values)
            at = pl.ds(row + 2, 1)
            cells[at, :] = cells[at, :] + level_sum(weight * terms)

        def put_ghost(row, values):
            put_ghost_rows(values, row, to_a, to_b)
            put_terms(row, values)

        def put_own(row, values):
            for f in range(FIELDS):
                part[f, row] = values[f]
            put_terms(row, values)

        backward_faces(1, ext, words, low_words, a_ext, fvy, vy, gl, gh, dvy, put_ghost)
        backward_own(1, ext, words, a_ext, fvx, ux, sdc, sdu, gl, gh, dvy, put_own)
        to_c[4] = binned(class_ref[...], cells[...])

    return kernel


def binned(classes, cells):
    lanes = lane_ids()
    slots = lax.broadcasted_iota(jnp.int32, (8, LANES), 0)
    total = jnp.zeros((8, LANES), jnp.float32)
    for first in range(0, NCLASS, 8):
        block = jnp.zeros((8, LANES), jnp.float32)
        for k in range(first, min(first + 8, NCLASS)):
            block = jnp.where(slots == k - first, level_sum(jnp.where(classes == k, cells, 0.0)), block)
        block = jnp.sum(block, axis=1, keepdims=True)
        total = jnp.where(lanes == first + slots, block, total)
    return jnp.broadcast_to(level_sum(total), (8, LANES))


def collect(part, from_a, from_b, pick, incoming):
    is_even = row_bases()
    a_row = jnp.where(is_even, ROWS - 2, 0)
    b_row = ROWS - 2 - a_row
    for f in range(FIELDS):
        for j in range(2):
            part[f, a_row + j] = part[f, a_row + j] + from_a[2 * f + j]
            part[f, b_row + j] = part[f, b_row + j] + from_b[2 * f + j]
    pos = strip_pos()
    at_left = (pos == 4) | (pos == 5)
    at_right = (pos == 2) | (pos == 3)
    for g in range(4):
        left, right = pick(g)
        for f in range(4 * g, min(4 * g + 4, FIELDS)):
            q = f % 4
            incoming[f] = jnp.where(at_left, roll(left, 4 - 4 * q), jnp.where(at_right, roll(right, -4 * q), 0.0))


def third_kernel(has_odd):
    def kernel(*refs):
        (_, ext, strip, carried_ref, fvy, vy, sfv, su) = refs[:8]
        drag_ref, low_ref, left_ref, edge_words, words = refs[8:13]
        from_a, from_b, from_c = refs[13:16]
        from_d = refs[16] if has_odd else None
        outs = refs[16 + has_odd :]
        part, to_a, to_b, to_c, a_ext, sdc, sdu, gl, gh, dvy = outs[:10]
        incoming, edges_a = outs[10:]
        pick = side_payloads(from_c, from_d)
        low_words, left_words = low_ref[...], left_ref[...]
        collect(part, from_a, from_b, pick, incoming)
        zero_edges(edges_a)
        for f in range(FIELDS):
            a_ext[f, 0] = jnp.zeros((8, LANES), jnp.float32)
            a_ext[f, ROWS + 1] = jnp.zeros((8, LANES), jnp.float32)
        edges = edge_lanes()
        weight = level_weight()

        def one_row(r, carry):
            c = [carried_ref[f, r] for f in range(FIELDS)]
            a = [part[f, r] + jnp.where(edges, roll(incoming[f], 124 - 16 * r), 0.0) for f in range(FIELDS)]
            a, _ = stepped_back(c, weight * spread(drag_ref, r + 2), a, False)
            for f in range(FIELDS):
                a_ext[f, r + 1] = a[f]
            add_edges(edges_a, a, r)
            return carry

        lax.fori_loop(0, ROWS, one_row, 0, unroll=4)
        backward_strip(0, strip, edges_a, edge_words, left_words, sfv, su, sdc, sdu, to_c)

        def put_ghost(row, values):
            put_ghost_rows(values, row, to_a, to_b)

        backward_faces(0, ext, words, low_words, a_ext, fvy, vy, gl, gh, dvy, put_ghost)

    return kernel


def own_kernel(ext, words, a_ext, fvx, ux, sdc, sdu, gl, gh, dvy, part):
    def put(row, values):
        for f in range(FIELDS):
            part[f, row] = values[f]

    backward_own(0, ext, words, a_ext, fvx, ux, sdc, sdu, gl, gh, dvy, put)


def last_kernel(has_odd):
    def kernel(*refs):
        _, from_a, from_b, from_c = refs[:4]
        from_d = refs[4] if has_odd else None
        out, part, incoming = refs[4 + has_odd :]
        pick = side_payloads(from_c, from_d)
        collect(part, from_a, from_b, pick, incoming)
        edges = edge_lanes()

        def one_row(r, carry):
            for f in range(FIELDS):
                value = part[f, r] + jnp.where(edges, roll(incoming[f], (124 - 16 * r) % LANES), 0.0)
                out[f, pl.ds(r, 8, stride=8), :] = value
            return carry

        lax.fori_loop(0, ROWS, one_row, 0, unroll=8)

    return kernel


def shaped(*shape, dtype=jnp.float32):
    return jax.ShapeDtypeStruct(shape, dtype)


def tiles(*shape, dtype=jnp.float32):
    return shaped(*shape, 8, LANES, dtype=dtype)


def scratch(*shape, dtype=jnp.float32):
    return pltpu.VMEM((*shape, 8, LANES), dtype)


def call(kernel, outs, scratches, args, smem=(), hbm=(), aliases=None):
    def space(k):
        return pltpu.SMEM if k in smem else pltpu.HBM if k in hbm else pltpu.VMEM

    return pl.pallas_call(
        kernel,
        out_shape=outs,
        in_specs=[pl.BlockSpec(memory_space=space(k)) for k in range(len(args))],
        out_specs=[pl.BlockSpec(memory_space=pltpu.VMEM)] * len(outs),
        scratch_shapes=scratches,
        input_output_aliases=aliases or {},
        compiler_params=pltpu.CompilerParams(vmem_limit_bytes=32 << 20),
    )(*args)


def swap(x, axis, first):
    peers = lax.axis_size(axis)
    pairs = [(i, i + 1) for i in range(first, peers - 1, 2)]
    if not pairs:
        return None
    return lax.ppermute(x, axis, pairs + [(j, i) for i, j in pairs])


def exchange(to_a, to_b, to_c):
    from_a = swap(to_a, "gy", 0)
    from_b = swap(to_b, "gy", 1)
    from_c = swap(to_c, "gx", 0)
    from_d = swap(to_c, "gx", 1)
    if from_b is None:
        from_b = jnp.zeros_like(to_b)
    return (from_a, from_b, from_c) + (() if from_d is None else (from_d,))


def add_partner(x, axis, distance):
    return x + lax.ppermute(x, axis, [(i, i ^ distance) for i in range(lax.axis_size(axis))])


def body(start_state, final_adjoint, face_words, terrain, drag_coef):
    nx, ny = lax.axis_size("gx"), lax.axis_size("gy")
    has_odd = nx > 2
    start = start_state.reshape(FIELDS, LEV * ROWS, LANES)
    adjoint = final_adjoint.reshape(FIELDS, LEV * ROWS, LANES)
    words = face_words.reshape(8 * ROWS, LANES)
    ints = jnp.int32

    ext, edges, edge_words, *payload = call(
        pack_kernel,
        [tiles(14, 12), tiles(14), tiles(dtype=ints), tiles(29), tiles(29), tiles(5)],
        [
            pltpu.VMEM(start.shape, jnp.float32),
            pltpu.VMEM(words.shape, ints),
            pltpu.VMEM(terrain.shape, ints),
            pltpu.SemaphoreType.DMA((3,)),
        ],
        [pltpu.with_memory_space_constraint(x, pltpu.HBM) for x in (start, words, terrain)],
        hbm=(0, 1, 2),
    )
    got = exchange(*payload)
    early = [tiles(14, 8), tiles(4, 8), tiles(14, 8), tiles(14, 9), tiles(4, 9)]
    fvx, ux, along, fvy, vy = call(early_kernel(0), early, [], [ext, words])
    res = call(
        first_kernel(has_odd),
        [tiles(14, 12), tiles(14, 9), tiles(4, 9), tiles(14), tiles(14, 8), tiles(14), tiles(4)]
        + [shaped(16, LANES), shaped(16, LANES, dtype=ints), tiles(dtype=ints), tiles(dtype=ints)]
        + [tiles(14, 12), tiles(14, 12), tiles(14), tiles(28), tiles(28), tiles(4)],
        [scratch(14)],
        [ext, fvy, vy, edges, edge_words, along, words, terrain, drag_coef, *got],
        smem=(8,),
        aliases={0: 0, 1: 1, 2: 2},
    )
    ext, fvy, vy, strip, carried_ref, sfv, su, drag_ref, class_ref, low_ref, left_ref = res[:11]
    middle, before, before_edges, *payload = res[11:]
    got = exchange(*payload)
    fvx2, ux2, along2, fvy2, vy2 = call(early_kernel(1), early, [], [middle, words])
    back = [tiles(14, 10), tiles(14), tiles(4), tiles(14, 15), tiles(14, 15), tiles(4, 15)]
    kept = [scratch(14, 10), scratch(14), scratch(14), scratch(4), scratch(14, 15), scratch(14, 15), scratch(4, 15)]
    part, *payload = call(
        second_kernel(has_odd),
        [tiles(14, 12), tiles(14, 12), tiles(14, 9), tiles(4, 9), tiles(14, 8), tiles(28), tiles(28), tiles(5)],
        [scratch(14), scratch(14), scratch(4), scratch(14), *kept, scratch(14), pltpu.VMEM((16, LANES), jnp.float32)],
        [middle, before, fvy2, vy2, before_edges, edge_words, along2, fvx2, ux2, words]
        + [drag_ref, class_ref, low_ref, left_ref, adjoint, *got],
        aliases={0: 0, 1: 1, 2: 2, 3: 3},
    )[4:]
    got = exchange(*payload)
    grads = payload[2][4] + got[2][4]
    steps = [("gx", 2**k) for k in range(1, 32) if 2**k < nx] + [("gy", 2**k) for k in range(1, 32) if 2**k < ny]
    grads = add_partner(add_partner(grads, "gy", 1), *steps[0])
    part, to_a, to_b, to_c, *adjoints = call(
        third_kernel(has_odd),
        [tiles(14, 8), tiles(28), tiles(28), tiles(4), *back],
        [scratch(14), scratch(14)],
        [part, ext, strip, carried_ref, fvy, vy, sfv, su, drag_ref, low_ref, left_ref, edge_words, words, *got],
        aliases={0: 0},
    )
    a_ext, sdc, sdu, gl, gh, dvy = adjoints
    grads, to_c = lax.optimization_barrier((grads, to_c))
    got = exchange(to_a, to_b, to_c)
    half = len(steps) // 2 + 1
    a_ext, from_a = lax.optimization_barrier((a_ext, got[0]))
    got = (from_a, *got[1:])
    for axis, distance in steps[1:half]:
        grads = add_partner(grads, axis, distance)
    (part,) = call(own_kernel, [tiles(14, 8)], [], [ext, words, a_ext, fvx, ux, sdc, sdu, gl, gh, dvy])
    for axis, distance in steps[half:]:
        grads = add_partner(grads, axis, distance)
    out, _ = call(
        last_kernel(has_odd),
        [shaped(FIELDS, LEV * ROWS, LANES), tiles(14, 8)],
        [scratch(14)],
        [part, *got],
        aliases={0: 1},
    )
    grad_scale = math.sqrt(NCLASS / (terrain.size * nx * ny * LEV))
    return (out.reshape(start_state.shape), grads[0, :NCLASS] * grad_scale)


def solution(mesh):
    placed = (
        P(None, None, "gy", "gx"),
        P(None, None, "gy", "gx"),
        P(None, None, None, "gy", "gx"),
        P("gy", "gx"),
        P(),
    )
    return jax.shard_map(
        body,
        mesh=mesh,
        in_specs=placed,
        out_specs=(P(None, None, "gy", "gx"), P()),
        check_vma=False,
    )
```

```python
import math

import jax
import jax.numpy as jnp
from jax import lax
from jax.experimental import pallas as pl
from jax.experimental.pallas import tpu as pltpu
from jax.sharding import PartitionSpec as P

LEV = 8
NCLASS = 24
FIELDS = 14
ROWS = 8
LANES = 128
PHASES = ((0, 5), (5, 3), (8, 3), (11, 3))
FACE = 0.3 * 0.5 * 0.5
COUPLING = 0.5
DRAG_STEP = 0.5
TERRAIN_SLOT = 2


def roll(v, shift):
    return pltpu.roll(v, shift % LANES if isinstance(shift, int) else shift, 1)


def lane_ids():
    return lax.broadcasted_iota(jnp.int32, (8, LANES), 1)


def strip_pos():
    return lane_ids() % 16


def strip_row():
    return lane_ids() // 16


def level_bits():
    levels = lax.broadcasted_iota(jnp.int32, (8, LANES), 0)
    return [jnp.left_shift(jnp.ones_like(levels), levels + LEV * k) for k in range(2)]


def edge_lanes():
    lanes = lane_ids()
    return (lanes < 2) | (lanes >= LANES - 2)


def spread(ref, index):
    return jnp.broadcast_to(ref[pl.ds(index, 1), :], (8, LANES))


def plane(step, direction, pair):
    return step * 4 + direction * 2 + pair


def position(axis):
    return lax.axis_index(axis), lax.axis_size(axis)


def into_slots(values):
    pos = strip_pos() // 4
    total = jnp.zeros((8, LANES), jnp.float32)
    for slot, value in enumerate(values):
        total = jnp.where(pos == slot, value, total)
    return total


def add_edges(edges_ref, values, row):
    mine = strip_row() == row
    for f, value in enumerate(values):
        edges_ref[f] = jnp.where(mine, roll(value, 16 * row + 4), edges_ref[f])


def zero_edges(edges_ref, count=FIELDS):
    for f in range(count):
        edges_ref[f] = jnp.zeros((8, LANES), edges_ref.dtype)


def edge_payload(edges_ref, out_ref):
    for g in range(4):
        fields = range(4 * g, min(4 * g + 4, FIELDS))
        out_ref[g] = into_slots([roll(edges_ref[f], 4 * (f % 4) - 2) for f in fields])


def side_payloads(even_ref, odd_ref):
    index, _ = position("gx")
    is_even = index % 2 == 0

    def pick(k):
        a = even_ref[k]
        b = jnp.zeros_like(a) if odd_ref is None else odd_ref[k]
        return jnp.where(is_even, b, a), jnp.where(is_even, a, b)

    return pick


def build_strip(edges_ref, pick, strip_ref):
    pos = strip_pos()
    for g in range(4):
        left, right = pick(g)
        for f in range(4 * g, min(4 * g + 4, FIELDS)):
            q = f % 4
            own = edges_ref[f]
            value = jnp.where(pos < 4, own, roll(right, 2 - 4 * q))
            value = jnp.where(pos < 6, value, roll(left, 6 - 4 * q))
            value = jnp.where(pos < 8, value, roll(own, 4))
            strip_ref[f] = jnp.where(pos < 12, value, 0.0)


def strip_words(edge_words_ref, left_words, which):
    pos = strip_pos()
    own = spread(edge_words_ref, which)
    left = jnp.broadcast_to(left_words[which : which + 1], (8, LANES))
    value = jnp.where(pos < 4, own, roll(own, 4))
    return jnp.where(pos == 7, roll(left, 4), value)


def strip_classes(edge_words_ref, pick):
    pos = strip_pos()
    own = spread(edge_words_ref, TERRAIN_SLOT)
    left, right = [jnp.broadcast_to(v[TERRAIN_SLOT : TERRAIN_SLOT + 1], (8, LANES)).astype(jnp.int32) for v in pick(4)]
    value = jnp.where(pos < 4, own, jnp.where(pos < 6, right, jnp.where(pos < 8, roll(left, 4), roll(own, 4))))
    return value


def face_walls():
    gx, nx = position("gx")
    pos = strip_pos()
    shut = ((pos == 7) & (gx == 0)) | ((pos == 3) & (gx == nx - 1))
    return jnp.where(shut, 0.0, FACE)


def row_wall(j):
    gy, ny = position("gy")
    shut = ((j == 0) & (gy == 0)) | ((j == ROWS) & (gy == ny - 1))
    return jnp.where(shut, 0.0, FACE)


def inverse_root(mass):
    return lax.rsqrt(mass * mass + 1.0)


def gather_edges(v):
    pos = strip_pos()
    return jnp.where((pos == 4) | (pos == 5), roll(v, -4), v)


def face_values(behind, here, ahead, beyond, flag):
    return jnp.where(flag, 3.0 * here - behind, 3.0 * ahead - beyond)


def forward_strip(step, strip, edge_words, left_words, sfv, su, sdx):
    bits = level_bits()
    walls = face_walls()
    for p, (lead, members) in enumerate(PHASES):
        word = strip_words(edge_words, left_words, plane(step, 0, p // 2))
        flag = (word & bits[p % 2]) != 0
        u = strip[lead + 1] * inverse_root(strip[lead])
        speed = walls * (u + roll(u, -1))
        su[p] = speed
        for f in range(lead, lead + members):
            c = strip[f]
            ahead = roll(c, -1)
            value = face_values(roll(c, 1), c, ahead, roll(c, -2), flag)
            sfv[f] = value
            flux = speed * value
            sdx[f] = gather_edges(flux - roll(flux, 1))


def forward_face(j, step, ext, words, low_words, fvy, vy):
    bits = level_bits()
    wall = FACE if low_words is None else row_wall(j)
    for p, (lead, members) in enumerate(PHASES):
        which = plane(step, 1, p // 2)
        word = face_word(j, words, low_words, which)
        flag = (word & bits[p % 2]) != 0
        v_low = ext[lead + 2, j + 1] * inverse_root(ext[lead, j + 1])
        v_high = ext[lead + 2, j + 2] * inverse_root(ext[lead, j + 2])
        vy[p, j] = wall * (v_low + v_high)
        for f in range(lead, lead + members):
            fvy[f, j] = face_values(ext[f, j], ext[f, j + 1], ext[f, j + 2], ext[f, j + 3], flag)


def face_word(j, words, low_words, which):
    if low_words is None:
        return spread(words, which * ROWS + j - 1)
    here = spread(words, which * ROWS + jnp.maximum(j - 1, 0))
    low = jnp.broadcast_to(low_words[which : which + 1], (8, LANES))
    return jnp.where(j == 0, low, here)


def carried_row(r, edges, ext, sdx, along, fvy, vy):
    carried = []
    for p, (lead, members) in enumerate(PHASES):
        below, above = vy[p, r], vy[p, r + 1]
        for f in range(lead, lead + members):
            seam = ext[f, r + 2] - roll(sdx[f], 124 - 16 * r)
            along_y = above * fvy[f, r + 1] - below * fvy[f, r]
            carried.append(jnp.where(edges, seam, along[f, r]) - along_y)
    return carried


def early_kernel(step):
    def kernel(ext, words, *refs):
        fvx, ux, along, fvy, vy = refs[-6:-1] if step == 0 else refs
        bits = level_bits()
        if step == 0:
            coef, coef_rows = refs[0], refs[-1]
            for k in range(NCLASS):
                coef_rows[pl.ds(k, 1), :] = jnp.full((1, LANES), coef[k], jnp.float32)

        def one_row(r, carry):
            for p, (lead, members) in enumerate(PHASES):
                word = spread(words, plane(step, 0, p // 2) * ROWS + r)
                flag = (word & bits[p % 2]) != 0
                u = ext[lead + 1, r + 2] * inverse_root(ext[lead, r + 2])
                speed = FACE * (u + roll(u, -1))
                ux[p, r] = speed
                for f in range(lead, lead + members):
                    c = ext[f, r + 2]
                    value = face_values(roll(c, 1), c, roll(c, -1), roll(c, -2), flag)
                    fvx[f, r] = value
                    flux = speed * value
                    along[f, r] = c - (flux - roll(flux, 1))
            return carry

        lax.fori_loop(0, ROWS, one_row, 0, unroll=2)
        for j in range(2, ROWS - 1):
            forward_face(j, step, ext, words, None, fvy, vy)

    return kernel


def outer_faces(step, ext, words, low_words, fvy, vy):
    for j in (0, 1, ROWS - 1, ROWS):
        forward_face(j, step, ext, words, low_words, fvy, vy)


def coupled(c):
    s = inverse_root(c[0])
    u, v = c[1] * s, c[2] * s
    gas_x, gas_y = c[1], c[2]
    out = [None] * FIELDS
    for lead, _ in PHASES[1:]:
        pull_x = COUPLING * (c[lead] * u - c[lead + 1])
        pull_y = COUPLING * (c[lead] * v - c[lead + 2])
        gas_x, gas_y = gas_x - pull_x, gas_y - pull_y
        out[lead] = c[lead]
        out[lead + 1], out[lead + 2] = c[lead + 1] + pull_x, c[lead + 2] + pull_y
    out[0], out[1], out[2], out[3], out[4] = c[0], gas_x, gas_y, c[3], c[4]
    return out, s, u, v


def dragged(q, drag):
    q = list(q)
    for lead, _ in PHASES:
        s = inverse_root(q[lead])
        u, v = q[lead + 1] * s, q[lead + 2] * s
        factor = 1.0 - drag * jnp.sqrt(u * u + v * v + 1.0)
        q[lead + 1], q[lead + 2] = q[lead + 1] * factor, q[lead + 2] * factor
    return q


def drag_terms(q, a):
    total = None
    for lead, _ in PHASES:
        s = inverse_root(q(lead))
        x, y = q(lead + 1), q(lead + 2)
        u, v = x * s, y * s
        term = jnp.sqrt(u * u + v * v + 1.0) * (a[lead + 1] * x + a[lead + 2] * y)
        total = term if total is None else total + term
    return -total


def stepped_back(c, drag, a, want_terms):
    q, s0, gas_u, gas_v = coupled(c)
    a = list(a)
    terms = jnp.zeros((8, LANES), jnp.float32)
    for lead, _ in PHASES:
        m, x, y = q[lead], q[lead + 1], q[lead + 2]
        s = s0 if lead == 0 else inverse_root(m)
        u, v = x * s, y * s
        energy = u * u + v * v
        root = lax.rsqrt(energy + 1.0)
        w = (energy + 1.0) * root
        dot = a[lead + 1] * x + a[lead + 2] * y
        if want_terms:
            terms = terms - w * dot
        k = drag * dot * root
        factor = 1.0 - drag * w
        ks = k * s
        a[lead + 1] = a[lead + 1] * factor - ks * u
        a[lead + 2] = a[lead + 2] * factor - ks * v
        a[lead] = a[lead] + k * energy * m * (s * s)
    du = jnp.zeros((8, LANES), jnp.float32)
    dv = jnp.zeros((8, LANES), jnp.float32)
    for lead, _ in PHASES[1:]:
        rx, ry = COUPLING * (a[lead + 1] - a[1]), COUPLING * (a[lead + 2] - a[2])
        a[lead] = a[lead] + rx * gas_u + ry * gas_v
        du, dv = du + c[lead] * rx, dv + c[lead] * ry
        a[lead + 1], a[lead + 2] = a[lead + 1] - rx, a[lead + 2] - ry
    a[1], a[2] = a[1] + du * s0, a[2] + dv * s0
    a[0] = a[0] - (gas_u * du + gas_v * dv) * c[0] * (s0 * s0)
    return a, terms


def add_speed_terms(total, state, lead, du, dv):
    m, x, y = state
    s = inverse_root(m)
    pull = None
    if du is not None:
        total[lead + 1] = total[lead + 1] + s * du
        pull = x * s * du
    if dv is not None:
        total[lead + 2] = total[lead + 2] + s * dv
        pull = y * s * dv if pull is None else pull + y * s * dv
    total[lead] = total[lead] - pull * m * (s * s)


def scatter_x(a, value, speed, flag):
    ahead = roll(a, -1) - a
    g = speed * ahead
    low = jnp.where(flag, g, 0.0)
    high = roll(g - low, 1)
    return 3.0 * (low + high) - roll(low, -1) - roll(high, 1), value * ahead


def expand_edges(own):
    pos = strip_pos()
    value = jnp.where(pos < 4, own, jnp.where((pos >= 8) & (pos < 12), roll(own, 4), 0.0))
    return value


def backward_strip(step, strip, edges_a, edge_words, left_words, sfv, su, sdc, sdu, out_c):
    bits = level_bits()
    walls = face_walls()
    ghosts = []
    for p, (lead, members) in enumerate(PHASES):
        word = strip_words(edge_words, left_words, plane(step, 0, p // 2))
        flag = (word & bits[p % 2]) != 0
        speed = su[p]
        du = jnp.zeros((8, LANES), jnp.float32)
        total = {}
        for f in range(lead, lead + members):
            total[f], term = scatter_x(expand_edges(edges_a[f]), sfv[f], speed, flag)
            sdc[f] = gather_edges(total[f])
            du = du + term
        du = walls * du
        du = du + roll(du, 1)
        sdu[p] = gather_edges(du)
        add_speed_terms(total, (strip[lead], strip[lead + 1], strip[lead + 2]), lead, du, None)
        ghosts.extend(total[f] for f in range(lead, lead + members))
    for g in range(4):
        fields = range(4 * g, min(4 * g + 4, FIELDS))
        out_c[g] = into_slots([roll(ghosts[f], 4 * (f % 4) - 4) for f in fields])
    return ghosts


def backward_faces(step, ext, words, low_words, a_ext, fvy, vy, gl, gh, dvy, put):
    bits = level_bits()
    zero = jnp.zeros((8, LANES), jnp.float32)
    for k in (0, 1, 2, 12, 13, 14):
        for f in range(FIELDS):
            gl[f, k] = zero
            gh[f, k] = zero
        for p in range(4):
            dvy[p, k] = zero

    def face(j, carry):
        wall = row_wall(j)
        for p, (lead, members) in enumerate(PHASES):
            word = face_word(j, words, low_words, plane(step, 1, p // 2))
            flag = (word & bits[p % 2]) != 0
            speed = vy[p, j]
            dv = jnp.zeros((8, LANES), jnp.float32)
            for f in range(lead, lead + members):
                ahead = a_ext[f, j + 1] - a_ext[f, j]
                g = speed * ahead
                low = jnp.where(flag, g, 0.0)
                gl[f, j + 3] = low
                gh[f, j + 3] = g - low
                dv = dv + fvy[f, j] * ahead
            dvy[p, j + 3] = wall * dv
        return carry

    lax.fori_loop(0, ROWS + 1, face, 0, unroll=9)
    for i in (-2, -1, ROWS, ROWS + 1):
        total = [transposed_y(gl, gh, f, i) for f in range(FIELDS)]
        for p, (lead, members) in enumerate(PHASES):
            dv = dvy[p, i + 4] + dvy[p, i + 3]
            state = (ext[lead, i + 2], ext[lead + 1, i + 2], ext[lead + 2, i + 2])
            add_speed_terms(total, state, lead, None, dv)
        put(i, total)


def transposed_y(gl, gh, f, i):
    return 3.0 * (gl[f, i + 4] + gh[f, i + 3]) - gl[f, i + 5] - gh[f, i + 2]


def backward_own(step, ext, words, a_ext, fvx, ux, sdc, sdu, gl, gh, dvy, put):
    bits = level_bits()
    edges = edge_lanes()

    def own(r, carry):
        total = [None] * FIELDS
        for p, (lead, members) in enumerate(PHASES):
            word = spread(words, plane(step, 0, p // 2) * ROWS + r)
            flag = (word & bits[p % 2]) != 0
            speed = ux[p, r]
            du = jnp.zeros((8, LANES), jnp.float32)
            for f in range(lead, lead + members):
                a = a_ext[f, r + 1]
                part, term = scatter_x(a, fvx[f, r], speed, flag)
                part = jnp.where(edges, roll(sdc[f], 124 - 16 * r), part)
                total[f] = a + part + transposed_y(gl, gh, f, r)
                du = du + term
            du = FACE * (du + roll(du, 1))
            du = jnp.where(edges, roll(sdu[p], 124 - 16 * r), du)
            dv = dvy[p, r + 4] + dvy[p, r + 3]
            state = (ext[lead, r + 2], ext[lead + 1, r + 2], ext[lead + 2, r + 2])
            add_speed_terms(total, state, lead, du, dv)
        put(r, total)
        return carry

    lax.fori_loop(0, ROWS, own, 0, unroll=2)


def level_weight():
    levels = lax.broadcasted_iota(jnp.int32, (8, LANES), 0)
    weight = jnp.full((8, LANES), DRAG_STEP, jnp.float32)
    for k in range(3):
        weight = jnp.where((levels // 2**k) % 2 == 1, weight * 0.5 ** (2**k), weight)
    return weight


def drag_table(classes, coef_rows):
    drag = jnp.zeros(classes.shape, jnp.float32)
    for k in range(NCLASS):
        drag = jnp.where(classes == k, jnp.broadcast_to(coef_rows[pl.ds(k, 1), :], classes.shape), drag)
    return drag


def level_sum(v):
    return jnp.sum(v, axis=0, keepdims=True)


def row_bases():
    gy, _ = position("gy")
    is_even = gy % 2 == 0
    return is_even


def fill_ghost_rows(ext, from_a, from_b):
    is_even = row_bases()
    a_row = jnp.where(is_even, ROWS + 2, 0)
    b_row = jnp.where(is_even, 0, ROWS + 2)
    for f in range(FIELDS):
        for j in range(2):
            ext[f, a_row + j] = from_a[2 * f + j]
            ext[f, b_row + j] = from_b[2 * f + j]


def put_edge_rows(source, offset, to_a, to_b):
    is_even = row_bases()
    a_row = jnp.where(is_even, ROWS - 2, 0) + offset
    b_row = jnp.where(is_even, 0, ROWS - 2) + offset
    for f in range(FIELDS):
        for j in range(2):
            to_a[2 * f + j] = source[f, a_row + j]
            to_b[2 * f + j] = source[f, b_row + j]


def pack_kernel(start_in, words_in, terrain_in, words, terrain, ext, edges, edge_words, to_a, to_b, to_c, start, sems):
    copies = [
        pltpu.make_async_copy(source, target, sems.at[k])
        for k, (source, target) in enumerate(((start_in, start), (words_in, words), (terrain_in, terrain)))
    ]
    for copy in copies:
        copy.start()
    zero_edges(edges)
    edge_words[...] = jnp.zeros((8, LANES), jnp.int32)
    slots = lax.broadcasted_iota(jnp.int32, (8, LANES), 0)
    for copy in copies:
        copy.wait()

    def one_row(r, carry):
        values = [start[f, pl.ds(r, 8, stride=8), :] for f in range(FIELDS)]
        for f in range(FIELDS):
            ext[f, r + 2] = values[f]
        add_edges(edges, values, r)
        mine = strip_row() == r
        row_words = jnp.where(slots == TERRAIN_SLOT, spread(terrain, r), words[pl.ds(r, 8, stride=8), :])
        edge_words[...] = jnp.where(mine, roll(row_words, (16 * r + 4) % LANES), edge_words[...])
        return carry

    lax.fori_loop(0, ROWS, one_row, 0, unroll=8)
    put_edge_rows(ext, 2, to_a, to_b)
    top = words[pl.ds(ROWS - 1, 8, stride=8), :]
    is_even = row_bases()
    a_row = jnp.where(is_even, ROWS - 2, 0)
    for target, row in ((to_a, a_row), (to_b, ROWS - 2 - a_row)):
        mixed = jnp.where(slots == 0, spread(terrain, row), jnp.where(slots == 1, spread(terrain, row + 1), top))
        target[2 * FIELDS] = mixed.astype(jnp.float32)
    edge_payload(edges, to_c)
    to_c[4] = edge_words[...].astype(jnp.float32)


def neighbour_words(from_a, from_b, pick):
    low = jnp.where(row_bases(), from_b[2 * FIELDS], from_a[2 * FIELDS]).astype(jnp.int32)
    left, _ = pick(4)
    return low, left.astype(jnp.int32)


def first_kernel(has_odd):
    def kernel(*refs):
        (_, _, _, edges, edge_words, along, words, terrain, coef, from_a, from_b, from_c) = refs[:12]
        from_d = refs[12] if has_odd else None
        outs = refs[12 + has_odd :]
        (ext, fvy, vy, strip, carried_ref, sfv, su, drag_ref, class_ref, low_ref, left_ref) = outs[:11]
        middle, before, before_edges, to_a, to_b, to_c = outs[11:17]
        (sdx,) = outs[17:]
        pick = side_payloads(from_c, from_d)
        fill_ghost_rows(ext, from_a, from_b)
        build_strip(edges, pick, strip)
        low_words, left_words = neighbour_words(from_a, from_b, pick)
        low_ref[...] = low_words
        left_ref[...] = left_words
        is_even = row_bases()
        a_row = jnp.where(is_even, ROWS + 2, 0)
        class_ref[pl.ds(2, ROWS), :] = terrain[...]
        for source, row in ((from_a, a_row), (from_b, ROWS + 2 - a_row)):
            for j in range(2):
                class_ref[pl.ds(row + j, 1), :] = source[2 * FIELDS, pl.ds(j, 1), :].astype(jnp.int32)
        class_ref[pl.ds(12, 4), :] = strip_classes(edge_words, pick)[:4]
        drag_ref[...] = drag_table(class_ref[...], coef)
        forward_strip(0, strip, edge_words, left_words, sfv, su, sdx)
        outer_faces(0, ext, words, low_words, fvy, vy)
        zero_edges(before_edges)
        weight = level_weight()
        seams = edge_lanes()

        def one_row(r, carry):
            c = carried_row(r, seams, ext, sdx, along, fvy, vy)
            for f in range(FIELDS):
                carried_ref[f, r] = c[f]
            q = coupled(c)[0]
            for f in range(FIELDS):
                before[f, r + 2] = q[f]
            add_edges(before_edges, q, r)
            q = dragged(q, weight * spread(drag_ref, r + 2))
            for f in range(FIELDS):
                middle[f, r + 2] = q[f]
            return carry

        lax.fori_loop(0, ROWS, one_row, 0, unroll=2)
        put_edge_rows(before, 2, to_a, to_b)
        edge_payload(before_edges, to_c)

    return kernel


def put_ghost_rows(values, row, to_a, to_b):
    is_even = row_bases()
    j = row % 2
    above = row >= ROWS

    @pl.when(is_even if above else jnp.logical_not(is_even))
    def _():
        for f in range(FIELDS):
            to_a[2 * f + j] = values[f]

    @pl.when(jnp.logical_not(is_even) if above else is_even)
    def _():
        for f in range(FIELDS):
            to_b[2 * f + j] = values[f]


def second_kernel(has_odd):
    def kernel(*refs):
        (_, _, _, _, before_edges, edge_words, along, fvx, ux, words) = refs[:10]
        (drag_ref, class_ref, low_ref, left_ref, adjoint, from_a, from_b, from_c) = refs[10:18]
        from_d = refs[18] if has_odd else None
        outs = refs[18 + has_odd :]
        ext, before, fvy, vy, part, to_a, to_b, to_c = outs[:8]
        (strip, sfv, su, sdx, a_ext, edges_a, sdc, sdu, gl, gh, dvy, before_strip, cells) = outs[8:]
        pick = side_payloads(from_c, from_d)
        low_words, left_words = low_ref[...], left_ref[...]
        weight = level_weight()
        fill_ghost_rows(before, from_a, from_b)
        for row in (0, 1, ROWS + 2, ROWS + 3):
            q = dragged([before[f, row] for f in range(FIELDS)], weight * spread(drag_ref, row))
            for f in range(FIELDS):
                ext[f, row] = q[f]
        build_strip(before_edges, pick, before_strip)
        q = dragged([before_strip[f] for f in range(FIELDS)], weight * spread(drag_ref, 12))
        for f in range(FIELDS):
            strip[f] = q[f]
        forward_strip(1, strip, edge_words, left_words, sfv, su, sdx)
        outer_faces(1, ext, words, low_words, fvy, vy)
        zero_edges(edges_a)
        for f in range(FIELDS):
            a_ext[f, 0] = jnp.zeros((8, LANES), jnp.float32)
            a_ext[f, ROWS + 1] = jnp.zeros((8, LANES), jnp.float32)
        cells[...] = jnp.zeros((16, LANES), jnp.float32)
        seams = edge_lanes()

        def one_row(r, carry):
            c = carried_row(r, seams, ext, sdx, along, fvy, vy)
            a = [adjoint[f, pl.ds(r, 8, stride=8), :] for f in range(FIELDS)]
            a, terms = stepped_back(c, weight * spread(drag_ref, r + 2), a, True)
            cells[pl.ds(r + 2, 1), :] = level_sum(weight * terms)
            for f in range(FIELDS):
                a_ext[f, r + 1] = a[f]
            add_edges(edges_a, a, r)
            return carry

        lax.fori_loop(0, ROWS, one_row, 0, unroll=2)
        ghosts = backward_strip(1, strip, edges_a, edge_words, left_words, sfv, su, sdc, sdu, to_c)
        pos = strip_pos()
        terms = jnp.where((pos >= 4) & (pos < 8), drag_terms(lambda f: before_strip[f], ghosts), 0.0)
        cells[pl.ds(12, 1), :] = level_sum(weight * terms)

        def put_terms(row, values):
            terms = drag_terms(lambda f: before[f, row + 2], values)
            at = pl.ds(row + 2, 1)
            cells[at, :] = cells[at, :] + level_sum(weight * terms)

        def put_ghost(row, values):
            put_ghost_rows(values, row, to_a, to_b)
            put_terms(row, values)

        def put_own(row, values):
            for f in range(FIELDS):
                part[f, row] = values[f]
            put_terms(row, values)

        backward_faces(1, ext, words, low_words, a_ext, fvy, vy, gl, gh, dvy, put_ghost)
        backward_own(1, ext, words, a_ext, fvx, ux, sdc, sdu, gl, gh, dvy, put_own)
        to_c[4] = binned(class_ref[...], cells[...])

    return kernel


def binned(classes, cells):
    lanes = lane_ids()
    slots = lax.broadcasted_iota(jnp.int32, (8, LANES), 0)
    total = jnp.zeros((8, LANES), jnp.float32)
    for first in range(0, NCLASS, 8):
        block = jnp.zeros((8, LANES), jnp.float32)
        for k in range(first, min(first + 8, NCLASS)):
            block = jnp.where(slots == k - first, level_sum(jnp.where(classes == k, cells, 0.0)), block)
        block = jnp.sum(block, axis=1, keepdims=True)
        total = jnp.where(lanes == first + slots, block, total)
    return jnp.broadcast_to(level_sum(total), (8, LANES))


def collect(part, from_a, from_b, pick, incoming):
    is_even = row_bases()
    a_row = jnp.where(is_even, ROWS - 2, 0)
    b_row = ROWS - 2 - a_row
    for f in range(FIELDS):
        for j in range(2):
            part[f, a_row + j] = part[f, a_row + j] + from_a[2 * f + j]
            part[f, b_row + j] = part[f, b_row + j] + from_b[2 * f + j]
    pos = strip_pos()
    at_left = (pos == 4) | (pos == 5)
    at_right = (pos == 2) | (pos == 3)
    for g in range(4):
        left, right = pick(g)
        for f in range(4 * g, min(4 * g + 4, FIELDS)):
            q = f % 4
            incoming[f] = jnp.where(at_left, roll(left, 4 - 4 * q), jnp.where(at_right, roll(right, -4 * q), 0.0))


def third_kernel(has_odd):
    def kernel(*refs):
        _, carried_ref, drag_ref, from_a, from_b, from_c = refs[:6]
        from_d = refs[6] if has_odd else None
        part, a_ext, edges_a, incoming = refs[6 + has_odd :]
        pick = side_payloads(from_c, from_d)
        collect(part, from_a, from_b, pick, incoming)
        zero_edges(edges_a)
        for f in range(FIELDS):
            a_ext[f, 0] = jnp.zeros((8, LANES), jnp.float32)
            a_ext[f, ROWS + 1] = jnp.zeros((8, LANES), jnp.float32)
        edges = edge_lanes()
        weight = level_weight()

        def one_row(r, carry):
            c = [carried_ref[f, r] for f in range(FIELDS)]
            a = [part[f, r] + jnp.where(edges, roll(incoming[f], 124 - 16 * r), 0.0) for f in range(FIELDS)]
            a, _ = stepped_back(c, weight * spread(drag_ref, r + 2), a, False)
            for f in range(FIELDS):
                a_ext[f, r + 1] = a[f]
            add_edges(edges_a, a, r)
            return carry

        lax.fori_loop(0, ROWS, one_row, 0, unroll=4)

    return kernel


def seam_kernel(a_ext, edges_a, ext, strip, fvy, vy, sfv, su, low_ref, left_ref, edge_words, words, grads, *outs):
    to_a, to_b, to_c, sdc, sdu, gl, gh, dvy = outs
    low_words, left_words = low_ref[...], left_ref[...]
    backward_strip(0, strip, edges_a, edge_words, left_words, sfv, su, sdc, sdu, to_c)

    def put_ghost(row, values):
        put_ghost_rows(values, row, to_a, to_b)

    backward_faces(0, ext, words, low_words, a_ext, fvy, vy, gl, gh, dvy, put_ghost)
    to_a[2 * FIELDS] = grads[...]


def own_kernel(ext, words, a_ext, fvx, ux, sdc, sdu, gl, gh, dvy, part):
    def put(row, values):
        for f in range(FIELDS):
            part[f, row] = values[f]

    backward_own(0, ext, words, a_ext, fvx, ux, sdc, sdu, gl, gh, dvy, put)


def last_kernel(has_odd):
    def kernel(*refs):
        _, from_a, from_b, from_c = refs[:4]
        from_d = refs[4] if has_odd else None
        out, part, incoming = refs[4 + has_odd :]
        pick = side_payloads(from_c, from_d)
        collect(part, from_a, from_b, pick, incoming)
        edges = edge_lanes()

        def one_row(r, carry):
            for f in range(FIELDS):
                value = part[f, r] + jnp.where(edges, roll(incoming[f], (124 - 16 * r) % LANES), 0.0)
                out[f, pl.ds(r, 8, stride=8), :] = value
            return carry

        lax.fori_loop(0, ROWS, one_row, 0, unroll=8)

    return kernel


def shaped(*shape, dtype=jnp.float32):
    return jax.ShapeDtypeStruct(shape, dtype)


def tiles(*shape, dtype=jnp.float32):
    return shaped(*shape, 8, LANES, dtype=dtype)


def scratch(*shape, dtype=jnp.float32):
    return pltpu.VMEM((*shape, 8, LANES), dtype)


def call(kernel, outs, scratches, args, smem=(), hbm=(), aliases=None):
    def space(k):
        return pltpu.SMEM if k in smem else pltpu.HBM if k in hbm else pltpu.VMEM

    return pl.pallas_call(
        kernel,
        out_shape=outs,
        in_specs=[pl.BlockSpec(memory_space=space(k)) for k in range(len(args))],
        out_specs=[pl.BlockSpec(memory_space=pltpu.VMEM)] * len(outs),
        scratch_shapes=scratches,
        input_output_aliases=aliases or {},
        compiler_params=pltpu.CompilerParams(vmem_limit_bytes=32 << 20),
    )(*args)


def swap(x, axis, first):
    peers = lax.axis_size(axis)
    pairs = [(i, i + 1) for i in range(first, peers - 1, 2)]
    if not pairs:
        return None
    return lax.ppermute(x, axis, pairs + [(j, i) for i, j in pairs])


def exchange(to_a, to_b, to_c):
    from_a = swap(to_a, "gy", 0)
    from_b = swap(to_b, "gy", 1)
    from_c = swap(to_c, "gx", 0)
    from_d = swap(to_c, "gx", 1)
    if from_b is None:
        from_b = jnp.zeros_like(to_b)
    return (from_a, from_b, from_c) + (() if from_d is None else (from_d,))


def add_partner(x, axis, distance):
    return x + lax.ppermute(x, axis, [(i, i ^ distance) for i in range(lax.axis_size(axis))])


def body(start_state, final_adjoint, face_words, terrain, drag_coef):
    nx, ny = lax.axis_size("gx"), lax.axis_size("gy")
    has_odd = nx > 2
    start = start_state.reshape(FIELDS, LEV * ROWS, LANES)
    adjoint = final_adjoint.reshape(FIELDS, LEV * ROWS, LANES)
    words = face_words.reshape(8 * ROWS, LANES)
    ints = jnp.int32

    words, terrain, ext, edges, edge_words, *payload = call(
        pack_kernel,
        [shaped(*words.shape, dtype=ints), shaped(*terrain.shape, dtype=ints)]
        + [tiles(14, 12), tiles(14), tiles(dtype=ints), tiles(29), tiles(29), tiles(5)],
        [
            pltpu.VMEM(start.shape, jnp.float32),
            pltpu.SemaphoreType.DMA((3,)),
        ],
        [pltpu.with_memory_space_constraint(x, pltpu.HBM) for x in (start, words, terrain)],
        hbm=(0, 1, 2),
    )
    got = exchange(*payload)
    early = [tiles(14, 8), tiles(4, 8), tiles(14, 8), tiles(14, 9), tiles(4, 9)]
    fvx, ux, along, fvy, vy, coef_rows = call(
        early_kernel(0), [*early, shaped(NCLASS, LANES)], [], [ext, words, drag_coef], smem=(2,)
    )
    res = call(
        first_kernel(has_odd),
        [tiles(14, 12), tiles(14, 9), tiles(4, 9), tiles(14), tiles(14, 8), tiles(14), tiles(4)]
        + [shaped(16, LANES), shaped(16, LANES, dtype=ints), tiles(dtype=ints), tiles(dtype=ints)]
        + [tiles(14, 12), tiles(14, 12), tiles(14), tiles(28), tiles(28), tiles(4)],
        [scratch(14)],
        [ext, fvy, vy, edges, edge_words, along, words, terrain, coef_rows, *got],
        aliases={0: 0, 1: 1, 2: 2},
    )
    ext, fvy, vy, strip, carried_ref, sfv, su, drag_ref, class_ref, low_ref, left_ref = res[:11]
    middle, before, before_edges, *payload = res[11:]
    got = exchange(*payload)
    fvx2, ux2, along2, fvy2, vy2 = call(early_kernel(1), early, [], [middle, words])
    kept = [scratch(14, 10), scratch(14), scratch(14), scratch(4), scratch(14, 15), scratch(14, 15), scratch(4, 15)]
    part, *payload = call(
        second_kernel(has_odd),
        [tiles(14, 12), tiles(14, 12), tiles(14, 9), tiles(4, 9), tiles(14, 8), tiles(28), tiles(28), tiles(5)],
        [scratch(14), scratch(14), scratch(4), scratch(14), *kept, scratch(14), pltpu.VMEM((16, LANES), jnp.float32)],
        [middle, before, fvy2, vy2, before_edges, edge_words, along2, fvx2, ux2, words]
        + [drag_ref, class_ref, low_ref, left_ref, adjoint, *got],
        aliases={0: 0, 1: 1, 2: 2, 3: 3},
    )[4:]
    got = exchange(*payload)
    grads = payload[2][4] + got[2][4]
    steps = [("gx", 2**k) for k in range(1, 32) if 2**k < nx] + [("gy", 2**k) for k in range(1, 32) if 2**k < ny]
    early_steps = len(steps) - 1
    for axis, distance in steps[:early_steps]:
        grads = add_partner(grads, axis, distance)
    _, a_ext, edges_a = call(
        third_kernel(has_odd),
        [tiles(14, 8), tiles(14, 10), tiles(14)],
        [scratch(14)],
        [part, carried_ref, drag_ref, *got],
        aliases={0: 0},
    )
    to_a, to_b, to_c, *adjoints = call(
        seam_kernel,
        [tiles(29), tiles(28), tiles(4), tiles(14), tiles(4), tiles(14, 15), tiles(14, 15), tiles(4, 15)],
        [],
        [a_ext, edges_a, ext, strip, fvy, vy, sfv, su, low_ref, left_ref, edge_words, words, grads],
    )
    sdc, sdu, gl, gh, dvy = adjoints
    got = exchange(to_a, to_b, to_c)
    grads = grads + got[0][2 * FIELDS]
    for axis, distance in steps[early_steps:]:
        grads = add_partner(grads, axis, distance)
    (part,) = call(own_kernel, [tiles(14, 8)], [], [ext, words, a_ext, fvx, ux, sdc, sdu, gl, gh, dvy])
    out, _ = call(
        last_kernel(has_odd),
        [shaped(FIELDS, LEV * ROWS, LANES), tiles(14, 8)],
        [scratch(14)],
        [part, *got],
        aliases={0: 1},
    )
    grad_scale = math.sqrt(NCLASS / (terrain.size * nx * ny * LEV))
    return (out.reshape(start_state.shape), grads[0, :NCLASS] * grad_scale)


def solution(mesh):
    placed = (
        P(None, None, "gy", "gx"),
        P(None, None, "gy", "gx"),
        P(None, None, None, "gy", "gx"),
        P("gy", "gx"),
        P(),
    )
    return jax.shard_map(
        body,
        mesh=mesh,
        in_specs=placed,
        out_specs=(P(None, None, "gy", "gx"), P()),
        check_vma=False,
    )
```

```python
import math

import jax
import jax.numpy as jnp
from jax import lax
from jax.experimental import pallas as pl
from jax.experimental.pallas import tpu as pltpu
from jax.sharding import PartitionSpec as P

LEV = 8
NCLASS = 24
FIELDS = 14
ROWS = 8
LANES = 128
PHASES = ((0, 5), (5, 3), (8, 3), (11, 3))
FACE = 0.3 * 0.5 * 0.5
COUPLING = 0.5
DRAG_STEP = 0.5
TERRAIN_SLOT = 2


def roll(v, shift):
    return pltpu.roll(v, shift % LANES if isinstance(shift, int) else shift, 1)


def lane_ids():
    return lax.broadcasted_iota(jnp.int32, (8, LANES), 1)


def strip_pos():
    return lane_ids() % 16


def strip_row():
    return lane_ids() // 16


def level_bits():
    levels = lax.broadcasted_iota(jnp.int32, (8, LANES), 0)
    return [jnp.left_shift(jnp.ones_like(levels), levels + LEV * k) for k in range(2)]


def edge_lanes():
    lanes = lane_ids()
    return (lanes < 2) | (lanes >= LANES - 2)


def spread(ref, index):
    return jnp.broadcast_to(ref[pl.ds(index, 1), :], (8, LANES))


def plane(step, direction, pair):
    return step * 4 + direction * 2 + pair


def position(axis):
    return lax.axis_index(axis), lax.axis_size(axis)


def into_slots(values):
    pos = strip_pos() // 4
    total = jnp.zeros((8, LANES), jnp.float32)
    for slot, value in enumerate(values):
        total = jnp.where(pos == slot, value, total)
    return total


def add_edges(edges_ref, values, row):
    mine = strip_row() == row
    for f, value in enumerate(values):
        edges_ref[f] = jnp.where(mine, roll(value, 16 * row + 4), edges_ref[f])


def zero_edges(edges_ref, count=FIELDS):
    for f in range(count):
        edges_ref[f] = jnp.zeros((8, LANES), edges_ref.dtype)


def edge_payload(edges_ref, out_ref):
    for g in range(4):
        fields = range(4 * g, min(4 * g + 4, FIELDS))
        out_ref[g] = into_slots([roll(edges_ref[f], 4 * (f % 4) - 2) for f in fields])


def side_payloads(even_ref, odd_ref):
    index, _ = position("gx")
    is_even = index % 2 == 0

    def pick(k):
        a = even_ref[k]
        b = jnp.zeros_like(a) if odd_ref is None else odd_ref[k]
        return jnp.where(is_even, b, a), jnp.where(is_even, a, b)

    return pick


def build_strip(edges_ref, pick, strip_ref):
    pos = strip_pos()
    for g in range(4):
        left, right = pick(g)
        for f in range(4 * g, min(4 * g + 4, FIELDS)):
            q = f % 4
            own = edges_ref[f]
            value = jnp.where(pos < 4, own, roll(right, 2 - 4 * q))
            value = jnp.where(pos < 6, value, roll(left, 6 - 4 * q))
            value = jnp.where(pos < 8, value, roll(own, 4))
            strip_ref[f] = jnp.where(pos < 12, value, 0.0)


def strip_words(edge_words_ref, left_words, which):
    pos = strip_pos()
    own = spread(edge_words_ref, which)
    left = jnp.broadcast_to(left_words[which : which + 1], (8, LANES))
    value = jnp.where(pos < 4, own, roll(own, 4))
    return jnp.where(pos == 7, roll(left, 4), value)


def strip_classes(edge_words_ref, pick):
    pos = strip_pos()
    own = spread(edge_words_ref, TERRAIN_SLOT)
    left, right = [jnp.broadcast_to(v[TERRAIN_SLOT : TERRAIN_SLOT + 1], (8, LANES)).astype(jnp.int32) for v in pick(4)]
    value = jnp.where(pos < 4, own, jnp.where(pos < 6, right, jnp.where(pos < 8, roll(left, 4), roll(own, 4))))
    return value


def face_walls():
    gx, nx = position("gx")
    pos = strip_pos()
    shut = ((pos == 7) & (gx == 0)) | ((pos == 3) & (gx == nx - 1))
    return jnp.where(shut, 0.0, FACE)


def row_wall(j):
    gy, ny = position("gy")
    shut = ((j == 0) & (gy == 0)) | ((j == ROWS) & (gy == ny - 1))
    return jnp.where(shut, 0.0, FACE)


def inverse_root(mass):
    return lax.rsqrt(mass * mass + 1.0)


def gather_edges(v):
    pos = strip_pos()
    return jnp.where((pos == 4) | (pos == 5), roll(v, -4), v)


def face_values(behind, here, ahead, beyond, flag):
    return jnp.where(flag, 3.0 * here - behind, 3.0 * ahead - beyond)


def forward_strip(step, strip, edge_words, left_words, sfv, su, sdx):
    bits = level_bits()
    walls = face_walls()
    for p, (lead, members) in enumerate(PHASES):
        word = strip_words(edge_words, left_words, plane(step, 0, p // 2))
        flag = (word & bits[p % 2]) != 0
        u = strip[lead + 1] * inverse_root(strip[lead])
        speed = walls * (u + roll(u, -1))
        su[p] = speed
        for f in range(lead, lead + members):
            c = strip[f]
            ahead = roll(c, -1)
            value = face_values(roll(c, 1), c, ahead, roll(c, -2), flag)
            sfv[f] = value
            flux = speed * value
            sdx[f] = gather_edges(flux - roll(flux, 1))


def forward_face(j, step, ext, words, low_words, fvy, vy):
    bits = level_bits()
    wall = FACE if low_words is None else row_wall(j)
    for p, (lead, members) in enumerate(PHASES):
        which = plane(step, 1, p // 2)
        word = face_word(j, words, low_words, which)
        flag = (word & bits[p % 2]) != 0
        v_low = ext[lead + 2, j + 1] * inverse_root(ext[lead, j + 1])
        v_high = ext[lead + 2, j + 2] * inverse_root(ext[lead, j + 2])
        vy[p, j] = wall * (v_low + v_high)
        for f in range(lead, lead + members):
            fvy[f, j] = face_values(ext[f, j], ext[f, j + 1], ext[f, j + 2], ext[f, j + 3], flag)


def face_word(j, words, low_words, which):
    if low_words is None:
        return spread(words, which * ROWS + j - 1)
    here = spread(words, which * ROWS + jnp.maximum(j - 1, 0))
    low = jnp.broadcast_to(low_words[which : which + 1], (8, LANES))
    return jnp.where(j == 0, low, here)


def carried_row(r, edges, ext, sdx, along, fvy, vy):
    carried = []
    for p, (lead, members) in enumerate(PHASES):
        below, above = vy[p, r], vy[p, r + 1]
        for f in range(lead, lead + members):
            seam = ext[f, r + 2] - roll(sdx[f], 124 - 16 * r)
            along_y = above * fvy[f, r + 1] - below * fvy[f, r]
            carried.append(jnp.where(edges, seam, along[f, r]) - along_y)
    return carried


def early_kernel(step):
    def kernel(ext, words, *refs):
        fvx, ux, along, fvy, vy = refs[-6:-1] if step == 0 else refs
        bits = level_bits()
        if step == 0:
            coef, coef_rows = refs[0], refs[-1]
            for k in range(NCLASS):
                coef_rows[pl.ds(k, 1), :] = jnp.full((1, LANES), coef[k], jnp.float32)

        def one_row(r, carry):
            for p, (lead, members) in enumerate(PHASES):
                word = spread(words, plane(step, 0, p // 2) * ROWS + r)
                flag = (word & bits[p % 2]) != 0
                u = ext[lead + 1, r + 2] * inverse_root(ext[lead, r + 2])
                speed = FACE * (u + roll(u, -1))
                ux[p, r] = speed
                for f in range(lead, lead + members):
                    c = ext[f, r + 2]
                    value = face_values(roll(c, 1), c, roll(c, -1), roll(c, -2), flag)
                    fvx[f, r] = value
                    flux = speed * value
                    along[f, r] = c - (flux - roll(flux, 1))
            return carry

        lax.fori_loop(0, ROWS, one_row, 0, unroll=2)
        for j in range(2, ROWS - 1):
            forward_face(j, step, ext, words, None, fvy, vy)

    return kernel


def outer_faces(step, ext, words, low_words, fvy, vy):
    for j in (0, 1, ROWS - 1, ROWS):
        forward_face(j, step, ext, words, low_words, fvy, vy)


def coupled(c):
    s = inverse_root(c[0])
    u, v = c[1] * s, c[2] * s
    gas_x, gas_y = c[1], c[2]
    out = [None] * FIELDS
    for lead, _ in PHASES[1:]:
        pull_x = COUPLING * (c[lead] * u - c[lead + 1])
        pull_y = COUPLING * (c[lead] * v - c[lead + 2])
        gas_x, gas_y = gas_x - pull_x, gas_y - pull_y
        out[lead] = c[lead]
        out[lead + 1], out[lead + 2] = c[lead + 1] + pull_x, c[lead + 2] + pull_y
    out[0], out[1], out[2], out[3], out[4] = c[0], gas_x, gas_y, c[3], c[4]
    return out, s, u, v


def dragged(q, drag):
    q = list(q)
    for lead, _ in PHASES:
        s = inverse_root(q[lead])
        u, v = q[lead + 1] * s, q[lead + 2] * s
        factor = 1.0 - drag * jnp.sqrt(u * u + v * v + 1.0)
        q[lead + 1], q[lead + 2] = q[lead + 1] * factor, q[lead + 2] * factor
    return q


def drag_terms(q, a):
    total = None
    for lead, _ in PHASES:
        s = inverse_root(q(lead))
        x, y = q(lead + 1), q(lead + 2)
        u, v = x * s, y * s
        term = jnp.sqrt(u * u + v * v + 1.0) * (a[lead + 1] * x + a[lead + 2] * y)
        total = term if total is None else total + term
    return -total


def stepped_back(c, drag, a, want_terms):
    q, s0, gas_u, gas_v = coupled(c)
    a = list(a)
    terms = jnp.zeros((8, LANES), jnp.float32)
    for lead, _ in PHASES:
        m, x, y = q[lead], q[lead + 1], q[lead + 2]
        s = s0 if lead == 0 else inverse_root(m)
        u, v = x * s, y * s
        energy = u * u + v * v
        root = lax.rsqrt(energy + 1.0)
        w = (energy + 1.0) * root
        dot = a[lead + 1] * x + a[lead + 2] * y
        if want_terms:
            terms = terms - w * dot
        k = drag * dot * root
        factor = 1.0 - drag * w
        ks = k * s
        a[lead + 1] = a[lead + 1] * factor - ks * u
        a[lead + 2] = a[lead + 2] * factor - ks * v
        a[lead] = a[lead] + k * energy * m * (s * s)
    du = jnp.zeros((8, LANES), jnp.float32)
    dv = jnp.zeros((8, LANES), jnp.float32)
    for lead, _ in PHASES[1:]:
        rx, ry = COUPLING * (a[lead + 1] - a[1]), COUPLING * (a[lead + 2] - a[2])
        a[lead] = a[lead] + rx * gas_u + ry * gas_v
        du, dv = du + c[lead] * rx, dv + c[lead] * ry
        a[lead + 1], a[lead + 2] = a[lead + 1] - rx, a[lead + 2] - ry
    a[1], a[2] = a[1] + du * s0, a[2] + dv * s0
    a[0] = a[0] - (gas_u * du + gas_v * dv) * c[0] * (s0 * s0)
    return a, terms


def add_speed_terms(total, state, lead, du, dv):
    m, x, y = state
    s = inverse_root(m)
    pull = None
    if du is not None:
        total[lead + 1] = total[lead + 1] + s * du
        pull = x * s * du
    if dv is not None:
        total[lead + 2] = total[lead + 2] + s * dv
        pull = y * s * dv if pull is None else pull + y * s * dv
    total[lead] = total[lead] - pull * m * (s * s)


def scatter_x(a, value, speed, flag):
    ahead = roll(a, -1) - a
    g = speed * ahead
    low = jnp.where(flag, g, 0.0)
    high = roll(g - low, 1)
    return 3.0 * (low + high) - roll(low, -1) - roll(high, 1), value * ahead


def expand_edges(own):
    pos = strip_pos()
    value = jnp.where(pos < 4, own, jnp.where((pos >= 8) & (pos < 12), roll(own, 4), 0.0))
    return value


def backward_strip(step, strip, edges_a, edge_words, left_words, sfv, su, sdc, sdu, out_c):
    bits = level_bits()
    walls = face_walls()
    ghosts = []
    for p, (lead, members) in enumerate(PHASES):
        word = strip_words(edge_words, left_words, plane(step, 0, p // 2))
        flag = (word & bits[p % 2]) != 0
        speed = su[p]
        du = jnp.zeros((8, LANES), jnp.float32)
        total = {}
        for f in range(lead, lead + members):
            total[f], term = scatter_x(expand_edges(edges_a[f]), sfv[f], speed, flag)
            sdc[f] = gather_edges(total[f])
            du = du + term
        du = walls * du
        du = du + roll(du, 1)
        sdu[p] = gather_edges(du)
        add_speed_terms(total, (strip[lead], strip[lead + 1], strip[lead + 2]), lead, du, None)
        ghosts.extend(total[f] for f in range(lead, lead + members))
    for g in range(4):
        fields = range(4 * g, min(4 * g + 4, FIELDS))
        out_c[g] = into_slots([roll(ghosts[f], 4 * (f % 4) - 4) for f in fields])
    return ghosts


def backward_faces(step, ext, words, low_words, a_ext, fvy, vy, gl, gh, dvy, put):
    bits = level_bits()
    zero = jnp.zeros((8, LANES), jnp.float32)
    for k in (0, 1, 2, 12, 13, 14):
        for f in range(FIELDS):
            gl[f, k] = zero
            gh[f, k] = zero
        for p in range(4):
            dvy[p, k] = zero

    def face(j, carry):
        wall = row_wall(j)
        for p, (lead, members) in enumerate(PHASES):
            word = face_word(j, words, low_words, plane(step, 1, p // 2))
            flag = (word & bits[p % 2]) != 0
            speed = vy[p, j]
            dv = jnp.zeros((8, LANES), jnp.float32)
            for f in range(lead, lead + members):
                ahead = a_ext[f, j + 1] - a_ext[f, j]
                g = speed * ahead
                low = jnp.where(flag, g, 0.0)
                gl[f, j + 3] = low
                gh[f, j + 3] = g - low
                dv = dv + fvy[f, j] * ahead
            dvy[p, j + 3] = wall * dv
        return carry

    lax.fori_loop(0, ROWS + 1, face, 0, unroll=9)
    for i in (-2, -1, ROWS, ROWS + 1):
        total = [transposed_y(gl, gh, f, i) for f in range(FIELDS)]
        for p, (lead, members) in enumerate(PHASES):
            dv = dvy[p, i + 4] + dvy[p, i + 3]
            state = (ext[lead, i + 2], ext[lead + 1, i + 2], ext[lead + 2, i + 2])
            add_speed_terms(total, state, lead, None, dv)
        put(i, total)


def transposed_y(gl, gh, f, i):
    return 3.0 * (gl[f, i + 4] + gh[f, i + 3]) - gl[f, i + 5] - gh[f, i + 2]


def backward_own(step, ext, words, a_ext, fvx, ux, sdc, sdu, gl, gh, dvy, put):
    bits = level_bits()
    edges = edge_lanes()

    def own(r, carry):
        total = [None] * FIELDS
        for p, (lead, members) in enumerate(PHASES):
            word = spread(words, plane(step, 0, p // 2) * ROWS + r)
            flag = (word & bits[p % 2]) != 0
            speed = ux[p, r]
            du = jnp.zeros((8, LANES), jnp.float32)
            for f in range(lead, lead + members):
                a = a_ext[f, r + 1]
                part, term = scatter_x(a, fvx[f, r], speed, flag)
                part = jnp.where(edges, roll(sdc[f], 124 - 16 * r), part)
                total[f] = a + part + transposed_y(gl, gh, f, r)
                du = du + term
            du = FACE * (du + roll(du, 1))
            du = jnp.where(edges, roll(sdu[p], 124 - 16 * r), du)
            dv = dvy[p, r + 4] + dvy[p, r + 3]
            state = (ext[lead, r + 2], ext[lead + 1, r + 2], ext[lead + 2, r + 2])
            add_speed_terms(total, state, lead, du, dv)
        put(r, total)
        return carry

    lax.fori_loop(0, ROWS, own, 0, unroll=2)


def level_weight():
    levels = lax.broadcasted_iota(jnp.int32, (8, LANES), 0)
    weight = jnp.full((8, LANES), DRAG_STEP, jnp.float32)
    for k in range(3):
        weight = jnp.where((levels // 2**k) % 2 == 1, weight * 0.5 ** (2**k), weight)
    return weight


def drag_table(classes, coef_rows):
    drag = jnp.zeros(classes.shape, jnp.float32)
    for k in range(NCLASS):
        drag = jnp.where(classes == k, jnp.broadcast_to(coef_rows[pl.ds(k, 1), :], classes.shape), drag)
    return drag


def level_sum(v):
    return jnp.sum(v, axis=0, keepdims=True)


def row_bases():
    gy, _ = position("gy")
    is_even = gy % 2 == 0
    return is_even


def fill_ghost_rows(ext, from_a, from_b):
    is_even = row_bases()
    a_row = jnp.where(is_even, ROWS + 2, 0)
    b_row = jnp.where(is_even, 0, ROWS + 2)
    for f in range(FIELDS):
        for j in range(2):
            ext[f, a_row + j] = from_a[2 * f + j]
            ext[f, b_row + j] = from_b[2 * f + j]


def put_edge_rows(source, offset, to_a, to_b):
    is_even = row_bases()
    a_row = jnp.where(is_even, ROWS - 2, 0) + offset
    b_row = jnp.where(is_even, 0, ROWS - 2) + offset
    for f in range(FIELDS):
        for j in range(2):
            to_a[2 * f + j] = source[f, a_row + j]
            to_b[2 * f + j] = source[f, b_row + j]


def pack_kernel(start_in, words_in, terrain_in, words, terrain, ext, edges, edge_words, to_a, to_b, to_c, start, sems):
    copies = [
        pltpu.make_async_copy(source, target, sems.at[k])
        for k, (source, target) in enumerate(((start_in, start), (words_in, words), (terrain_in, terrain)))
    ]
    for copy in copies:
        copy.start()
    zero_edges(edges)
    edge_words[...] = jnp.zeros((8, LANES), jnp.int32)
    slots = lax.broadcasted_iota(jnp.int32, (8, LANES), 0)
    for copy in copies:
        copy.wait()

    def one_row(r, carry):
        values = [start[f, pl.ds(r, 8, stride=8), :] for f in range(FIELDS)]
        for f in range(FIELDS):
            ext[f, r + 2] = values[f]
        add_edges(edges, values, r)
        mine = strip_row() == r
        row_words = jnp.where(slots == TERRAIN_SLOT, spread(terrain, r), words[pl.ds(r, 8, stride=8), :])
        edge_words[...] = jnp.where(mine, roll(row_words, (16 * r + 4) % LANES), edge_words[...])
        return carry

    lax.fori_loop(0, ROWS, one_row, 0, unroll=8)
    put_edge_rows(ext, 2, to_a, to_b)
    top = words[pl.ds(ROWS - 1, 8, stride=8), :]
    is_even = row_bases()
    a_row = jnp.where(is_even, ROWS - 2, 0)
    for target, row in ((to_a, a_row), (to_b, ROWS - 2 - a_row)):
        mixed = jnp.where(slots == 0, spread(terrain, row), jnp.where(slots == 1, spread(terrain, row + 1), top))
        target[2 * FIELDS] = mixed.astype(jnp.float32)
    edge_payload(edges, to_c)
    to_c[4] = edge_words[...].astype(jnp.float32)


def neighbour_words(from_a, from_b, pick):
    low = jnp.where(row_bases(), from_b[2 * FIELDS], from_a[2 * FIELDS]).astype(jnp.int32)
    left, _ = pick(4)
    return low, left.astype(jnp.int32)


def first_kernel(has_odd):
    def kernel(*refs):
        (_, _, _, edges, edge_words, along, words, terrain, coef, from_a, from_b, from_c) = refs[:12]
        from_d = refs[12] if has_odd else None
        outs = refs[12 + has_odd :]
        (ext, fvy, vy, strip, carried_ref, sfv, su, drag_ref, class_ref, low_ref, left_ref) = outs[:11]
        middle, before, before_edges, to_a, to_b, to_c = outs[11:17]
        (sdx,) = outs[17:]
        pick = side_payloads(from_c, from_d)
        fill_ghost_rows(ext, from_a, from_b)
        build_strip(edges, pick, strip)
        low_words, left_words = neighbour_words(from_a, from_b, pick)
        low_ref[...] = low_words
        left_ref[...] = left_words
        is_even = row_bases()
        a_row = jnp.where(is_even, ROWS + 2, 0)
        class_ref[pl.ds(2, ROWS), :] = terrain[...]
        for source, row in ((from_a, a_row), (from_b, ROWS + 2 - a_row)):
            for j in range(2):
                class_ref[pl.ds(row + j, 1), :] = source[2 * FIELDS, pl.ds(j, 1), :].astype(jnp.int32)
        class_ref[pl.ds(12, 4), :] = strip_classes(edge_words, pick)[:4]
        drag_ref[...] = drag_table(class_ref[...], coef)
        forward_strip(0, strip, edge_words, left_words, sfv, su, sdx)
        outer_faces(0, ext, words, low_words, fvy, vy)
        zero_edges(before_edges)
        weight = level_weight()
        seams = edge_lanes()

        def one_row(r, carry):
            c = carried_row(r, seams, ext, sdx, along, fvy, vy)
            for f in range(FIELDS):
                carried_ref[f, r] = c[f]
            q = coupled(c)[0]
            for f in range(FIELDS):
                before[f, r + 2] = q[f]
            add_edges(before_edges, q, r)
            q = dragged(q, weight * spread(drag_ref, r + 2))
            for f in range(FIELDS):
                middle[f, r + 2] = q[f]
            return carry

        lax.fori_loop(0, ROWS, one_row, 0, unroll=2)
        put_edge_rows(before, 2, to_a, to_b)
        edge_payload(before_edges, to_c)

    return kernel


def put_ghost_rows(values, row, to_a, to_b):
    is_even = row_bases()
    j = row % 2
    above = row >= ROWS

    @pl.when(is_even if above else jnp.logical_not(is_even))
    def _():
        for f in range(FIELDS):
            to_a[2 * f + j] = values[f]

    @pl.when(jnp.logical_not(is_even) if above else is_even)
    def _():
        for f in range(FIELDS):
            to_b[2 * f + j] = values[f]


def second_kernel(has_odd):
    def kernel(*refs):
        (_, _, _, _, before_edges, edge_words, along, fvx, ux, words) = refs[:10]
        (drag_ref, class_ref, low_ref, left_ref, adjoint, from_a, from_b, from_c) = refs[10:18]
        from_d = refs[18] if has_odd else None
        outs = refs[18 + has_odd :]
        ext, before, fvy, vy, part, to_a, to_b, to_c = outs[:8]
        (strip, sfv, su, sdx, a_ext, edges_a, sdc, sdu, gl, gh, dvy, before_strip, cells) = outs[8:]
        pick = side_payloads(from_c, from_d)
        low_words, left_words = low_ref[...], left_ref[...]
        weight = level_weight()
        fill_ghost_rows(before, from_a, from_b)
        for row in (0, 1, ROWS + 2, ROWS + 3):
            q = dragged([before[f, row] for f in range(FIELDS)], weight * spread(drag_ref, row))
            for f in range(FIELDS):
                ext[f, row] = q[f]
        build_strip(before_edges, pick, before_strip)
        q = dragged([before_strip[f] for f in range(FIELDS)], weight * spread(drag_ref, 12))
        for f in range(FIELDS):
            strip[f] = q[f]
        forward_strip(1, strip, edge_words, left_words, sfv, su, sdx)
        outer_faces(1, ext, words, low_words, fvy, vy)
        zero_edges(edges_a)
        for f in range(FIELDS):
            a_ext[f, 0] = jnp.zeros((8, LANES), jnp.float32)
            a_ext[f, ROWS + 1] = jnp.zeros((8, LANES), jnp.float32)
        cells[...] = jnp.zeros((16, LANES), jnp.float32)
        seams = edge_lanes()

        def one_row(r, carry):
            c = carried_row(r, seams, ext, sdx, along, fvy, vy)
            a = [adjoint[f, pl.ds(r, 8, stride=8), :] for f in range(FIELDS)]
            a, terms = stepped_back(c, weight * spread(drag_ref, r + 2), a, True)
            cells[pl.ds(r + 2, 1), :] = level_sum(weight * terms)
            for f in range(FIELDS):
                a_ext[f, r + 1] = a[f]
            add_edges(edges_a, a, r)
            return carry

        lax.fori_loop(0, ROWS, one_row, 0, unroll=2)
        ghosts = backward_strip(1, strip, edges_a, edge_words, left_words, sfv, su, sdc, sdu, to_c)
        pos = strip_pos()
        terms = jnp.where((pos >= 4) & (pos < 8), drag_terms(lambda f: before_strip[f], ghosts), 0.0)
        cells[pl.ds(12, 1), :] = level_sum(weight * terms)

        def put_terms(row, values):
            terms = drag_terms(lambda f: before[f, row + 2], values)
            at = pl.ds(row + 2, 1)
            cells[at, :] = cells[at, :] + level_sum(weight * terms)

        def put_ghost(row, values):
            put_ghost_rows(values, row, to_a, to_b)
            put_terms(row, values)

        def put_own(row, values):
            for f in range(FIELDS):
                part[f, row] = values[f]
            put_terms(row, values)

        backward_faces(1, ext, words, low_words, a_ext, fvy, vy, gl, gh, dvy, put_ghost)
        backward_own(1, ext, words, a_ext, fvx, ux, sdc, sdu, gl, gh, dvy, put_own)
        to_c[4] = binned(class_ref[...], cells[...])

    return kernel


def binned(classes, cells):
    lanes = lane_ids()
    slots = lax.broadcasted_iota(jnp.int32, (8, LANES), 0)
    total = jnp.zeros((8, LANES), jnp.float32)
    for first in range(0, NCLASS, 8):
        block = jnp.zeros((8, LANES), jnp.float32)
        for k in range(first, min(first + 8, NCLASS)):
            block = jnp.where(slots == k - first, level_sum(jnp.where(classes == k, cells, 0.0)), block)
        block = jnp.sum(block, axis=1, keepdims=True)
        total = jnp.where(lanes == first + slots, block, total)
    return jnp.broadcast_to(level_sum(total), (8, LANES))


def collect(part, from_a, from_b, pick, incoming):
    is_even = row_bases()
    a_row = jnp.where(is_even, ROWS - 2, 0)
    b_row = ROWS - 2 - a_row
    for f in range(FIELDS):
        for j in range(2):
            part[f, a_row + j] = part[f, a_row + j] + from_a[2 * f + j]
            part[f, b_row + j] = part[f, b_row + j] + from_b[2 * f + j]
    pos = strip_pos()
    at_left = (pos == 4) | (pos == 5)
    at_right = (pos == 2) | (pos == 3)
    for g in range(4):
        left, right = pick(g)
        for f in range(4 * g, min(4 * g + 4, FIELDS)):
            q = f % 4
            incoming[f] = jnp.where(at_left, roll(left, 4 - 4 * q), jnp.where(at_right, roll(right, -4 * q), 0.0))


def third_kernel(has_odd):
    def kernel(*refs):
        _, carried_ref, drag_ref, from_a, from_b, from_c = refs[:6]
        from_d = refs[6] if has_odd else None
        part, a_ext, edges_a, incoming = refs[6 + has_odd :]
        pick = side_payloads(from_c, from_d)
        collect(part, from_a, from_b, pick, incoming)
        zero_edges(edges_a)
        for f in range(FIELDS):
            a_ext[f, 0] = jnp.zeros((8, LANES), jnp.float32)
            a_ext[f, ROWS + 1] = jnp.zeros((8, LANES), jnp.float32)
        edges = edge_lanes()
        weight = level_weight()

        def one_row(r, carry):
            c = [carried_ref[f, r] for f in range(FIELDS)]
            a = [part[f, r] + jnp.where(edges, roll(incoming[f], 124 - 16 * r), 0.0) for f in range(FIELDS)]
            a, _ = stepped_back(c, weight * spread(drag_ref, r + 2), a, False)
            for f in range(FIELDS):
                a_ext[f, r + 1] = a[f]
            add_edges(edges_a, a, r)
            return carry

        lax.fori_loop(0, ROWS, one_row, 0, unroll=4)

    return kernel


def seam_kernel(a_ext, edges_a, ext, strip, fvy, vy, sfv, su, *refs):
    low_ref, left_ref, edge_words, words, grads, arriving, *outs = refs
    to_a, to_b, to_c, sdc, sdu, gl, gh, dvy = outs
    low_words, left_words = low_ref[...], left_ref[...]
    backward_strip(0, strip, edges_a, edge_words, left_words, sfv, su, sdc, sdu, to_c)

    def put_ghost(row, values):
        put_ghost_rows(values, row, to_a, to_b)

    backward_faces(0, ext, words, low_words, a_ext, fvy, vy, gl, gh, dvy, put_ghost)
    to_a[2 * FIELDS] = grads[...] + arriving[...]


def own_kernel(ext, words, a_ext, fvx, ux, sdc, sdu, gl, gh, dvy, part):
    def put(row, values):
        for f in range(FIELDS):
            part[f, row] = values[f]

    backward_own(0, ext, words, a_ext, fvx, ux, sdc, sdu, gl, gh, dvy, put)


def last_kernel(has_odd):
    def kernel(*refs):
        _, from_a, from_b, from_c = refs[:4]
        from_d = refs[4] if has_odd else None
        out, part, incoming = refs[4 + has_odd :]
        pick = side_payloads(from_c, from_d)
        collect(part, from_a, from_b, pick, incoming)
        edges = edge_lanes()

        def one_row(r, carry):
            for f in range(FIELDS):
                value = part[f, r] + jnp.where(edges, roll(incoming[f], (124 - 16 * r) % LANES), 0.0)
                out[f, pl.ds(r, 8, stride=8), :] = value
            return carry

        lax.fori_loop(0, ROWS, one_row, 0, unroll=8)

    return kernel


def shaped(*shape, dtype=jnp.float32):
    return jax.ShapeDtypeStruct(shape, dtype)


def tiles(*shape, dtype=jnp.float32):
    return shaped(*shape, 8, LANES, dtype=dtype)


def scratch(*shape, dtype=jnp.float32):
    return pltpu.VMEM((*shape, 8, LANES), dtype)


def call(kernel, outs, scratches, args, smem=(), hbm=(), aliases=None):
    def space(k):
        return pltpu.SMEM if k in smem else pltpu.HBM if k in hbm else pltpu.VMEM

    return pl.pallas_call(
        kernel,
        out_shape=outs,
        in_specs=[pl.BlockSpec(memory_space=space(k)) for k in range(len(args))],
        out_specs=[pl.BlockSpec(memory_space=pltpu.VMEM)] * len(outs),
        scratch_shapes=scratches,
        input_output_aliases=aliases or {},
        compiler_params=pltpu.CompilerParams(vmem_limit_bytes=32 << 20),
    )(*args)


def swap(x, axis, first):
    peers = lax.axis_size(axis)
    pairs = [(i, i + 1) for i in range(first, peers - 1, 2)]
    if not pairs:
        return None
    return lax.ppermute(x, axis, pairs + [(j, i) for i, j in pairs])


def exchange(to_a, to_b, to_c):
    from_a = swap(to_a, "gy", 0)
    from_b = swap(to_b, "gy", 1)
    from_c = swap(to_c, "gx", 0)
    from_d = swap(to_c, "gx", 1)
    if from_b is None:
        from_b = jnp.zeros_like(to_b)
    return (from_a, from_b, from_c) + (() if from_d is None else (from_d,))


def from_partner(x, axis, distance):
    return lax.ppermute(x, axis, [(i, i ^ distance) for i in range(lax.axis_size(axis))])


def add_partner(x, axis, distance):
    return x + from_partner(x, axis, distance)


def body(start_state, final_adjoint, face_words, terrain, drag_coef):
    nx, ny = lax.axis_size("gx"), lax.axis_size("gy")
    has_odd = nx > 2
    start = start_state.reshape(FIELDS, LEV * ROWS, LANES)
    adjoint = final_adjoint.reshape(FIELDS, LEV * ROWS, LANES)
    words = face_words.reshape(8 * ROWS, LANES)
    ints = jnp.int32

    words, terrain, ext, edges, edge_words, *payload = call(
        pack_kernel,
        [shaped(*words.shape, dtype=ints), shaped(*terrain.shape, dtype=ints)]
        + [tiles(14, 12), tiles(14), tiles(dtype=ints), tiles(29), tiles(29), tiles(5)],
        [
            pltpu.VMEM(start.shape, jnp.float32),
            pltpu.SemaphoreType.DMA((3,)),
        ],
        [pltpu.with_memory_space_constraint(x, pltpu.HBM) for x in (start, words, terrain)],
        hbm=(0, 1, 2),
    )
    got = exchange(*payload)
    early = [tiles(14, 8), tiles(4, 8), tiles(14, 8), tiles(14, 9), tiles(4, 9)]
    fvx, ux, along, fvy, vy, coef_rows = call(
        early_kernel(0), [*early, shaped(NCLASS, LANES)], [], [ext, words, drag_coef], smem=(2,)
    )
    res = call(
        first_kernel(has_odd),
        [tiles(14, 12), tiles(14, 9), tiles(4, 9), tiles(14), tiles(14, 8), tiles(14), tiles(4)]
        + [shaped(16, LANES), shaped(16, LANES, dtype=ints), tiles(dtype=ints), tiles(dtype=ints)]
        + [tiles(14, 12), tiles(14, 12), tiles(14), tiles(28), tiles(28), tiles(4)],
        [scratch(14)],
        [ext, fvy, vy, edges, edge_words, along, words, terrain, coef_rows, *got],
        aliases={0: 0, 1: 1, 2: 2},
    )
    ext, fvy, vy, strip, carried_ref, sfv, su, drag_ref, class_ref, low_ref, left_ref = res[:11]
    middle, before, before_edges, *payload = res[11:]
    got = exchange(*payload)
    fvx2, ux2, along2, fvy2, vy2 = call(early_kernel(1), early, [], [middle, words])
    kept = [scratch(14, 10), scratch(14), scratch(14), scratch(4), scratch(14, 15), scratch(14, 15), scratch(4, 15)]
    part, *payload = call(
        second_kernel(has_odd),
        [tiles(14, 12), tiles(14, 12), tiles(14, 9), tiles(4, 9), tiles(14, 8), tiles(28), tiles(28), tiles(5)],
        [scratch(14), scratch(14), scratch(4), scratch(14), *kept, scratch(14), pltpu.VMEM((16, LANES), jnp.float32)],
        [middle, before, fvy2, vy2, before_edges, edge_words, along2, fvx2, ux2, words]
        + [drag_ref, class_ref, low_ref, left_ref, adjoint, *got],
        aliases={0: 0, 1: 1, 2: 2, 3: 3},
    )[4:]
    got = exchange(*payload)
    grads = payload[2][4] + got[2][4]
    steps = [("gx", 2**k) for k in range(1, 32) if 2**k < nx] + [("gy", 2**k) for k in range(1, 32) if 2**k < ny]
    steps = steps[::-1]
    early_steps = 1
    for axis, distance in steps[: early_steps - 1]:
        grads = add_partner(grads, axis, distance)
    arriving = from_partner(grads, *steps[early_steps - 1])
    _, a_ext, edges_a = call(
        third_kernel(has_odd),
        [tiles(14, 8), tiles(14, 10), tiles(14)],
        [scratch(14)],
        [part, carried_ref, drag_ref, *got],
        aliases={0: 0},
    )
    to_a, to_b, to_c, *adjoints = call(
        seam_kernel,
        [tiles(29), tiles(28), tiles(4), tiles(14), tiles(4), tiles(14, 15), tiles(14, 15), tiles(4, 15)],
        [],
        [a_ext, edges_a, ext, strip, fvy, vy, sfv, su, low_ref, left_ref, edge_words, words, grads, arriving],
    )
    sdc, sdu, gl, gh, dvy = adjoints
    got = exchange(to_a, to_b, to_c)
    grads = to_a[2 * FIELDS] + got[0][2 * FIELDS]
    for axis, distance in steps[early_steps:]:
        grads = add_partner(grads, axis, distance)
    (part,) = call(own_kernel, [tiles(14, 8)], [], [ext, words, a_ext, fvx, ux, sdc, sdu, gl, gh, dvy])
    out, _ = call(
        last_kernel(has_odd),
        [shaped(FIELDS, LEV * ROWS, LANES), tiles(14, 8)],
        [scratch(14)],
        [part, *got],
        aliases={0: 1},
    )
    grad_scale = math.sqrt(NCLASS / (terrain.size * nx * ny * LEV))
    return (out.reshape(start_state.shape), grads[0, :NCLASS] * grad_scale)


def solution(mesh):
    placed = (
        P(None, None, "gy", "gx"),
        P(None, None, "gy", "gx"),
        P(None, None, None, "gy", "gx"),
        P("gy", "gx"),
        P(),
    )
    return jax.shard_map(
        body,
        mesh=mesh,
        in_specs=placed,
        out_specs=(P(None, None, "gy", "gx"), P()),
        check_vma=False,
    )
```

```python
import math

import jax
import jax.numpy as jnp
from jax import lax
from jax.experimental import pallas as pl
from jax.experimental.pallas import tpu as pltpu
from jax.sharding import PartitionSpec as P

LEV = 8
NCLASS = 24
FIELDS = 14
ROWS = 8
LANES = 128
HALVES = (range(7), range(7, FIELDS))
PHASES = ((0, 5), (5, 3), (8, 3), (11, 3))
FACE = 0.3 * 0.5 * 0.5
COUPLING = 0.5
DRAG_STEP = 0.5
TERRAIN_SLOT = 2


def roll(v, shift):
    return pltpu.roll(v, shift % LANES if isinstance(shift, int) else shift, 1)


def lane_ids():
    return lax.broadcasted_iota(jnp.int32, (8, LANES), 1)


def strip_pos():
    return lane_ids() % 16


def strip_row():
    return lane_ids() // 16


def level_bits():
    levels = lax.broadcasted_iota(jnp.int32, (8, LANES), 0)
    return [jnp.left_shift(jnp.ones_like(levels), levels + LEV * k) for k in range(2)]


def edge_lanes():
    lanes = lane_ids()
    return (lanes < 2) | (lanes >= LANES - 2)


def spread(ref, index):
    return jnp.broadcast_to(ref[pl.ds(index, 1), :], (8, LANES))


def plane(step, direction, pair):
    return step * 4 + direction * 2 + pair


def position(axis):
    return lax.axis_index(axis), lax.axis_size(axis)


def into_slots(values):
    pos = strip_pos() // 4
    total = jnp.zeros((8, LANES), jnp.float32)
    for slot, value in enumerate(values):
        total = jnp.where(pos == slot, value, total)
    return total


def add_edges(edges_ref, values, row):
    mine = strip_row() == row
    for f, value in enumerate(values):
        edges_ref[f] = jnp.where(mine, roll(value, 16 * row + 4), edges_ref[f])


def zero_edges(edges_ref, count=FIELDS):
    for f in range(count):
        edges_ref[f] = jnp.zeros((8, LANES), edges_ref.dtype)


def edge_payload(edges_ref, out_ref):
    for g in range(4):
        fields = range(4 * g, min(4 * g + 4, FIELDS))
        out_ref[g] = into_slots([roll(edges_ref[f], 4 * (f % 4) - 2) for f in fields])


def side_payloads(even_ref, odd_ref):
    index, _ = position("gx")
    is_even = index % 2 == 0

    def pick(k):
        a = even_ref[k]
        b = jnp.zeros_like(a) if odd_ref is None else odd_ref[k]
        return jnp.where(is_even, b, a), jnp.where(is_even, a, b)

    return pick


def build_strip(edges_ref, pick, strip_ref):
    pos = strip_pos()
    for g in range(4):
        left, right = pick(g)
        for f in range(4 * g, min(4 * g + 4, FIELDS)):
            q = f % 4
            own = edges_ref[f]
            value = jnp.where(pos < 4, own, roll(right, 2 - 4 * q))
            value = jnp.where(pos < 6, value, roll(left, 6 - 4 * q))
            value = jnp.where(pos < 8, value, roll(own, 4))
            strip_ref[f] = jnp.where(pos < 12, value, 0.0)


def strip_words(edge_words_ref, left_words, which):
    pos = strip_pos()
    own = spread(edge_words_ref, which)
    left = jnp.broadcast_to(left_words[which : which + 1], (8, LANES))
    value = jnp.where(pos < 4, own, roll(own, 4))
    return jnp.where(pos == 7, roll(left, 4), value)


def strip_classes(edge_words_ref, pick):
    pos = strip_pos()
    own = spread(edge_words_ref, TERRAIN_SLOT)
    left, right = [jnp.broadcast_to(v[TERRAIN_SLOT : TERRAIN_SLOT + 1], (8, LANES)).astype(jnp.int32) for v in pick(4)]
    value = jnp.where(pos < 4, own, jnp.where(pos < 6, right, jnp.where(pos < 8, roll(left, 4), roll(own, 4))))
    return value


def face_walls():
    gx, nx = position("gx")
    pos = strip_pos()
    shut = ((pos == 7) & (gx == 0)) | ((pos == 3) & (gx == nx - 1))
    return jnp.where(shut, 0.0, FACE)


def row_wall(j):
    gy, ny = position("gy")
    shut = ((j == 0) & (gy == 0)) | ((j == ROWS) & (gy == ny - 1))
    return jnp.where(shut, 0.0, FACE)


def inverse_root(mass):
    return lax.rsqrt(mass * mass + 1.0)


def gather_edges(v):
    pos = strip_pos()
    return jnp.where((pos == 4) | (pos == 5), roll(v, -4), v)


def face_values(behind, here, ahead, beyond, flag):
    return jnp.where(flag, 3.0 * here - behind, 3.0 * ahead - beyond)


def forward_strip(step, strip, edge_words, left_words, sfv, su, sdx):
    bits = level_bits()
    walls = face_walls()
    for p, (lead, members) in enumerate(PHASES):
        word = strip_words(edge_words, left_words, plane(step, 0, p // 2))
        flag = (word & bits[p % 2]) != 0
        u = strip[lead + 1] * inverse_root(strip[lead])
        speed = walls * (u + roll(u, -1))
        su[p] = speed
        for f in range(lead, lead + members):
            c = strip[f]
            ahead = roll(c, -1)
            value = face_values(roll(c, 1), c, ahead, roll(c, -2), flag)
            sfv[f] = value
            flux = speed * value
            sdx[f] = gather_edges(flux - roll(flux, 1))


def forward_face(j, step, ext, words, low_words, fvy, vy):
    bits = level_bits()
    wall = FACE if low_words is None else row_wall(j)
    for p, (lead, members) in enumerate(PHASES):
        which = plane(step, 1, p // 2)
        word = face_word(j, words, low_words, which)
        flag = (word & bits[p % 2]) != 0
        v_low = ext[lead + 2, j + 1] * inverse_root(ext[lead, j + 1])
        v_high = ext[lead + 2, j + 2] * inverse_root(ext[lead, j + 2])
        vy[p, j] = wall * (v_low + v_high)
        for f in range(lead, lead + members):
            fvy[f, j] = face_values(ext[f, j], ext[f, j + 1], ext[f, j + 2], ext[f, j + 3], flag)


def face_word(j, words, low_words, which):
    if low_words is None:
        return spread(words, which * ROWS + j - 1)
    here = spread(words, which * ROWS + jnp.maximum(j - 1, 0))
    low = jnp.broadcast_to(low_words[which : which + 1], (8, LANES))
    return jnp.where(j == 0, low, here)


def carried_row(r, edges, ext, sdx, along, fvy, vy):
    carried = []
    for p, (lead, members) in enumerate(PHASES):
        below, above = vy[p, r], vy[p, r + 1]
        for f in range(lead, lead + members):
            seam = ext[f, r + 2] - roll(sdx[f], 124 - 16 * r)
            along_y = above * fvy[f, r + 1] - below * fvy[f, r]
            carried.append(jnp.where(edges, seam, along[f, r]) - along_y)
    return carried


def early_kernel(step):
    def kernel(ext, words, *refs):
        fvx, ux, along, fvy, vy = refs[-6:-1] if step == 0 else refs
        bits = level_bits()
        if step == 0:
            coef, coef_rows = refs[0], refs[-1]
            for k in range(NCLASS):
                coef_rows[pl.ds(k, 1), :] = jnp.full((1, LANES), coef[k], jnp.float32)

        def one_row(r, carry):
            for p, (lead, members) in enumerate(PHASES):
                word = spread(words, plane(step, 0, p // 2) * ROWS + r)
                flag = (word & bits[p % 2]) != 0
                u = ext[lead + 1, r + 2] * inverse_root(ext[lead, r + 2])
                speed = FACE * (u + roll(u, -1))
                ux[p, r] = speed
                for f in range(lead, lead + members):
                    c = ext[f, r + 2]
                    value = face_values(roll(c, 1), c, roll(c, -1), roll(c, -2), flag)
                    fvx[f, r] = value
                    flux = speed * value
                    along[f, r] = c - (flux - roll(flux, 1))
            return carry

        lax.fori_loop(0, ROWS, one_row, 0, unroll=2)
        for j in range(2, ROWS - 1):
            forward_face(j, step, ext, words, None, fvy, vy)

    return kernel


def outer_faces(step, ext, words, low_words, fvy, vy):
    for j in (0, 1, ROWS - 1, ROWS):
        forward_face(j, step, ext, words, low_words, fvy, vy)


def coupled(c):
    s = inverse_root(c[0])
    u, v = c[1] * s, c[2] * s
    gas_x, gas_y = c[1], c[2]
    out = [None] * FIELDS
    for lead, _ in PHASES[1:]:
        pull_x = COUPLING * (c[lead] * u - c[lead + 1])
        pull_y = COUPLING * (c[lead] * v - c[lead + 2])
        gas_x, gas_y = gas_x - pull_x, gas_y - pull_y
        out[lead] = c[lead]
        out[lead + 1], out[lead + 2] = c[lead + 1] + pull_x, c[lead + 2] + pull_y
    out[0], out[1], out[2], out[3], out[4] = c[0], gas_x, gas_y, c[3], c[4]
    return out, s, u, v


def dragged(q, drag):
    q = list(q)
    for lead, _ in PHASES:
        s = inverse_root(q[lead])
        u, v = q[lead + 1] * s, q[lead + 2] * s
        factor = 1.0 - drag * jnp.sqrt(u * u + v * v + 1.0)
        q[lead + 1], q[lead + 2] = q[lead + 1] * factor, q[lead + 2] * factor
    return q


def drag_terms(q, a):
    total = None
    for lead, _ in PHASES:
        s = inverse_root(q(lead))
        x, y = q(lead + 1), q(lead + 2)
        u, v = x * s, y * s
        term = jnp.sqrt(u * u + v * v + 1.0) * (a[lead + 1] * x + a[lead + 2] * y)
        total = term if total is None else total + term
    return -total


def stepped_back(c, drag, a, want_terms):
    q, s0, gas_u, gas_v = coupled(c)
    a = list(a)
    terms = jnp.zeros((8, LANES), jnp.float32)
    for lead, _ in PHASES:
        m, x, y = q[lead], q[lead + 1], q[lead + 2]
        s = s0 if lead == 0 else inverse_root(m)
        u, v = x * s, y * s
        energy = u * u + v * v
        root = lax.rsqrt(energy + 1.0)
        w = (energy + 1.0) * root
        dot = a[lead + 1] * x + a[lead + 2] * y
        if want_terms:
            terms = terms - w * dot
        k = drag * dot * root
        factor = 1.0 - drag * w
        ks = k * s
        a[lead + 1] = a[lead + 1] * factor - ks * u
        a[lead + 2] = a[lead + 2] * factor - ks * v
        a[lead] = a[lead] + k * energy * m * (s * s)
    du = jnp.zeros((8, LANES), jnp.float32)
    dv = jnp.zeros((8, LANES), jnp.float32)
    for lead, _ in PHASES[1:]:
        rx, ry = COUPLING * (a[lead + 1] - a[1]), COUPLING * (a[lead + 2] - a[2])
        a[lead] = a[lead] + rx * gas_u + ry * gas_v
        du, dv = du + c[lead] * rx, dv + c[lead] * ry
        a[lead + 1], a[lead + 2] = a[lead + 1] - rx, a[lead + 2] - ry
    a[1], a[2] = a[1] + du * s0, a[2] + dv * s0
    a[0] = a[0] - (gas_u * du + gas_v * dv) * c[0] * (s0 * s0)
    return a, terms


def add_speed_terms(total, state, lead, du, dv):
    m, x, y = state
    s = inverse_root(m)
    pull = None
    if du is not None:
        total[lead + 1] = total[lead + 1] + s * du
        pull = x * s * du
    if dv is not None:
        total[lead + 2] = total[lead + 2] + s * dv
        pull = y * s * dv if pull is None else pull + y * s * dv
    total[lead] = total[lead] - pull * m * (s * s)


def scatter_x(a, value, speed, flag):
    ahead = roll(a, -1) - a
    g = speed * ahead
    low = jnp.where(flag, g, 0.0)
    high = roll(g - low, 1)
    return 3.0 * (low + high) - roll(low, -1) - roll(high, 1), value * ahead


def expand_edges(own):
    pos = strip_pos()
    value = jnp.where(pos < 4, own, jnp.where((pos >= 8) & (pos < 12), roll(own, 4), 0.0))
    return value


def backward_strip(step, strip, edges_a, edge_words, left_words, sfv, su, sdc, sdu, out_c):
    bits = level_bits()
    walls = face_walls()
    ghosts = []
    for p, (lead, members) in enumerate(PHASES):
        word = strip_words(edge_words, left_words, plane(step, 0, p // 2))
        flag = (word & bits[p % 2]) != 0
        speed = su[p]
        du = jnp.zeros((8, LANES), jnp.float32)
        total = {}
        for f in range(lead, lead + members):
            total[f], term = scatter_x(expand_edges(edges_a[f]), sfv[f], speed, flag)
            sdc[f] = gather_edges(total[f])
            du = du + term
        du = walls * du
        du = du + roll(du, 1)
        sdu[p] = gather_edges(du)
        add_speed_terms(total, (strip[lead], strip[lead + 1], strip[lead + 2]), lead, du, None)
        ghosts.extend(total[f] for f in range(lead, lead + members))
    for g in range(4):
        fields = range(4 * g, min(4 * g + 4, FIELDS))
        out_c[g] = into_slots([roll(ghosts[f], 4 * (f % 4) - 4) for f in fields])
    return ghosts


def backward_faces(step, ext, words, low_words, a_ext, fvy, vy, gl, gh, dvy, put):
    bits = level_bits()
    zero = jnp.zeros((8, LANES), jnp.float32)
    for k in (0, 1, 2, 12, 13, 14):
        for f in range(FIELDS):
            gl[f, k] = zero
            gh[f, k] = zero
        for p in range(4):
            dvy[p, k] = zero

    def face(j, carry):
        wall = row_wall(j)
        for p, (lead, members) in enumerate(PHASES):
            word = face_word(j, words, low_words, plane(step, 1, p // 2))
            flag = (word & bits[p % 2]) != 0
            speed = vy[p, j]
            dv = jnp.zeros((8, LANES), jnp.float32)
            for f in range(lead, lead + members):
                ahead = a_ext[f, j + 1] - a_ext[f, j]
                g = speed * ahead
                low = jnp.where(flag, g, 0.0)
                gl[f, j + 3] = low
                gh[f, j + 3] = g - low
                dv = dv + fvy[f, j] * ahead
            dvy[p, j + 3] = wall * dv
        return carry

    lax.fori_loop(0, ROWS + 1, face, 0, unroll=9)
    for i in (-2, -1, ROWS, ROWS + 1):
        total = [transposed_y(gl, gh, f, i) for f in range(FIELDS)]
        for p, (lead, members) in enumerate(PHASES):
            dv = dvy[p, i + 4] + dvy[p, i + 3]
            state = (ext[lead, i + 2], ext[lead + 1, i + 2], ext[lead + 2, i + 2])
            add_speed_terms(total, state, lead, None, dv)
        put(i, total)


def transposed_y(gl, gh, f, i):
    return 3.0 * (gl[f, i + 4] + gh[f, i + 3]) - gl[f, i + 5] - gh[f, i + 2]


def backward_own(step, ext, words, a_ext, fvx, ux, sdc, sdu, gl, gh, dvy, put):
    bits = level_bits()
    edges = edge_lanes()

    def own(r, carry):
        total = [None] * FIELDS
        for p, (lead, members) in enumerate(PHASES):
            word = spread(words, plane(step, 0, p // 2) * ROWS + r)
            flag = (word & bits[p % 2]) != 0
            speed = ux[p, r]
            du = jnp.zeros((8, LANES), jnp.float32)
            for f in range(lead, lead + members):
                a = a_ext[f, r + 1]
                part, term = scatter_x(a, fvx[f, r], speed, flag)
                part = jnp.where(edges, roll(sdc[f], 124 - 16 * r), part)
                total[f] = a + part + transposed_y(gl, gh, f, r)
                du = du + term
            du = FACE * (du + roll(du, 1))
            du = jnp.where(edges, roll(sdu[p], 124 - 16 * r), du)
            dv = dvy[p, r + 4] + dvy[p, r + 3]
            state = (ext[lead, r + 2], ext[lead + 1, r + 2], ext[lead + 2, r + 2])
            add_speed_terms(total, state, lead, du, dv)
        put(r, total)
        return carry

    lax.fori_loop(0, ROWS, own, 0, unroll=2)


def level_weight():
    levels = lax.broadcasted_iota(jnp.int32, (8, LANES), 0)
    weight = jnp.full((8, LANES), DRAG_STEP, jnp.float32)
    for k in range(3):
        weight = jnp.where((levels // 2**k) % 2 == 1, weight * 0.5 ** (2**k), weight)
    return weight


def drag_table(classes, coef_rows):
    drag = jnp.zeros(classes.shape, jnp.float32)
    for k in range(NCLASS):
        drag = jnp.where(classes == k, jnp.broadcast_to(coef_rows[pl.ds(k, 1), :], classes.shape), drag)
    return drag


def level_sum(v):
    return jnp.sum(v, axis=0, keepdims=True)


def row_bases():
    gy, _ = position("gy")
    is_even = gy % 2 == 0
    return is_even


def fill_ghost_rows(ext, from_a, from_b):
    is_even = row_bases()
    a_row = jnp.where(is_even, ROWS + 2, 0)
    b_row = jnp.where(is_even, 0, ROWS + 2)
    for f in range(FIELDS):
        for j in range(2):
            ext[f, a_row + j] = from_a[2 * f + j]
            ext[f, b_row + j] = from_b[2 * f + j]


def put_edge_rows(source, offset, to_a, to_b):
    is_even = row_bases()
    a_row = jnp.where(is_even, ROWS - 2, 0) + offset
    b_row = jnp.where(is_even, 0, ROWS - 2) + offset
    for f in range(FIELDS):
        for j in range(2):
            to_a[2 * f + j] = source[f, a_row + j]
            to_b[2 * f + j] = source[f, b_row + j]


def pack_kernel(start_in, words_in, terrain_in, words, terrain, ext, edges, edge_words, to_a, to_b, to_c, start, sems):
    copies = [
        pltpu.make_async_copy(source, target, sems.at[k])
        for k, (source, target) in enumerate(((start_in, start), (words_in, words), (terrain_in, terrain)))
    ]
    for copy in copies:
        copy.start()
    zero_edges(edges)
    edge_words[...] = jnp.zeros((8, LANES), jnp.int32)
    slots = lax.broadcasted_iota(jnp.int32, (8, LANES), 0)
    for copy in copies:
        copy.wait()

    def one_row(r, carry):
        values = [start[f, pl.ds(r, 8, stride=8), :] for f in range(FIELDS)]
        for f in range(FIELDS):
            ext[f, r + 2] = values[f]
        add_edges(edges, values, r)
        mine = strip_row() == r
        row_words = jnp.where(slots == TERRAIN_SLOT, spread(terrain, r), words[pl.ds(r, 8, stride=8), :])
        edge_words[...] = jnp.where(mine, roll(row_words, (16 * r + 4) % LANES), edge_words[...])
        return carry

    lax.fori_loop(0, ROWS, one_row, 0, unroll=8)
    put_edge_rows(ext, 2, to_a, to_b)
    top = words[pl.ds(ROWS - 1, 8, stride=8), :]
    is_even = row_bases()
    a_row = jnp.where(is_even, ROWS - 2, 0)
    for target, row in ((to_a, a_row), (to_b, ROWS - 2 - a_row)):
        mixed = jnp.where(slots == 0, spread(terrain, row), jnp.where(slots == 1, spread(terrain, row + 1), top))
        target[2 * FIELDS] = mixed.astype(jnp.float32)
    edge_payload(edges, to_c)
    to_c[4] = edge_words[...].astype(jnp.float32)


def neighbour_words(from_a, from_b, pick):
    low = jnp.where(row_bases(), from_b[2 * FIELDS], from_a[2 * FIELDS]).astype(jnp.int32)
    left, _ = pick(4)
    return low, left.astype(jnp.int32)


def first_kernel(has_odd):
    def kernel(*refs):
        (_, _, _, edges, edge_words, along, words, terrain, coef, from_a, from_b, from_c) = refs[:12]
        from_d = refs[12] if has_odd else None
        outs = refs[12 + has_odd :]
        (ext, fvy, vy, strip, carried_ref, sfv, su, drag_ref, class_ref, low_ref, left_ref) = outs[:11]
        middle, before, before_edges, to_a, to_b, to_c = outs[11:17]
        (sdx,) = outs[17:]
        pick = side_payloads(from_c, from_d)
        fill_ghost_rows(ext, from_a, from_b)
        build_strip(edges, pick, strip)
        low_words, left_words = neighbour_words(from_a, from_b, pick)
        low_ref[...] = low_words
        left_ref[...] = left_words
        is_even = row_bases()
        a_row = jnp.where(is_even, ROWS + 2, 0)
        class_ref[pl.ds(2, ROWS), :] = terrain[...]
        for source, row in ((from_a, a_row), (from_b, ROWS + 2 - a_row)):
            for j in range(2):
                class_ref[pl.ds(row + j, 1), :] = source[2 * FIELDS, pl.ds(j, 1), :].astype(jnp.int32)
        class_ref[pl.ds(12, 4), :] = strip_classes(edge_words, pick)[:4]
        drag_ref[...] = drag_table(class_ref[...], coef)
        forward_strip(0, strip, edge_words, left_words, sfv, su, sdx)
        outer_faces(0, ext, words, low_words, fvy, vy)
        zero_edges(before_edges)
        weight = level_weight()
        seams = edge_lanes()

        def one_row(r, carry):
            c = carried_row(r, seams, ext, sdx, along, fvy, vy)
            for f in range(FIELDS):
                carried_ref[f, r] = c[f]
            q = coupled(c)[0]
            for f in range(FIELDS):
                before[f, r + 2] = q[f]
            add_edges(before_edges, q, r)
            q = dragged(q, weight * spread(drag_ref, r + 2))
            for f in range(FIELDS):
                middle[f, r + 2] = q[f]
            return carry

        lax.fori_loop(0, ROWS, one_row, 0, unroll=2)
        put_edge_rows(before, 2, to_a, to_b)
        edge_payload(before_edges, to_c)

    return kernel


def put_ghost_rows(values, row, to_a, to_b):
    is_even = row_bases()
    j = row % 2
    above = row >= ROWS

    @pl.when(is_even if above else jnp.logical_not(is_even))
    def _():
        for f in range(FIELDS):
            to_a[2 * f + j] = values[f]

    @pl.when(jnp.logical_not(is_even) if above else is_even)
    def _():
        for f in range(FIELDS):
            to_b[2 * f + j] = values[f]


def second_kernel(has_odd):
    def kernel(*refs):
        (_, _, _, _, before_edges, edge_words, along, fvx, ux, words) = refs[:10]
        (drag_ref, class_ref, low_ref, left_ref, adjoint, from_a, from_b, from_c) = refs[10:18]
        from_d = refs[18] if has_odd else None
        outs = refs[18 + has_odd :]
        ext, before, fvy, vy, part, to_a, to_b, to_c = outs[:8]
        (strip, sfv, su, sdx, a_ext, edges_a, sdc, sdu, gl, gh, dvy, before_strip, cells) = outs[8:]
        pick = side_payloads(from_c, from_d)
        low_words, left_words = low_ref[...], left_ref[...]
        weight = level_weight()
        fill_ghost_rows(before, from_a, from_b)
        for row in (0, 1, ROWS + 2, ROWS + 3):
            q = dragged([before[f, row] for f in range(FIELDS)], weight * spread(drag_ref, row))
            for f in range(FIELDS):
                ext[f, row] = q[f]
        build_strip(before_edges, pick, before_strip)
        q = dragged([before_strip[f] for f in range(FIELDS)], weight * spread(drag_ref, 12))
        for f in range(FIELDS):
            strip[f] = q[f]
        forward_strip(1, strip, edge_words, left_words, sfv, su, sdx)
        outer_faces(1, ext, words, low_words, fvy, vy)
        zero_edges(edges_a)
        for f in range(FIELDS):
            a_ext[f, 0] = jnp.zeros((8, LANES), jnp.float32)
            a_ext[f, ROWS + 1] = jnp.zeros((8, LANES), jnp.float32)
        cells[...] = jnp.zeros((16, LANES), jnp.float32)
        seams = edge_lanes()

        def one_row(r, carry):
            c = carried_row(r, seams, ext, sdx, along, fvy, vy)
            a = [adjoint[f, pl.ds(r, 8, stride=8), :] for f in range(FIELDS)]
            a, terms = stepped_back(c, weight * spread(drag_ref, r + 2), a, True)
            cells[pl.ds(r + 2, 1), :] = level_sum(weight * terms)
            for f in range(FIELDS):
                a_ext[f, r + 1] = a[f]
            add_edges(edges_a, a, r)
            return carry

        lax.fori_loop(0, ROWS, one_row, 0, unroll=2)
        ghosts = backward_strip(1, strip, edges_a, edge_words, left_words, sfv, su, sdc, sdu, to_c)
        pos = strip_pos()
        terms = jnp.where((pos >= 4) & (pos < 8), drag_terms(lambda f: before_strip[f], ghosts), 0.0)
        cells[pl.ds(12, 1), :] = level_sum(weight * terms)

        def put_terms(row, values):
            terms = drag_terms(lambda f: before[f, row + 2], values)
            at = pl.ds(row + 2, 1)
            cells[at, :] = cells[at, :] + level_sum(weight * terms)

        def put_ghost(row, values):
            put_ghost_rows(values, row, to_a, to_b)
            put_terms(row, values)

        def put_own(row, values):
            for f in range(FIELDS):
                part[f, row] = values[f]
            put_terms(row, values)

        backward_faces(1, ext, words, low_words, a_ext, fvy, vy, gl, gh, dvy, put_ghost)
        backward_own(1, ext, words, a_ext, fvx, ux, sdc, sdu, gl, gh, dvy, put_own)
        to_c[4] = binned(class_ref[...], cells[...])

    return kernel


def binned(classes, cells):
    lanes = lane_ids()
    slots = lax.broadcasted_iota(jnp.int32, (8, LANES), 0)
    total = jnp.zeros((8, LANES), jnp.float32)
    for first in range(0, NCLASS, 8):
        block = jnp.zeros((8, LANES), jnp.float32)
        for k in range(first, min(first + 8, NCLASS)):
            block = jnp.where(slots == k - first, level_sum(jnp.where(classes == k, cells, 0.0)), block)
        block = jnp.sum(block, axis=1, keepdims=True)
        total = jnp.where(lanes == first + slots, block, total)
    return jnp.broadcast_to(level_sum(total), (8, LANES))


def collect(part, from_a, from_b, pick, incoming):
    is_even = row_bases()
    a_row = jnp.where(is_even, ROWS - 2, 0)
    b_row = ROWS - 2 - a_row
    for f in range(FIELDS):
        for j in range(2):
            part[f, a_row + j] = part[f, a_row + j] + from_a[2 * f + j]
            part[f, b_row + j] = part[f, b_row + j] + from_b[2 * f + j]
    pos = strip_pos()
    at_left = (pos == 4) | (pos == 5)
    at_right = (pos == 2) | (pos == 3)
    for g in range(4):
        left, right = pick(g)
        for f in range(4 * g, min(4 * g + 4, FIELDS)):
            q = f % 4
            incoming[f] = jnp.where(at_left, roll(left, 4 - 4 * q), jnp.where(at_right, roll(right, -4 * q), 0.0))


def third_kernel(has_odd):
    def kernel(*refs):
        _, carried_ref, drag_ref, from_a, from_b, from_c = refs[:6]
        from_d = refs[6] if has_odd else None
        part, a_ext, edges_a, incoming = refs[6 + has_odd :]
        pick = side_payloads(from_c, from_d)
        collect(part, from_a, from_b, pick, incoming)
        zero_edges(edges_a)
        for f in range(FIELDS):
            a_ext[f, 0] = jnp.zeros((8, LANES), jnp.float32)
            a_ext[f, ROWS + 1] = jnp.zeros((8, LANES), jnp.float32)
        edges = edge_lanes()
        weight = level_weight()

        def one_row(r, carry):
            c = [carried_ref[f, r] for f in range(FIELDS)]
            a = [part[f, r] + jnp.where(edges, roll(incoming[f], 124 - 16 * r), 0.0) for f in range(FIELDS)]
            a, _ = stepped_back(c, weight * spread(drag_ref, r + 2), a, False)
            for f in range(FIELDS):
                a_ext[f, r + 1] = a[f]
            add_edges(edges_a, a, r)
            return carry

        lax.fori_loop(0, ROWS, one_row, 0, unroll=4)

    return kernel


def seam_kernel(a_ext, edges_a, ext, strip, fvy, vy, sfv, su, *refs):
    low_ref, left_ref, edge_words, words, grads, arriving, *outs = refs
    to_a, to_b, to_c, sdc, sdu, gl, gh, dvy = outs
    low_words, left_words = low_ref[...], left_ref[...]
    backward_strip(0, strip, edges_a, edge_words, left_words, sfv, su, sdc, sdu, to_c)

    def put_ghost(row, values):
        put_ghost_rows(values, row, to_a, to_b)

    backward_faces(0, ext, words, low_words, a_ext, fvy, vy, gl, gh, dvy, put_ghost)
    to_a[2 * FIELDS] = grads[...] + arriving[...]


def own_kernel(ext, words, a_ext, fvx, ux, sdc, sdu, gl, gh, dvy, part):
    def put(row, values):
        for f in range(FIELDS):
            part[f, row] = values[f]

    backward_own(0, ext, words, a_ext, fvx, ux, sdc, sdu, gl, gh, dvy, put)


def last_kernel(has_odd):
    def kernel(*refs):
        _, from_a, from_b, from_c = refs[:4]
        from_d = refs[4] if has_odd else None
        out, part, incoming, staged, sems = refs[4 + has_odd :]
        pick = side_payloads(from_c, from_d)
        collect(part, from_a, from_b, pick, incoming)
        edges = edge_lanes()

        copies = []
        for k, fields in enumerate(HALVES):
            for r in range(ROWS):
                for f in fields:
                    value = part[f, r] + jnp.where(edges, roll(incoming[f], (124 - 16 * r) % LANES), 0.0)
                    staged[f, pl.ds(r, 8, stride=8), :] = value
            span = pl.ds(fields[0], len(fields))
            copies.append(pltpu.make_async_copy(staged.at[span], out.at[span], sems.at[k]))
            copies[-1].start()
        for copy in copies:
            copy.wait()

    return kernel


def shaped(*shape, dtype=jnp.float32):
    return jax.ShapeDtypeStruct(shape, dtype)


def tiles(*shape, dtype=jnp.float32):
    return shaped(*shape, 8, LANES, dtype=dtype)


def scratch(*shape, dtype=jnp.float32):
    return pltpu.VMEM((*shape, 8, LANES), dtype)


def call(kernel, outs, scratches, args, smem=(), hbm=(), aliases=None, hbm_outs=()):
    def space(k):
        return pltpu.SMEM if k in smem else pltpu.HBM if k in hbm else pltpu.VMEM

    return pl.pallas_call(
        kernel,
        out_shape=outs,
        in_specs=[pl.BlockSpec(memory_space=space(k)) for k in range(len(args))],
        out_specs=[pl.BlockSpec(memory_space=pltpu.HBM if k in hbm_outs else pltpu.VMEM) for k in range(len(outs))],
        scratch_shapes=scratches,
        input_output_aliases=aliases or {},
        compiler_params=pltpu.CompilerParams(vmem_limit_bytes=32 << 20),
    )(*args)


def swap(x, axis, first):
    peers = lax.axis_size(axis)
    pairs = [(i, i + 1) for i in range(first, peers - 1, 2)]
    if not pairs:
        return None
    return lax.ppermute(x, axis, pairs + [(j, i) for i, j in pairs])


def exchange(to_a, to_b, to_c):
    from_a = swap(to_a, "gy", 0)
    from_b = swap(to_b, "gy", 1)
    from_c = swap(to_c, "gx", 0)
    from_d = swap(to_c, "gx", 1)
    if from_b is None:
        from_b = jnp.zeros_like(to_b)
    return (from_a, from_b, from_c) + (() if from_d is None else (from_d,))


def from_partner(x, axis, distance):
    return lax.ppermute(x, axis, [(i, i ^ distance) for i in range(lax.axis_size(axis))])


def add_partner(x, axis, distance):
    return x + from_partner(x, axis, distance)


def body(start_state, final_adjoint, face_words, terrain, drag_coef):
    nx, ny = lax.axis_size("gx"), lax.axis_size("gy")
    has_odd = nx > 2
    start = start_state.reshape(FIELDS, LEV * ROWS, LANES)
    adjoint = final_adjoint.reshape(FIELDS, LEV * ROWS, LANES)
    words = face_words.reshape(8 * ROWS, LANES)
    ints = jnp.int32

    words, terrain, ext, edges, edge_words, *payload = call(
        pack_kernel,
        [shaped(*words.shape, dtype=ints), shaped(*terrain.shape, dtype=ints)]
        + [tiles(14, 12), tiles(14), tiles(dtype=ints), tiles(29), tiles(29), tiles(5)],
        [
            pltpu.VMEM(start.shape, jnp.float32),
            pltpu.SemaphoreType.DMA((3,)),
        ],
        [pltpu.with_memory_space_constraint(x, pltpu.HBM) for x in (start, words, terrain)],
        hbm=(0, 1, 2),
    )
    got = exchange(*payload)
    early = [tiles(14, 8), tiles(4, 8), tiles(14, 8), tiles(14, 9), tiles(4, 9)]
    fvx, ux, along, fvy, vy, coef_rows = call(
        early_kernel(0), [*early, shaped(NCLASS, LANES)], [], [ext, words, drag_coef], smem=(2,)
    )
    res = call(
        first_kernel(has_odd),
        [tiles(14, 12), tiles(14, 9), tiles(4, 9), tiles(14), tiles(14, 8), tiles(14), tiles(4)]
        + [shaped(16, LANES), shaped(16, LANES, dtype=ints), tiles(dtype=ints), tiles(dtype=ints)]
        + [tiles(14, 12), tiles(14, 12), tiles(14), tiles(28), tiles(28), tiles(4)],
        [scratch(14)],
        [ext, fvy, vy, edges, edge_words, along, words, terrain, coef_rows, *got],
        aliases={0: 0, 1: 1, 2: 2},
    )
    ext, fvy, vy, strip, carried_ref, sfv, su, drag_ref, class_ref, low_ref, left_ref = res[:11]
    middle, before, before_edges, *payload = res[11:]
    got = exchange(*payload)
    fvx2, ux2, along2, fvy2, vy2 = call(early_kernel(1), early, [], [middle, words])
    kept = [scratch(14, 10), scratch(14), scratch(14), scratch(4), scratch(14, 15), scratch(14, 15), scratch(4, 15)]
    part, *payload = call(
        second_kernel(has_odd),
        [tiles(14, 12), tiles(14, 12), tiles(14, 9), tiles(4, 9), tiles(14, 8), tiles(28), tiles(28), tiles(5)],
        [scratch(14), scratch(14), scratch(4), scratch(14), *kept, scratch(14), pltpu.VMEM((16, LANES), jnp.float32)],
        [middle, before, fvy2, vy2, before_edges, edge_words, along2, fvx2, ux2, words]
        + [drag_ref, class_ref, low_ref, left_ref, adjoint, *got],
        aliases={0: 0, 1: 1, 2: 2, 3: 3},
    )[4:]
    got = exchange(*payload)
    grads = payload[2][4] + got[2][4]
    steps = [("gx", 2**k) for k in range(1, 32) if 2**k < nx] + [("gy", 2**k) for k in range(1, 32) if 2**k < ny]
    steps = steps[::-1]
    early_steps = 1
    for axis, distance in steps[: early_steps - 1]:
        grads = add_partner(grads, axis, distance)
    arriving = from_partner(grads, *steps[early_steps - 1])
    _, a_ext, edges_a = call(
        third_kernel(has_odd),
        [tiles(14, 8), tiles(14, 10), tiles(14)],
        [scratch(14)],
        [part, carried_ref, drag_ref, *got],
        aliases={0: 0},
    )
    to_a, to_b, to_c, *adjoints = call(
        seam_kernel,
        [tiles(29), tiles(28), tiles(4), tiles(14), tiles(4), tiles(14, 15), tiles(14, 15), tiles(4, 15)],
        [],
        [a_ext, edges_a, ext, strip, fvy, vy, sfv, su, low_ref, left_ref, edge_words, words, grads, arriving],
    )
    sdc, sdu, gl, gh, dvy = adjoints
    got = exchange(to_a, to_b, to_c)
    grads = to_a[2 * FIELDS] + got[0][2 * FIELDS]
    for axis, distance in steps[early_steps:-1]:
        grads = add_partner(grads, axis, distance)
    (part,) = call(own_kernel, [tiles(14, 8)], [], [ext, words, a_ext, fvx, ux, sdc, sdu, gl, gh, dvy])
    grads, part = lax.optimization_barrier((grads, part))
    grads = add_partner(grads, *steps[-1])
    out, _ = call(
        last_kernel(has_odd),
        [shaped(FIELDS, LEV * ROWS, LANES), tiles(14, 8)],
        [scratch(14), pltpu.VMEM(start.shape, jnp.float32), pltpu.SemaphoreType.DMA((2,))],
        [part, *got],
        aliases={0: 1},
        hbm_outs=(0,),
    )
    grad_scale = math.sqrt(NCLASS / (terrain.size * nx * ny * LEV))
    return (out.reshape(start_state.shape), grads[0, :NCLASS] * grad_scale)


def solution(mesh):
    placed = (
        P(None, None, "gy", "gx"),
        P(None, None, "gy", "gx"),
        P(None, None, None, "gy", "gx"),
        P("gy", "gx"),
        P(),
    )
    return jax.shard_map(
        body,
        mesh=mesh,
        in_specs=placed,
        out_specs=(P(None, None, "gy", "gx"), P()),
        check_vma=False,
    )
```

```python
import math

import jax
import jax.numpy as jnp
from jax import lax
from jax.experimental import pallas as pl
from jax.experimental.pallas import tpu as pltpu
from jax.sharding import PartitionSpec as P

LEV = 8
NCLASS = 24
FIELDS = 14
ROWS = 8
LANES = 128
PHASES = ((0, 5), (5, 3), (8, 3), (11, 3))
FACE = 0.3 * 0.5 * 0.5
COUPLING = 0.5
DRAG_STEP = 0.5
TERRAIN_SLOT = 2


def roll(v, shift):
    return pltpu.roll(v, shift % LANES if isinstance(shift, int) else shift, 1)


def lane_ids():
    return lax.broadcasted_iota(jnp.int32, (8, LANES), 1)


def strip_pos():
    return lane_ids() % 16


def strip_row():
    return lane_ids() // 16


def level_bits():
    levels = lax.broadcasted_iota(jnp.int32, (8, LANES), 0)
    return [jnp.left_shift(jnp.ones_like(levels), levels + LEV * k) for k in range(2)]


def edge_lanes():
    lanes = lane_ids()
    return (lanes < 2) | (lanes >= LANES - 2)


def spread(ref, index):
    return jnp.broadcast_to(ref[pl.ds(index, 1), :], (8, LANES))


def plane(step, direction, pair):
    return step * 4 + direction * 2 + pair


def position(axis):
    return lax.axis_index(axis), lax.axis_size(axis)


def into_slots(values):
    pos = strip_pos() // 4
    total = jnp.zeros((8, LANES), jnp.float32)
    for slot, value in enumerate(values):
        total = jnp.where(pos == slot, value, total)
    return total


def add_edges(edges_ref, values, row):
    mine = strip_row() == row
    for f, value in enumerate(values):
        edges_ref[f] = jnp.where(mine, roll(value, 16 * row + 4), edges_ref[f])


def zero_edges(edges_ref, count=FIELDS):
    for f in range(count):
        edges_ref[f] = jnp.zeros((8, LANES), edges_ref.dtype)


def edge_payload(edges_ref, out_ref):
    for g in range(4):
        fields = range(4 * g, min(4 * g + 4, FIELDS))
        out_ref[g] = into_slots([roll(edges_ref[f], 4 * (f % 4) - 2) for f in fields])


def side_payloads(even_ref, odd_ref):
    index, _ = position("gx")
    is_even = index % 2 == 0

    def pick(k):
        a = even_ref[k]
        b = jnp.zeros_like(a) if odd_ref is None else odd_ref[k]
        return jnp.where(is_even, b, a), jnp.where(is_even, a, b)

    return pick


def build_strip(edges_ref, pick, strip_ref):
    pos = strip_pos()
    for g in range(4):
        left, right = pick(g)
        for f in range(4 * g, min(4 * g + 4, FIELDS)):
            q = f % 4
            own = edges_ref[f]
            value = jnp.where(pos < 4, own, roll(right, 2 - 4 * q))
            value = jnp.where(pos < 6, value, roll(left, 6 - 4 * q))
            value = jnp.where(pos < 8, value, roll(own, 4))
            strip_ref[f] = jnp.where(pos < 12, value, 0.0)


def strip_words(edge_words_ref, left_words, which):
    pos = strip_pos()
    own = spread(edge_words_ref, which)
    left = jnp.broadcast_to(left_words[which : which + 1], (8, LANES))
    value = jnp.where(pos < 4, own, roll(own, 4))
    return jnp.where(pos == 7, roll(left, 4), value)


def strip_classes(edge_words_ref, pick):
    pos = strip_pos()
    own = spread(edge_words_ref, TERRAIN_SLOT)
    left, right = [jnp.broadcast_to(v[TERRAIN_SLOT : TERRAIN_SLOT + 1], (8, LANES)).astype(jnp.int32) for v in pick(4)]
    value = jnp.where(pos < 4, own, jnp.where(pos < 6, right, jnp.where(pos < 8, roll(left, 4), roll(own, 4))))
    return value


def face_walls():
    gx, nx = position("gx")
    pos = strip_pos()
    shut = ((pos == 7) & (gx == 0)) | ((pos == 3) & (gx == nx - 1))
    return jnp.where(shut, 0.0, FACE)


def row_wall(j):
    gy, ny = position("gy")
    shut = ((j == 0) & (gy == 0)) | ((j == ROWS) & (gy == ny - 1))
    return jnp.where(shut, 0.0, FACE)


def inverse_root(mass):
    return lax.rsqrt(mass * mass + 1.0)


def gather_edges(v):
    pos = strip_pos()
    return jnp.where((pos == 4) | (pos == 5), roll(v, -4), v)


def face_values(behind, here, ahead, beyond, flag):
    return jnp.where(flag, 3.0 * here - behind, 3.0 * ahead - beyond)


def forward_strip(step, strip, edge_words, left_words, sfv, su, sdx):
    bits = level_bits()
    walls = face_walls()
    for p, (lead, members) in enumerate(PHASES):
        word = strip_words(edge_words, left_words, plane(step, 0, p // 2))
        flag = (word & bits[p % 2]) != 0
        u = strip[lead + 1] * inverse_root(strip[lead])
        speed = walls * (u + roll(u, -1))
        su[p] = speed
        for f in range(lead, lead + members):
            c = strip[f]
            ahead = roll(c, -1)
            value = face_values(roll(c, 1), c, ahead, roll(c, -2), flag)
            sfv[f] = value
            flux = speed * value
            sdx[f] = gather_edges(flux - roll(flux, 1))


def forward_face(j, step, ext, words, low_words, fvy, vy):
    bits = level_bits()
    wall = FACE if low_words is None else row_wall(j)
    for p, (lead, members) in enumerate(PHASES):
        which = plane(step, 1, p // 2)
        word = face_word(j, words, low_words, which)
        flag = (word & bits[p % 2]) != 0
        v_low = ext[lead + 2, j + 1] * inverse_root(ext[lead, j + 1])
        v_high = ext[lead + 2, j + 2] * inverse_root(ext[lead, j + 2])
        vy[p, j] = wall * (v_low + v_high)
        for f in range(lead, lead + members):
            fvy[f, j] = face_values(ext[f, j], ext[f, j + 1], ext[f, j + 2], ext[f, j + 3], flag)


def face_word(j, words, low_words, which):
    if low_words is None:
        return spread(words, which * ROWS + j - 1)
    here = spread(words, which * ROWS + jnp.maximum(j - 1, 0))
    low = jnp.broadcast_to(low_words[which : which + 1], (8, LANES))
    return jnp.where(j == 0, low, here)


def carried_row(r, edges, ext, sdx, along, fvy, vy):
    carried = []
    for p, (lead, members) in enumerate(PHASES):
        below, above = vy[p, r], vy[p, r + 1]
        for f in range(lead, lead + members):
            seam = ext[f, r + 2] - roll(sdx[f], 124 - 16 * r)
            along_y = above * fvy[f, r + 1] - below * fvy[f, r]
            carried.append(jnp.where(edges, seam, along[f, r]) - along_y)
    return carried


def early_kernel(step):
    def kernel(ext, words, *refs):
        extra, fvx, ux, along, fvy, vy, extra_rows = refs
        bits = level_bits()
        if step == 0:
            for k in range(NCLASS):
                extra_rows[pl.ds(k, 1), :] = jnp.full((1, LANES), extra[k], jnp.float32)
        else:
            for f in range(FIELDS):
                for r in range(ROWS):
                    extra_rows[f, r] = extra[f, pl.ds(r, 8, stride=8), :]

        def one_row(r, carry):
            for p, (lead, members) in enumerate(PHASES):
                word = spread(words, plane(step, 0, p // 2) * ROWS + r)
                flag = (word & bits[p % 2]) != 0
                u = ext[lead + 1, r + 2] * inverse_root(ext[lead, r + 2])
                speed = FACE * (u + roll(u, -1))
                ux[p, r] = speed
                for f in range(lead, lead + members):
                    c = ext[f, r + 2]
                    value = face_values(roll(c, 1), c, roll(c, -1), roll(c, -2), flag)
                    fvx[f, r] = value
                    flux = speed * value
                    along[f, r] = c - (flux - roll(flux, 1))
            return carry

        lax.fori_loop(0, ROWS, one_row, 0, unroll=2)
        for j in range(2, ROWS - 1):
            forward_face(j, step, ext, words, None, fvy, vy)

    return kernel


def outer_faces(step, ext, words, low_words, fvy, vy):
    for j in (0, 1, ROWS - 1, ROWS):
        forward_face(j, step, ext, words, low_words, fvy, vy)


def coupled(c):
    s = inverse_root(c[0])
    u, v = c[1] * s, c[2] * s
    gas_x, gas_y = c[1], c[2]
    out = [None] * FIELDS
    for lead, _ in PHASES[1:]:
        pull_x = COUPLING * (c[lead] * u - c[lead + 1])
        pull_y = COUPLING * (c[lead] * v - c[lead + 2])
        gas_x, gas_y = gas_x - pull_x, gas_y - pull_y
        out[lead] = c[lead]
        out[lead + 1], out[lead + 2] = c[lead + 1] + pull_x, c[lead + 2] + pull_y
    out[0], out[1], out[2], out[3], out[4] = c[0], gas_x, gas_y, c[3], c[4]
    return out, s, u, v


def dragged(q, drag):
    q = list(q)
    for lead, _ in PHASES:
        s = inverse_root(q[lead])
        u, v = q[lead + 1] * s, q[lead + 2] * s
        factor = 1.0 - drag * jnp.sqrt(u * u + v * v + 1.0)
        q[lead + 1], q[lead + 2] = q[lead + 1] * factor, q[lead + 2] * factor
    return q


def drag_terms(q, a):
    total = None
    for lead, _ in PHASES:
        s = inverse_root(q(lead))
        x, y = q(lead + 1), q(lead + 2)
        u, v = x * s, y * s
        term = jnp.sqrt(u * u + v * v + 1.0) * (a[lead + 1] * x + a[lead + 2] * y)
        total = term if total is None else total + term
    return -total


def stepped_back(c, drag, a, want_terms):
    q, s0, gas_u, gas_v = coupled(c)
    a = list(a)
    terms = jnp.zeros((8, LANES), jnp.float32)
    for lead, _ in PHASES:
        m, x, y = q[lead], q[lead + 1], q[lead + 2]
        s = s0 if lead == 0 else inverse_root(m)
        u, v = x * s, y * s
        energy = u * u + v * v
        root = lax.rsqrt(energy + 1.0)
        w = (energy + 1.0) * root
        dot = a[lead + 1] * x + a[lead + 2] * y
        if want_terms:
            terms = terms - w * dot
        k = drag * dot * root
        factor = 1.0 - drag * w
        ks = k * s
        a[lead + 1] = a[lead + 1] * factor - ks * u
        a[lead + 2] = a[lead + 2] * factor - ks * v
        a[lead] = a[lead] + k * energy * m * (s * s)
    du = jnp.zeros((8, LANES), jnp.float32)
    dv = jnp.zeros((8, LANES), jnp.float32)
    for lead, _ in PHASES[1:]:
        rx, ry = COUPLING * (a[lead + 1] - a[1]), COUPLING * (a[lead + 2] - a[2])
        a[lead] = a[lead] + rx * gas_u + ry * gas_v
        du, dv = du + c[lead] * rx, dv + c[lead] * ry
        a[lead + 1], a[lead + 2] = a[lead + 1] - rx, a[lead + 2] - ry
    a[1], a[2] = a[1] + du * s0, a[2] + dv * s0
    a[0] = a[0] - (gas_u * du + gas_v * dv) * c[0] * (s0 * s0)
    return a, terms


def add_speed_terms(total, state, lead, du, dv):
    m, x, y = state
    s = inverse_root(m)
    pull = None
    if du is not None:
        total[lead + 1] = total[lead + 1] + s * du
        pull = x * s * du
    if dv is not None:
        total[lead + 2] = total[lead + 2] + s * dv
        pull = y * s * dv if pull is None else pull + y * s * dv
    total[lead] = total[lead] - pull * m * (s * s)


def scatter_x(a, value, speed, flag):
    ahead = roll(a, -1) - a
    g = speed * ahead
    low = jnp.where(flag, g, 0.0)
    high = roll(g - low, 1)
    return 3.0 * (low + high) - roll(low, -1) - roll(high, 1), value * ahead


def expand_edges(own):
    pos = strip_pos()
    value = jnp.where(pos < 4, own, jnp.where((pos >= 8) & (pos < 12), roll(own, 4), 0.0))
    return value


def backward_strip(step, strip, edges_a, edge_words, left_words, sfv, su, sdc, sdu, out_c):
    bits = level_bits()
    walls = face_walls()
    ghosts = []
    for p, (lead, members) in enumerate(PHASES):
        word = strip_words(edge_words, left_words, plane(step, 0, p // 2))
        flag = (word & bits[p % 2]) != 0
        speed = su[p]
        du = jnp.zeros((8, LANES), jnp.float32)
        total = {}
        for f in range(lead, lead + members):
            total[f], term = scatter_x(expand_edges(edges_a[f]), sfv[f], speed, flag)
            sdc[f] = gather_edges(total[f])
            du = du + term
        du = walls * du
        du = du + roll(du, 1)
        sdu[p] = gather_edges(du)
        add_speed_terms(total, (strip[lead], strip[lead + 1], strip[lead + 2]), lead, du, None)
        ghosts.extend(total[f] for f in range(lead, lead + members))
    for g in range(4):
        fields = range(4 * g, min(4 * g + 4, FIELDS))
        out_c[g] = into_slots([roll(ghosts[f], 4 * (f % 4) - 4) for f in fields])
    return ghosts


def backward_faces(step, ext, words, low_words, a_ext, fvy, vy, gl, gh, dvy, put):
    bits = level_bits()
    zero = jnp.zeros((8, LANES), jnp.float32)
    for k in (0, 1, 2, 12, 13, 14):
        for f in range(FIELDS):
            gl[f, k] = zero
            gh[f, k] = zero
        for p in range(4):
            dvy[p, k] = zero

    def face(j, carry):
        wall = row_wall(j)
        for p, (lead, members) in enumerate(PHASES):
            word = face_word(j, words, low_words, plane(step, 1, p // 2))
            flag = (word & bits[p % 2]) != 0
            speed = vy[p, j]
            dv = jnp.zeros((8, LANES), jnp.float32)
            for f in range(lead, lead + members):
                ahead = a_ext[f, j + 1] - a_ext[f, j]
                g = speed * ahead
                low = jnp.where(flag, g, 0.0)
                gl[f, j + 3] = low
                gh[f, j + 3] = g - low
                dv = dv + fvy[f, j] * ahead
            dvy[p, j + 3] = wall * dv
        return carry

    lax.fori_loop(0, ROWS + 1, face, 0, unroll=9)
    for i in (-2, -1, ROWS, ROWS + 1):
        total = [transposed_y(gl, gh, f, i) for f in range(FIELDS)]
        for p, (lead, members) in enumerate(PHASES):
            dv = dvy[p, i + 4] + dvy[p, i + 3]
            state = (ext[lead, i + 2], ext[lead + 1, i + 2], ext[lead + 2, i + 2])
            add_speed_terms(total, state, lead, None, dv)
        put(i, total)


def transposed_y(gl, gh, f, i):
    return 3.0 * (gl[f, i + 4] + gh[f, i + 3]) - gl[f, i + 5] - gh[f, i + 2]


def backward_own(step, ext, words, a_ext, fvx, ux, sdc, sdu, gl, gh, dvy, put):
    bits = level_bits()
    edges = edge_lanes()

    def own(r, carry):
        total = [None] * FIELDS
        for p, (lead, members) in enumerate(PHASES):
            word = spread(words, plane(step, 0, p // 2) * ROWS + r)
            flag = (word & bits[p % 2]) != 0
            speed = ux[p, r]
            du = jnp.zeros((8, LANES), jnp.float32)
            for f in range(lead, lead + members):
                a = a_ext[f, r + 1]
                part, term = scatter_x(a, fvx[f, r], speed, flag)
                part = jnp.where(edges, roll(sdc[f], 124 - 16 * r), part)
                total[f] = a + part + transposed_y(gl, gh, f, r)
                du = du + term
            du = FACE * (du + roll(du, 1))
            du = jnp.where(edges, roll(sdu[p], 124 - 16 * r), du)
            dv = dvy[p, r + 4] + dvy[p, r + 3]
            state = (ext[lead, r + 2], ext[lead + 1, r + 2], ext[lead + 2, r + 2])
            add_speed_terms(total, state, lead, du, dv)
        put(r, total)
        return carry

    lax.fori_loop(0, ROWS, own, 0, unroll=2)


def level_weight():
    levels = lax.broadcasted_iota(jnp.int32, (8, LANES), 0)
    weight = jnp.full((8, LANES), DRAG_STEP, jnp.float32)
    for k in range(3):
        weight = jnp.where((levels // 2**k) % 2 == 1, weight * 0.5 ** (2**k), weight)
    return weight


def drag_table(classes, coef_rows):
    drag = jnp.zeros(classes.shape, jnp.float32)
    for k in range(NCLASS):
        drag = jnp.where(classes == k, jnp.broadcast_to(coef_rows[pl.ds(k, 1), :], classes.shape), drag)
    return drag


def level_sum(v):
    return jnp.sum(v, axis=0, keepdims=True)


def row_bases():
    gy, _ = position("gy")
    is_even = gy % 2 == 0
    return is_even


def fill_ghost_rows(ext, from_a, from_b):
    is_even = row_bases()
    a_row = jnp.where(is_even, ROWS + 2, 0)
    b_row = jnp.where(is_even, 0, ROWS + 2)
    for f in range(FIELDS):
        for j in range(2):
            ext[f, a_row + j] = from_a[2 * f + j]
            ext[f, b_row + j] = from_b[2 * f + j]


def put_edge_rows(source, offset, to_a, to_b):
    is_even = row_bases()
    a_row = jnp.where(is_even, ROWS - 2, 0) + offset
    b_row = jnp.where(is_even, 0, ROWS - 2) + offset
    for f in range(FIELDS):
        for j in range(2):
            to_a[2 * f + j] = source[f, a_row + j]
            to_b[2 * f + j] = source[f, b_row + j]


def pack_kernel(start_in, words_in, terrain_in, words, terrain, ext, edges, edge_words, to_a, to_b, to_c, start, sems):
    copies = [
        pltpu.make_async_copy(source, target, sems.at[k])
        for k, (source, target) in enumerate(((start_in, start), (words_in, words), (terrain_in, terrain)))
    ]
    for copy in copies:
        copy.start()
    zero_edges(edges)
    edge_words[...] = jnp.zeros((8, LANES), jnp.int32)
    slots = lax.broadcasted_iota(jnp.int32, (8, LANES), 0)
    for copy in copies:
        copy.wait()

    def one_row(r, carry):
        values = [start[f, pl.ds(r, 8, stride=8), :] for f in range(FIELDS)]
        for f in range(FIELDS):
            ext[f, r + 2] = values[f]
        add_edges(edges, values, r)
        mine = strip_row() == r
        row_words = jnp.where(slots == TERRAIN_SLOT, spread(terrain, r), words[pl.ds(r, 8, stride=8), :])
        edge_words[...] = jnp.where(mine, roll(row_words, (16 * r + 4) % LANES), edge_words[...])
        return carry

    lax.fori_loop(0, ROWS, one_row, 0, unroll=8)
    put_edge_rows(ext, 2, to_a, to_b)
    top = words[pl.ds(ROWS - 1, 8, stride=8), :]
    is_even = row_bases()
    a_row = jnp.where(is_even, ROWS - 2, 0)
    for target, row in ((to_a, a_row), (to_b, ROWS - 2 - a_row)):
        mixed = jnp.where(slots == 0, spread(terrain, row), jnp.where(slots == 1, spread(terrain, row + 1), top))
        target[2 * FIELDS] = mixed.astype(jnp.float32)
    edge_payload(edges, to_c)
    to_c[4] = edge_words[...].astype(jnp.float32)


def neighbour_words(from_a, from_b, pick):
    low = jnp.where(row_bases(), from_b[2 * FIELDS], from_a[2 * FIELDS]).astype(jnp.int32)
    left, _ = pick(4)
    return low, left.astype(jnp.int32)


def first_kernel(has_odd):
    def kernel(*refs):
        (_, _, _, edges, edge_words, along, words, terrain, coef, from_a, from_b, from_c) = refs[:12]
        from_d = refs[12] if has_odd else None
        outs = refs[12 + has_odd :]
        (ext, fvy, vy, strip, carried_ref, sfv, su, drag_ref, class_ref, low_ref, left_ref) = outs[:11]
        middle, before, before_edges, to_a, to_b, to_c = outs[11:17]
        (sdx,) = outs[17:]
        pick = side_payloads(from_c, from_d)
        fill_ghost_rows(ext, from_a, from_b)
        build_strip(edges, pick, strip)
        low_words, left_words = neighbour_words(from_a, from_b, pick)
        low_ref[...] = low_words
        left_ref[...] = left_words
        is_even = row_bases()
        a_row = jnp.where(is_even, ROWS + 2, 0)
        class_ref[pl.ds(2, ROWS), :] = terrain[...]
        for source, row in ((from_a, a_row), (from_b, ROWS + 2 - a_row)):
            for j in range(2):
                class_ref[pl.ds(row + j, 1), :] = source[2 * FIELDS, pl.ds(j, 1), :].astype(jnp.int32)
        class_ref[pl.ds(12, 4), :] = strip_classes(edge_words, pick)[:4]
        drag_ref[...] = drag_table(class_ref[...], coef)
        forward_strip(0, strip, edge_words, left_words, sfv, su, sdx)
        outer_faces(0, ext, words, low_words, fvy, vy)
        zero_edges(before_edges)
        weight = level_weight()
        seams = edge_lanes()

        def one_row(r, carry):
            c = carried_row(r, seams, ext, sdx, along, fvy, vy)
            for f in range(FIELDS):
                carried_ref[f, r] = c[f]
            q = coupled(c)[0]
            for f in range(FIELDS):
                before[f, r + 2] = q[f]
            add_edges(before_edges, q, r)
            q = dragged(q, weight * spread(drag_ref, r + 2))
            for f in range(FIELDS):
                middle[f, r + 2] = q[f]
            return carry

        lax.fori_loop(0, ROWS, one_row, 0, unroll=2)
        put_edge_rows(before, 2, to_a, to_b)
        edge_payload(before_edges, to_c)

    return kernel


def put_ghost_rows(values, row, to_a, to_b):
    is_even = row_bases()
    j = row % 2
    above = row >= ROWS

    @pl.when(is_even if above else jnp.logical_not(is_even))
    def _():
        for f in range(FIELDS):
            to_a[2 * f + j] = values[f]

    @pl.when(jnp.logical_not(is_even) if above else is_even)
    def _():
        for f in range(FIELDS):
            to_b[2 * f + j] = values[f]


def second_kernel(has_odd):
    def kernel(*refs):
        (_, _, _, _, before_edges, edge_words, along, fvx, ux, words) = refs[:10]
        (drag_ref, class_ref, low_ref, left_ref, adjoint, from_a, from_b, from_c) = refs[10:18]
        from_d = refs[18] if has_odd else None
        outs = refs[18 + has_odd :]
        ext, before, fvy, vy, part, to_a, to_b, to_c = outs[:8]
        (strip, sfv, su, sdx, a_ext, edges_a, sdc, sdu, gl, gh, dvy, before_strip, cells) = outs[8:]
        pick = side_payloads(from_c, from_d)
        low_words, left_words = low_ref[...], left_ref[...]
        weight = level_weight()
        fill_ghost_rows(before, from_a, from_b)
        for row in (0, 1, ROWS + 2, ROWS + 3):
            q = dragged([before[f, row] for f in range(FIELDS)], weight * spread(drag_ref, row))
            for f in range(FIELDS):
                ext[f, row] = q[f]
        build_strip(before_edges, pick, before_strip)
        q = dragged([before_strip[f] for f in range(FIELDS)], weight * spread(drag_ref, 12))
        for f in range(FIELDS):
            strip[f] = q[f]
        forward_strip(1, strip, edge_words, left_words, sfv, su, sdx)
        outer_faces(1, ext, words, low_words, fvy, vy)
        zero_edges(edges_a)
        for f in range(FIELDS):
            a_ext[f, 0] = jnp.zeros((8, LANES), jnp.float32)
            a_ext[f, ROWS + 1] = jnp.zeros((8, LANES), jnp.float32)
        cells[...] = jnp.zeros((16, LANES), jnp.float32)
        seams = edge_lanes()

        def one_row(r, carry):
            c = carried_row(r, seams, ext, sdx, along, fvy, vy)
            a = [adjoint[f, r] for f in range(FIELDS)]
            a, terms = stepped_back(c, weight * spread(drag_ref, r + 2), a, True)
            cells[pl.ds(r + 2, 1), :] = level_sum(weight * terms)
            for f in range(FIELDS):
                a_ext[f, r + 1] = a[f]
            add_edges(edges_a, a, r)
            return carry

        lax.fori_loop(0, ROWS, one_row, 0, unroll=2)
        ghosts = backward_strip(1, strip, edges_a, edge_words, left_words, sfv, su, sdc, sdu, to_c)
        pos = strip_pos()
        terms = jnp.where((pos >= 4) & (pos < 8), drag_terms(lambda f: before_strip[f], ghosts), 0.0)
        cells[pl.ds(12, 1), :] = level_sum(weight * terms)

        def put_terms(row, values):
            terms = drag_terms(lambda f: before[f, row + 2], values)
            at = pl.ds(row + 2, 1)
            cells[at, :] = cells[at, :] + level_sum(weight * terms)

        def put_ghost(row, values):
            put_ghost_rows(values, row, to_a, to_b)
            put_terms(row, values)

        def put_own(row, values):
            for f in range(FIELDS):
                part[f, row] = values[f]
            put_terms(row, values)

        backward_faces(1, ext, words, low_words, a_ext, fvy, vy, gl, gh, dvy, put_ghost)
        backward_own(1, ext, words, a_ext, fvx, ux, sdc, sdu, gl, gh, dvy, put_own)
        to_c[4] = binned(class_ref[...], cells[...])

    return kernel


def binned(classes, cells):
    lanes = lane_ids()
    slots = lax.broadcasted_iota(jnp.int32, (8, LANES), 0)
    total = jnp.zeros((8, LANES), jnp.float32)
    for first in range(0, NCLASS, 8):
        block = jnp.zeros((8, LANES), jnp.float32)
        for k in range(first, min(first + 8, NCLASS)):
            block = jnp.where(slots == k - first, level_sum(jnp.where(classes == k, cells, 0.0)), block)
        block = jnp.sum(block, axis=1, keepdims=True)
        total = jnp.where(lanes == first + slots, block, total)
    return jnp.broadcast_to(level_sum(total), (8, LANES))


def collect(part, from_a, from_b, pick, incoming):
    is_even = row_bases()
    a_row = jnp.where(is_even, ROWS - 2, 0)
    b_row = ROWS - 2 - a_row
    for f in range(FIELDS):
        for j in range(2):
            part[f, a_row + j] = part[f, a_row + j] + from_a[2 * f + j]
            part[f, b_row + j] = part[f, b_row + j] + from_b[2 * f + j]
    pos = strip_pos()
    at_left = (pos == 4) | (pos == 5)
    at_right = (pos == 2) | (pos == 3)
    for g in range(4):
        left, right = pick(g)
        for f in range(4 * g, min(4 * g + 4, FIELDS)):
            q = f % 4
            incoming[f] = jnp.where(at_left, roll(left, 4 - 4 * q), jnp.where(at_right, roll(right, -4 * q), 0.0))


def third_kernel(has_odd):
    def kernel(*refs):
        _, carried_ref, drag_ref, from_a, from_b, from_c = refs[:6]
        from_d = refs[6] if has_odd else None
        part, a_ext, edges_a, incoming = refs[6 + has_odd :]
        pick = side_payloads(from_c, from_d)
        collect(part, from_a, from_b, pick, incoming)
        zero_edges(edges_a)
        for f in range(FIELDS):
            a_ext[f, 0] = jnp.zeros((8, LANES), jnp.float32)
            a_ext[f, ROWS + 1] = jnp.zeros((8, LANES), jnp.float32)
        edges = edge_lanes()
        weight = level_weight()

        def one_row(r, carry):
            c = [carried_ref[f, r] for f in range(FIELDS)]
            a = [part[f, r] + jnp.where(edges, roll(incoming[f], 124 - 16 * r), 0.0) for f in range(FIELDS)]
            a, _ = stepped_back(c, weight * spread(drag_ref, r + 2), a, False)
            for f in range(FIELDS):
                a_ext[f, r + 1] = a[f]
            add_edges(edges_a, a, r)
            return carry

        lax.fori_loop(0, ROWS, one_row, 0, unroll=4)

    return kernel


def seam_kernel(a_ext, edges_a, ext, strip, fvy, vy, sfv, su, *refs):
    low_ref, left_ref, edge_words, words, grads, arriving, *outs = refs
    to_a, to_b, to_c, sdc, sdu, gl, gh, dvy = outs
    low_words, left_words = low_ref[...], left_ref[...]
    backward_strip(0, strip, edges_a, edge_words, left_words, sfv, su, sdc, sdu, to_c)

    def put_ghost(row, values):
        put_ghost_rows(values, row, to_a, to_b)

    backward_faces(0, ext, words, low_words, a_ext, fvy, vy, gl, gh, dvy, put_ghost)
    to_a[2 * FIELDS] = grads[...] + arriving[...]


def own_kernel(ext, words, a_ext, fvx, ux, sdc, sdu, gl, gh, dvy, part):
    def put(row, values):
        for f in range(FIELDS):
            part[f, row] = values[f]

    backward_own(0, ext, words, a_ext, fvx, ux, sdc, sdu, gl, gh, dvy, put)


def last_kernel(has_odd):
    def kernel(*refs):
        _, from_a, from_b, from_c = refs[:4]
        from_d = refs[4] if has_odd else None
        out, part, incoming = refs[4 + has_odd :]
        pick = side_payloads(from_c, from_d)
        collect(part, from_a, from_b, pick, incoming)
        edges = edge_lanes()

        def one_row(r, carry):
            for f in range(FIELDS):
                value = part[f, r] + jnp.where(edges, roll(incoming[f], (124 - 16 * r) % LANES), 0.0)
                out[f, pl.ds(r, 8, stride=8), :] = value
            return carry

        lax.fori_loop(0, ROWS, one_row, 0, unroll=8)

    return kernel


def shaped(*shape, dtype=jnp.float32):
    return jax.ShapeDtypeStruct(shape, dtype)


def tiles(*shape, dtype=jnp.float32):
    return shaped(*shape, 8, LANES, dtype=dtype)


def scratch(*shape, dtype=jnp.float32):
    return pltpu.VMEM((*shape, 8, LANES), dtype)


def call(kernel, outs, scratches, args, smem=(), hbm=(), aliases=None):
    def space(k):
        return pltpu.SMEM if k in smem else pltpu.HBM if k in hbm else pltpu.VMEM

    return pl.pallas_call(
        kernel,
        out_shape=outs,
        in_specs=[pl.BlockSpec(memory_space=space(k)) for k in range(len(args))],
        out_specs=[pl.BlockSpec(memory_space=pltpu.VMEM)] * len(outs),
        scratch_shapes=scratches,
        input_output_aliases=aliases or {},
        compiler_params=pltpu.CompilerParams(vmem_limit_bytes=32 << 20),
    )(*args)


def swap(x, axis, first):
    peers = lax.axis_size(axis)
    pairs = [(i, i + 1) for i in range(first, peers - 1, 2)]
    if not pairs:
        return None
    return lax.ppermute(x, axis, pairs + [(j, i) for i, j in pairs])


def exchange(to_a, to_b, to_c):
    from_a = swap(to_a, "gy", 0)
    from_b = swap(to_b, "gy", 1)
    from_c = swap(to_c, "gx", 0)
    from_d = swap(to_c, "gx", 1)
    if from_b is None:
        from_b = jnp.zeros_like(to_b)
    return (from_a, from_b, from_c) + (() if from_d is None else (from_d,))


def from_partner(x, axis, distance):
    return lax.ppermute(x, axis, [(i, i ^ distance) for i in range(lax.axis_size(axis))])


def add_partner(x, axis, distance):
    return x + from_partner(x, axis, distance)


def body(start_state, final_adjoint, face_words, terrain, drag_coef):
    nx, ny = lax.axis_size("gx"), lax.axis_size("gy")
    has_odd = nx > 2
    start = start_state.reshape(FIELDS, LEV * ROWS, LANES)
    adjoint = final_adjoint.reshape(FIELDS, LEV * ROWS, LANES)
    words = face_words.reshape(8 * ROWS, LANES)
    ints = jnp.int32

    words, terrain, ext, edges, edge_words, *payload = call(
        pack_kernel,
        [shaped(*words.shape, dtype=ints), shaped(*terrain.shape, dtype=ints)]
        + [tiles(14, 12), tiles(14), tiles(dtype=ints), tiles(29), tiles(29), tiles(5)],
        [
            pltpu.VMEM(start.shape, jnp.float32),
            pltpu.SemaphoreType.DMA((3,)),
        ],
        [pltpu.with_memory_space_constraint(x, pltpu.HBM) for x in (start, words, terrain)],
        hbm=(0, 1, 2),
    )
    got = exchange(*payload)
    early = [tiles(14, 8), tiles(4, 8), tiles(14, 8), tiles(14, 9), tiles(4, 9)]
    fvx, ux, along, fvy, vy, coef_rows = call(
        early_kernel(0), [*early, shaped(NCLASS, LANES)], [], [ext, words, drag_coef], smem=(2,)
    )
    res = call(
        first_kernel(has_odd),
        [tiles(14, 12), tiles(14, 9), tiles(4, 9), tiles(14), tiles(14, 8), tiles(14), tiles(4)]
        + [shaped(16, LANES), shaped(16, LANES, dtype=ints), tiles(dtype=ints), tiles(dtype=ints)]
        + [tiles(14, 12), tiles(14, 12), tiles(14), tiles(28), tiles(28), tiles(4)],
        [scratch(14)],
        [ext, fvy, vy, edges, edge_words, along, words, terrain, coef_rows, *got],
        aliases={0: 0, 1: 1, 2: 2},
    )
    ext, fvy, vy, strip, carried_ref, sfv, su, drag_ref, class_ref, low_ref, left_ref = res[:11]
    middle, before, before_edges, *payload = res[11:]
    got = exchange(*payload)
    fvx2, ux2, along2, fvy2, vy2, adjoint_rows = call(
        early_kernel(1), [*early, tiles(14, 8)], [], [middle, words, adjoint]
    )
    kept = [scratch(14, 10), scratch(14), scratch(14), scratch(4), scratch(14, 15), scratch(14, 15), scratch(4, 15)]
    part, *payload = call(
        second_kernel(has_odd),
        [tiles(14, 12), tiles(14, 12), tiles(14, 9), tiles(4, 9), tiles(14, 8), tiles(28), tiles(28), tiles(5)],
        [scratch(14), scratch(14), scratch(4), scratch(14), *kept, scratch(14), pltpu.VMEM((16, LANES), jnp.float32)],
        [middle, before, fvy2, vy2, before_edges, edge_words, along2, fvx2, ux2, words]
        + [drag_ref, class_ref, low_ref, left_ref, adjoint_rows, *got],
        aliases={0: 0, 1: 1, 2: 2, 3: 3},
    )[4:]
    got = exchange(*payload)
    grads = payload[2][4] + got[2][4]
    steps = [("gx", 2**k) for k in range(1, 32) if 2**k < nx] + [("gy", 2**k) for k in range(1, 32) if 2**k < ny]
    steps = steps[::-1]
    early_steps = 1
    for axis, distance in steps[: early_steps - 1]:
        grads = add_partner(grads, axis, distance)
    arriving = from_partner(grads, *steps[early_steps - 1])
    _, a_ext, edges_a = call(
        third_kernel(has_odd),
        [tiles(14, 8), tiles(14, 10), tiles(14)],
        [scratch(14)],
        [part, carried_ref, drag_ref, *got],
        aliases={0: 0},
    )
    to_a, to_b, to_c, *adjoints = call(
        seam_kernel,
        [tiles(29), tiles(28), tiles(4), tiles(14), tiles(4), tiles(14, 15), tiles(14, 15), tiles(4, 15)],
        [],
        [a_ext, edges_a, ext, strip, fvy, vy, sfv, su, low_ref, left_ref, edge_words, words, grads, arriving],
    )
    sdc, sdu, gl, gh, dvy = adjoints
    got = exchange(to_a, to_b, to_c)
    grads = to_a[2 * FIELDS] + got[0][2 * FIELDS]
    for axis, distance in steps[early_steps:]:
        grads = add_partner(grads, axis, distance)
    (part,) = call(own_kernel, [tiles(14, 8)], [], [ext, words, a_ext, fvx, ux, sdc, sdu, gl, gh, dvy])
    out, _ = call(
        last_kernel(has_odd),
        [shaped(FIELDS, LEV * ROWS, LANES), tiles(14, 8)],
        [scratch(14)],
        [part, *got],
        aliases={0: 1},
    )
    grad_scale = math.sqrt(NCLASS / (terrain.size * nx * ny * LEV))
    return (out.reshape(start_state.shape), grads[0, :NCLASS] * grad_scale)


def solution(mesh):
    placed = (
        P(None, None, "gy", "gx"),
        P(None, None, "gy", "gx"),
        P(None, None, None, "gy", "gx"),
        P("gy", "gx"),
        P(),
    )
    return jax.shard_map(
        body,
        mesh=mesh,
        in_specs=placed,
        out_specs=(P(None, None, "gy", "gx"), P()),
        check_vma=False,
    )
```
